256 devices in a mesh: dp: 8 (over z), tensor: 32 (over y, x, core).
Axes of the slice: x: 4, y: 4, z: 8, core: 2. Of those that a mesh axis runs over, the one named last changes fastest.
Arguments:
- hidden: bfloat16 [16384, 1536], P(('dp', 'tensor')), parts along dimension 0, may hold values from -6 to 6
- segment_ids: int32 [16384], P('dp'), parts along dimension 0, may hold values from 0 to 5, never falling along the last dimension, each value on 1 to 1024 neighbouring positions
- routes: int32 [16384, 8], P(('dp', 'tensor')), parts along dimension 0, may hold values from 0 to 39, all different within a row; in each aligned block of 512 rows (0 to 511, 512 to 1023, ...) at most 204 rows name the same one
- route_weights: bfloat16 [16384, 8], P(('dp', 'tensor')), parts along dimension 0, may hold values from 0.099609375 to 1
- attn_gain: float32 [1536], replicated, may hold values from 0.1 to 1.9
- w_qkv: bfloat16 [1536, 2560], P(None, 'tensor')
- w_out: bfloat16 [1536, 1536], P(None, 'tensor'), may hold values from -0.15625 to 0.15625
- ffn_gain: float32 [1536], replicated, may hold values from 0.1 to 1.9
- w_gate_up: bfloat16 [160, 1536, 256], P('tensor'), may hold values from -0.15625 to 0.15625
- w_down: bfloat16 [160, 128, 1536], P('tensor'), may hold values from -0.25 to 0.25
Outputs:
- after_attention: bfloat16 [16384, 1536], P(('dp', 'tensor')), parts along dimension 0
- hidden_out: bfloat16 [16384, 1536], P(('dp', 'tensor')), parts along dimension 0
- kv_cache: bfloat16 [32, 4096, 128], P('tensor', 'dp'), parts along dimension 1
The draws below stay inside these ranges and needn't reach their ends.
There are 8 independent parts, one for each index of `dp`. The reference program is written for one: setup_inputs(seed, part) draws one part's arguments, and reference() takes and returns one part's arrays. A program takes and returns all parts, laid end to end along the dimension named above; an argument that names none is the same for every part. Nothing has to cross between parts.
Inputs may be any that keep to these rules, and one draw needn't show every extreme that they name: `segment_ids`: prompt numbers never fall along the sequence; each prompt has 1 to 1024 tokens, one exactly 1024. `routes`: each token names 8 different experts. In each aligned block of 512 tokens no expert is named by more than 204 tokens, a bound that some block reaches.
All inputs are finite; a program needn't handle non-finite values.
Results may differ from the reference program's by a relative error of at most 0.0075.
Values may be sent and summed in bfloat16 or wider, within the bound.
A program may use at most 128 MiB of HBM per device.

```python
import math
import jax
import jax.numpy as jnp
import numpy as np
from jax import lax

D = 1536
QH = 24
KVH = 8
HD = 64
E = 40
FF = 512
TOPK = 8
SEQ = 2048
PROMPTS = 6
GQ = 3
QUARTERS = 4
UNITS = 128
MOST = 204
LONGEST = 1024


def draw_w_qkv(key, part):
    group_width = (GQ + 2) * HD
    layout = jax.random.normal(key, (D, KVH, group_width), jnp.float32) / math.sqrt(D)
    permuted = layout.reshape(D, KVH, QUARTERS, group_width // QUARTERS).transpose(0, 2, 1, 3).reshape(D, KVH * group_width)
    return permuted.astype(jnp.bfloat16)


def block_levels(rng, extent, cuts, smallest, high):
    loudness = 1.0
    for dim, parts in cuts:
        draws = jax.random.uniform(jax.random.fold_in(jax.random.fold_in(rng, 6), dim), (parts,), jnp.float32, smallest / len(cuts), high / len(cuts))
        loudness = loudness * jnp.repeat(jnp.exp(draws), extent[dim] // parts).reshape((-1,) + (1,) * (len(extent) - 1 - dim))
    return loudness


def length_profile(count, total, limit, skew):
    portions = [(1 << 20) // math.isqrt(grade ** skew) + 1 for grade in range(2, count + 1)]
    rest, given = total - limit - (count - 1), [1] * (count - 1)
    while rest > 0:
        movable = [i for i in range(count - 1) if given[i] < limit]
        mass, budget = sum([portions[i] for i in movable]), rest
        for i in movable:
            addition = min(limit - given[i], max(1, budget * portions[i] // mass), rest)
            given[i] = given[i] + addition
            rest = rest - addition
    return np.array([limit] + given)


def uneven(own_key, amount, total, reach, lean):
    if amount == 2:
        one = jax.random.randint(own_key, (), max(1, total - reach), min(reach, total - 1) + 1)
        return jnp.stack([one, total - one])
    sizes = jnp.asarray(length_profile(amount, total, reach, lean), jnp.int32)
    couples = (amount - 1) // 2
    source_of, sink = sizes[1:1 + 2 * couples:2], sizes[2:2 + 2 * couples:2]
    slack = jnp.minimum(source_of - 1, reach - sink)
    moved = jax.random.randint(jax.random.fold_in(own_key, 1), (couples,), 0, 1 << 20) % (slack + 1)
    sizes = sizes.at[1:1 + 2 * couples:2].set(source_of - moved).at[2:2 + 2 * couples:2].set(sink + moved)
    return sizes[jax.random.permutation(jax.random.fold_in(own_key, 2), amount)]


def routed_block(own_key, own, number, rows, amount, top, reach, lean):
    sequence = jax.random.permutation(own_key, amount)
    crowded, usual = shares(amount, rows * top, reach, lean, True), shares(amount, rows * top, reach, lean, False)
    places = jnp.arange(amount)

    def named(tallies, turn):
        used = int((tallies > 0).sum())
        fixed = max(1, used // 4)
        shifted = fixed + (places - fixed + turn * (used - fixed)) % max(1, amount - fixed)
        return jnp.zeros((amount,), jnp.int32).at[sequence[jnp.where(places < fixed, places, shifted)]].set(jnp.asarray(tallies, jnp.int32))

    tallies = jnp.where(number % 4 == 0, named(crowded, number // 4), named(usual, number - number // 4 - 1))
    mixed = jax.random.permutation(jax.random.fold_in(own, 3), amount)
    source_of, receiver = mixed[0:amount // 2 * 2:2], mixed[1:amount // 2 * 2:2]
    slack = jnp.minimum(tallies[source_of] - 1, reach - tallies[receiver]) // 2
    slack = jnp.where((source_of == sequence[0]) | (receiver == sequence[0]) | (tallies[receiver] == 0), 0, jnp.maximum(slack, 0))
    shifted = jax.random.randint(jax.random.fold_in(own, 4), (amount // 2,), 0, 1 << 20) % (slack + 1)
    tallies = tallies.at[source_of].add(-shifted).at[receiver].add(shifted)
    labels = jnp.searchsorted(jnp.cumsum(tallies), jnp.arange(rows * top), side="right").astype(jnp.int32)
    listing = labels.reshape(top, rows).T
    listing = listing[jax.random.permutation(jax.random.fold_in(own, 1), rows)]
    turn = jax.random.randint(jax.random.fold_in(own, 2), (rows, 1), 0, top)
    return jnp.take_along_axis(listing, (jnp.arange(top)[None, :] + turn) % top, axis=1)


def shares(amount, total, reach, skew, full):
    loads = [(1 << 20) // math.isqrt(grade ** skew) + 1 for grade in range(1, amount + 1)]
    largest = reach if full else min(reach, max(-(-total // amount), total * loads[0] // sum(loads)))
    least = 1 if total - largest >= amount - 1 else 0
    holding, surplus = [largest] + [least] * (amount - 1), total - largest - least * (amount - 1)
    while surplus > 0:
        free = [i for i in range(1, amount) if holding[i] < largest] or [i for i in range(1, amount) if holding[i] < reach]
        whole, remaining = sum([loads[i] for i in free]), surplus
        for i in free:
            extra = min(reach - holding[i], max(1, remaining * loads[i] // whole), surplus)
            holding[i] = holding[i] + extra
            surplus = surplus - extra
    return np.array(holding)


def gaussian(rng, shape, spread, limit, split=(), kind=jnp.bfloat16):
    result = spread * jax.random.normal(rng, shape, jnp.float32)
    if split:
        result = result * block_levels(rng, shape, split, -0.22, 0.18)
    return jnp.clip(result, -limit, limit).astype(kind)


def setup_inputs(seed: int = 0, part: int = 0) -> dict:
    streams_of = jax.random.split(jax.random.key(seed), 11)
    own_keys = jax.random.split(jax.random.fold_in(streams_of[10], part), 11)
    hidden = gaussian(own_keys[0], (SEQ, D), 1.0, 6.0, ((0, 32),))
    segment_ids = jnp.searchsorted(jnp.cumsum(uneven(own_keys[1], PROMPTS, SEQ, LONGEST, 2)), jnp.arange(SEQ), side="right").astype(jnp.int32)
    routes_keys = jax.random.split(jax.random.fold_in(own_keys[2], 1), SEQ // (SEQ // QUARTERS))
    routes_turns = jax.random.permutation(jax.random.fold_in(own_keys[2], 3), SEQ // (SEQ // QUARTERS))
    routes = jax.vmap(lambda own, number: routed_block(jax.random.fold_in(own_keys[2], 2), own, number, SEQ // QUARTERS, E, TOPK, MOST, 2))(routes_keys, routes_turns).reshape((SEQ, TOPK))
    route_weights = jnp.clip(0.099609375 + 0.9003906 * jax.random.uniform(own_keys[3], (SEQ, TOPK), jnp.float32) ** block_levels(own_keys[3], (SEQ, TOPK), ((0, 32),), -0.2, 0.2), 0.099609375, 1.0).astype(jnp.bfloat16)
    attn_gain = jnp.clip(1.0 + 0.18 * jax.random.normal(streams_of[4], (D,), jnp.float32), 0.1, 1.9)
    w_qkv = draw_w_qkv(jax.random.fold_in(streams_of[10], 71), part)
    w_out = gaussian(streams_of[6], (D, QH * HD), (QH * HD) ** -0.5, 0.15625, ((1, 32),))
    ffn_gain = jnp.clip(1.0 + 0.18 * jax.random.normal(streams_of[7], (D,), jnp.float32), 0.1, 1.9)
    w_gate_up = gaussian(streams_of[8], (QUARTERS * E, D, 2 * UNITS), D ** -0.5, 0.15625, ((0, 32),))
    w_down = gaussian(streams_of[9], (QUARTERS * E, UNITS, D), FF ** -0.5, 0.25, ((0, 32),))
    return {"hidden": hidden, "segment_ids": segment_ids, "routes": routes, "route_weights": route_weights, "attn_gain": attn_gain, "w_qkv": w_qkv, "w_out": w_out, "ffn_gain": ffn_gain, "w_gate_up": w_gate_up, "w_down": w_down}


attn_scale = 0.015625
residual_scale = 0.22
rope_base = 10000.0
norm_eps = 1e-06

def rms_norm(row_block, gain_row):
    widened = row_block.astype(jnp.float32)
    mean_square = lax.optimization_barrier(jnp.mean(widened * widened, axis=-1, keepdims=True))
    return (widened * lax.rsqrt(mean_square + norm_eps) * gain_row).astype(jnp.bfloat16)

def segment_starts(segment_ids):
    places = jnp.arange(segment_ids.shape[0], dtype=jnp.int32)
    earlier = jnp.concatenate([segment_ids[:1] - 1, segment_ids[:-1]])
    boundary = jnp.where(segment_ids != earlier, places, jnp.zeros_like(places))
    return lax.cummax(boundary, axis=0)

def rotate(vectors, positions):
    half_width = vectors.shape[-1] // 2
    freq_steps = jnp.arange(half_width, dtype=jnp.float32)
    frequency = jnp.exp(freq_steps * (-2.0 * math.log(rope_base) / vectors.shape[-1]))
    angles = positions.astype(jnp.float32)[:, None] * frequency[None, :]
    cosine = jnp.cos(angles)[:, None, :]
    sine_part = jnp.sin(angles)[:, None, :]
    first_half = vectors[..., :half_width]
    second_half = vectors[..., half_width:]
    return jnp.concatenate([first_half * cosine - second_half * sine_part, second_half * cosine + first_half * sine_part], axis=-1)

def group_columns(weight, quarters):
    row_count = weight.shape[0]
    piece_width = weight.shape[1] // (KVH * quarters)
    return weight.reshape(row_count, quarters, KVH, piece_width).transpose(0, 2, 1, 3).reshape(row_count, KVH, quarters * piece_width)

def reference(hidden, segment_ids, routes, route_weights, attn_gain, w_qkv, w_out, ffn_gain, w_gate_up, w_down):
    normed = rms_norm(hidden, attn_gain)
    starts = segment_starts(segment_ids)
    places = jnp.arange(SEQ, dtype=jnp.int32)
    positions = places - starts
    qkv_cols = group_columns(w_qkv, QUARTERS)
    out_cols = group_columns(w_out, QUARTERS)
    projected = jnp.dot(normed, qkv_cols.reshape(D, KVH * (GQ + 2) * HD), preferred_element_type=jnp.float32).reshape(SEQ, KVH, GQ + 2, HD)
    queries = rotate(projected[:, :, :GQ].reshape(SEQ, KVH * GQ, HD), positions).astype(jnp.bfloat16).reshape(SEQ, KVH, GQ, HD)
    keys = rotate(projected[:, :, GQ], positions).astype(jnp.bfloat16)
    values = projected[:, :, GQ + 1].astype(jnp.bfloat16)
    cache_rows = jnp.concatenate([keys, values], axis=-1)
    kv_cache = cache_rows.reshape(QUARTERS, SEQ // QUARTERS, KVH, 2 * HD).transpose(0, 2, 1, 3).reshape(QUARTERS * KVH, SEQ // QUARTERS, 2 * HD)
    block_rows = min(256, SEQ)
    keys_wide = keys.astype(jnp.float32)
    values_wide = values.astype(jnp.float32)

    def attend(block_index):
        first_row = block_index * block_rows
        block_queries = lax.dynamic_slice_in_dim(queries, first_row, block_rows, 0).astype(jnp.float32)
        query_places = first_row + jnp.arange(block_rows, dtype=jnp.int32)
        query_starts = lax.dynamic_slice_in_dim(starts, first_row, block_rows, 0)
        allowed = (places[None, :] <= query_places[:, None]) & (places[None, :] >= query_starts[:, None])
        scores = jnp.einsum('qgjd,kgd->gjqk', block_queries, keys_wide) * attn_scale
        scores = jnp.where(allowed[None, None], scores, -jnp.inf)
        row_peak = lax.optimization_barrier(jnp.max(scores, axis=-1, keepdims=True))
        weights = jnp.exp(scores - row_peak)
        totals = lax.optimization_barrier(jnp.sum(weights, axis=-1))
        rounded = lax.optimization_barrier(weights.astype(jnp.bfloat16)).astype(jnp.float32)
        mixed = jnp.einsum('gjqk,kgd->qgjd', rounded, values_wide) / totals.transpose(2, 0, 1)[..., None]
        return mixed.astype(jnp.bfloat16).reshape(block_rows, QH * HD)
    attended = lax.map(attend, jnp.arange(SEQ // block_rows, dtype=jnp.int32)).reshape(SEQ, QH * HD)
    projection = jnp.einsum('sc,dc->sd', attended.astype(jnp.float32), out_cols.reshape(D, QH * HD).astype(jnp.float32))
    after_attention = (hidden.astype(jnp.float32) + residual_scale * projection).astype(jnp.bfloat16)
    expert_in = rms_norm(after_attention, ffn_gain)
    split_in = w_gate_up.reshape(QUARTERS, E, D, 2, UNITS)
    gate_all = split_in[:, :, :, 0].transpose(1, 2, 0, 3).reshape(E, D, FF)
    up_all = split_in[:, :, :, 1].transpose(1, 2, 0, 3).reshape(E, D, FF)
    down_all = w_down.reshape(QUARTERS, E, UNITS, D).transpose(1, 0, 2, 3).reshape(E, FF, D)
    shares_all = route_weights.astype(jnp.float32)

    def add_expert(running, pieces):
        expert_id, gate_w, up_w, down_w = pieces
        route_share = lax.optimization_barrier(jnp.sum(jnp.where(routes == expert_id, shares_all, jnp.zeros_like(shares_all)), axis=1))
        gate_val = jnp.dot(expert_in, gate_w, preferred_element_type=jnp.float32)
        up_val = jnp.dot(expert_in, up_w, preferred_element_type=jnp.float32)
        inner_act = (jax.nn.silu(gate_val) * up_val).astype(jnp.bfloat16)
        output = jnp.dot(inner_act, down_w, preferred_element_type=jnp.float32)
        return (running + route_share[:, None] * output, None)
    expert_sum, unused = lax.scan(add_expert, jnp.zeros((SEQ, D), jnp.float32), (jnp.arange(E, dtype=jnp.int32), gate_all, up_all, down_all))
    hidden_out = (after_attention.astype(jnp.float32) + residual_scale * expert_sum).astype(jnp.bfloat16)
    return (after_attention, hidden_out, kv_cache)
```

```python
import math

import jax
import jax.numpy as jnp
from jax import lax
from jax.sharding import PartitionSpec as P
from jax.experimental import pallas as pl
from jax.experimental.pallas import tpu as pltpu

KVH = 8
HD = 64
GQ = 3


attn_scale = 0.015625
residual_scale = 0.22
rope_base = 10000.0
norm_eps = 1e-06
masked_floor = -1e30


def partner(value, axis, apart):
    mask = 2**apart
    pairs = [(source, source ^ mask) for source in range(lax.axis_size(axis))]
    return lax.ppermute(value, axis, pairs)


def rms_norm(row_block, gain_row):
    widened = row_block.astype(jnp.float32)
    mean_square = jnp.mean(widened * widened, axis=-1, keepdims=True)
    return (widened * lax.rsqrt(mean_square + norm_eps) * gain_row).astype(jnp.bfloat16)


def segment_starts(segment_ids):
    places = jnp.arange(segment_ids.shape[0], dtype=jnp.int32)
    earlier = jnp.concatenate([segment_ids[:1] - 1, segment_ids[:-1]])
    boundary = jnp.where(segment_ids != earlier, places, jnp.zeros_like(places))
    return lax.cummax(boundary, axis=0)


def rotate(vectors, positions):
    half_width = vectors.shape[-1] // 2
    freq_steps = jnp.arange(half_width, dtype=jnp.float32)
    frequency = jnp.exp(freq_steps * (-2.0 * math.log(rope_base) / vectors.shape[-1]))
    angles = positions.astype(jnp.float32)[:, None] * frequency[None, :]
    cosine = jnp.cos(angles)[:, None, :]
    sine_part = jnp.sin(angles)[:, None, :]
    first_half = vectors[..., :half_width]
    second_half = vectors[..., half_width:]
    return jnp.concatenate(
        [
            first_half * cosine - second_half * sine_part,
            second_half * cosine + first_half * sine_part,
        ],
        axis=-1,
    )


def gather_levels(parts, level_bits, join_axes, sender):
    index_now = lax.axis_index("tensor")
    for level_bit in level_bits:
        arrived = sender(parts, level_bit)
        is_upper = index_now >> level_bit & 1 == 1
        joined_parts = []
        for own_part, peer_part, join_axis in zip(parts, arrived, join_axes):
            lower_first = jnp.concatenate([own_part, peer_part], join_axis)
            upper_first = jnp.concatenate([peer_part, own_part], join_axis)
            joined_parts.append(jnp.where(is_upper, upper_first, lower_first))
        parts = tuple(joined_parts)
    return parts


def fold_levels(partial_sum, level_bits, sender):
    index_now = lax.axis_index("tensor")
    for level_bit in reversed(level_bits):
        half_rows = partial_sum.shape[0] // 2
        lower_rows = partial_sum[:half_rows]
        upper_rows = partial_sum[half_rows:]
        is_upper = index_now >> level_bit & 1 == 1
        kept_rows = jnp.where(is_upper, upper_rows, lower_rows)
        sent_rows = jnp.where(is_upper, lower_rows, upper_rows)
        partial_sum = kept_rows + sender(sent_rows, level_bit)
    return partial_sum


def project_pairs(row_block, w_pairs, positions):
    head_size = w_pairs.shape[1] // 2
    paired = jnp.dot(row_block, w_pairs, preferred_element_type=jnp.float32)
    rotated = rotate(paired[:, None, :head_size], positions)[:, 0]
    return jnp.concatenate([rotated, paired[:, head_size:]], axis=1).astype(jnp.bfloat16)


def expert_block(rows_ref, share_ref, gate_up_ref, down_ref, out_ref):
    rows = rows_ref[...]
    inner_width = down_ref.shape[1]
    total = jnp.zeros(out_ref.shape, jnp.float32)
    for expert in range(gate_up_ref.shape[0]):
        both = jnp.dot(rows, gate_up_ref[expert], preferred_element_type=jnp.float32)
        gate_val = both[:, :inner_width]
        up_val = both[:, inner_width:]
        inner_act = (jax.nn.silu(gate_val) * up_val).astype(jnp.bfloat16)
        produced = jnp.dot(inner_act, down_ref[expert], preferred_element_type=jnp.float32)
        total = total + share_ref[:, expert : expert + 1] * produced
    out_ref[...] = total.astype(out_ref.dtype)


def dense_experts(rows_all, shares, gate_up, down_proj):
    row_count, model_width = rows_all.shape
    expert_count = gate_up.shape[0]
    tile = 256
    return pl.pallas_call(
        expert_block,
        grid=(row_count // tile,),
        in_specs=[
            pl.BlockSpec((tile, model_width), lambda i: (i, 0)),
            pl.BlockSpec((tile, expert_count), lambda i: (i, 0)),
            pl.BlockSpec(gate_up.shape, lambda i: (0, 0, 0)),
            pl.BlockSpec(down_proj.shape, lambda i: (0, 0, 0)),
        ],
        out_specs=pl.BlockSpec((tile, model_width), lambda i: (i, 0)),
        out_shape=jax.ShapeDtypeStruct((row_count, model_width), jnp.bfloat16),
        compiler_params=pltpu.CompilerParams(vmem_limit_bytes=48 * 1024 * 1024),
    )(rows_all, shares, gate_up, down_proj)


def on_device(
    hidden, segment_ids, routes, route_weights, attn_gain, w_qkv, w_out, ffn_gain, w_gate_up, w_down
):
    device_count = lax.axis_size("tensor")
    quarters = device_count // KVH
    index_now = lax.axis_index("tensor")
    quarter_index = index_now // KVH
    group_index = index_now % KVH
    group_bits = list(range(KVH.bit_length() - 1))
    quarter_bits = list(range(len(group_bits), device_count.bit_length() - 1))
    seq_len = segment_ids.shape[0]
    rows_quarter = seq_len // quarters
    model_width = hidden.shape[1]
    starts = segment_starts(segment_ids)
    expert_total = w_gate_up.shape[0] * KVH
    expert_ids = jnp.arange(expert_total, dtype=jnp.int32)
    share_table = jnp.sum(
        jnp.where(
            routes[:, None, :] == expert_ids[None, :, None],
            route_weights[:, None, :],
            jnp.zeros((), route_weights.dtype),
        ),
        axis=2,
    )
    shares_all = lax.all_gather(share_table, "tensor", axis=0, tiled=True)
    positions = jnp.arange(seq_len, dtype=jnp.int32) - starts
    own_positions = lax.dynamic_slice_in_dim(
        positions, quarter_index * rows_quarter, rows_quarter, 0
    )
    normed = rms_norm(hidden, attn_gain)
    qkv_width = w_qkv.shape[1]
    joined = jnp.concatenate([w_qkv, w_out], axis=1)
    (gathered_cols,) = gather_levels(
        (joined,),
        quarter_bits,
        (1,),
        lambda payload, level_bit: (partner(payload[0], "tensor", level_bit),),
    )
    by_quarter = gathered_cols.reshape(model_width, quarters, joined.shape[1])
    w_group = by_quarter[:, :, :qkv_width].reshape(model_width, quarters * qkv_width)
    w_attn_out = by_quarter[:, :, qkv_width:].reshape(model_width, GQ * HD)
    w_query = w_group[:, : GQ * HD]
    w_pairs = w_group[:, GQ * HD :]
    all_rows = lax.all_gather(normed, "tensor", axis=0, tiled=True)
    own_rows = lax.dynamic_slice_in_dim(all_rows, quarter_index * rows_quarter, rows_quarter, 0)
    key_values = project_pairs(all_rows, w_pairs, positions)
    kv_block = lax.dynamic_slice_in_dim(key_values, quarter_index * rows_quarter, rows_quarter, 0)
    query_proj = jnp.dot(own_rows, w_query, preferred_element_type=jnp.float32).reshape(
        rows_quarter, GQ, HD
    )
    queries_heads = rotate(query_proj, own_positions).astype(jnp.bfloat16).transpose(1, 0, 2)
    block_rows = min(256, rows_quarter)
    key_block = min(512, seq_len)

    def attend(block_number):
        first_row = block_number * block_rows
        block_queries = lax.dynamic_slice_in_dim(queries_heads, first_row, block_rows, 1).reshape(
            GQ * block_rows, HD
        )
        first_place = quarter_index * rows_quarter + first_row
        query_places = first_place + jnp.arange(block_rows, dtype=jnp.int32)
        query_starts = lax.dynamic_slice_in_dim(starts, first_place, block_rows, 0)
        lowest = query_starts[0] // key_block
        highest = (first_place + block_rows - 1) // key_block + 1

        def step_keys(key_number, loop_state):
            row_peak, totals, accumulated = loop_state
            key_offset = key_number * key_block
            block_pairs = lax.dynamic_slice_in_dim(key_values, key_offset, key_block, 0)
            key_places = key_offset + jnp.arange(key_block, dtype=jnp.int32)
            allowed = (key_places[None, :] <= query_places[:, None]) & (
                key_places[None, :] >= query_starts[:, None]
            )
            scores = (
                lax.dot_general(
                    block_queries,
                    block_pairs[:, :HD],
                    (((1,), (1,)), ((), ())),
                    preferred_element_type=jnp.float32,
                )
                * attn_scale
            )
            scores = jnp.where(jnp.tile(allowed, (GQ, 1)), scores, -jnp.inf)
            new_peak = jnp.maximum(row_peak, jnp.max(scores, axis=1))
            weights = jnp.exp(scores - new_peak[:, None])
            factor = jnp.exp(row_peak - new_peak)
            totals = totals * factor + jnp.sum(weights, axis=1)
            accumulated = accumulated * factor[:, None] + jnp.dot(
                weights.astype(jnp.bfloat16),
                block_pairs[:, HD:],
                preferred_element_type=jnp.float32,
            )
            return (new_peak, totals, accumulated)

        start_state = (
            jnp.full((GQ * block_rows,), masked_floor, jnp.float32),
            jnp.zeros((GQ * block_rows,), jnp.float32),
            jnp.zeros((GQ * block_rows, HD), jnp.float32),
        )
        row_peak, totals, accumulated = lax.fori_loop(lowest, highest, step_keys, start_state)
        mixed = (accumulated / totals[:, None]).astype(jnp.bfloat16).reshape(GQ, block_rows, HD)
        return mixed.transpose(1, 0, 2).reshape(block_rows, GQ * HD)

    attended = lax.map(attend, jnp.arange(rows_quarter // block_rows, dtype=jnp.int32)).reshape(
        rows_quarter, GQ * HD
    )
    partial_proj = lax.dot_general(
        attended, w_attn_out, (((1,), (1,)), ((), ())), preferred_element_type=jnp.float32
    )
    projection = fold_levels(
        partial_proj,
        group_bits,
        lambda sent_rows, level_bit: partner(
            sent_rows.astype(jnp.bfloat16), "tensor", level_bit
        ).astype(sent_rows.dtype),
    )
    after_attention = (hidden.astype(jnp.float32) + residual_scale * projection).astype(
        jnp.bfloat16
    )
    expert_in = rms_norm(after_attention, ffn_gain)
    local_experts = w_gate_up.shape[0]
    rows_all = lax.all_gather(expert_in, "tensor", axis=0, tiled=True)
    local_shares = lax.dynamic_slice_in_dim(
        shares_all, group_index * local_experts, local_experts, 1
    ).astype(jnp.float32)
    expert_part = dense_experts(rows_all, local_shares, w_gate_up, w_down)
    expert_sum = lax.psum_scatter(
        expert_part, "tensor", scatter_dimension=0, tiled=True
    ).astype(jnp.float32)
    hidden_out = (after_attention.astype(jnp.float32) + residual_scale * expert_sum).astype(
        jnp.bfloat16
    )
    return (after_attention, hidden_out, kv_block[None])


def solution(mesh):
    placed = (
        P(("dp", "tensor"), None),
        P("dp"),
        P(("dp", "tensor"), None),
        P(("dp", "tensor"), None),
        P(),
        P(None, "tensor"),
        P(None, "tensor"),
        P(),
        P("tensor", None, None),
        P("tensor", None, None),
    )
    return jax.shard_map(
        on_device,
        mesh=mesh,
        in_specs=placed,
        out_specs=(P(("dp", "tensor"), None), P(("dp", "tensor"), None), P("tensor", "dp", None)),
        check_vma=False,
    )
```

```python
import math

import jax
import jax.numpy as jnp
from jax import lax
from jax.sharding import PartitionSpec as P
from jax.experimental import pallas as pl
from jax.experimental.pallas import tpu as pltpu

KVH = 8
HD = 64
GQ = 3
CHIPS = ("ty", "tx")
TENSOR = ("ty", "tx", "tc")


attn_scale = 0.015625
residual_scale = 0.22
rope_base = 10000.0
norm_eps = 1e-06
masked_floor = -1e30


def partner(value, axis, apart):
    mask = 2**apart
    pairs = [(source, source ^ mask) for source in range(lax.axis_size(axis))]
    return lax.ppermute(value, axis, pairs)


def rms_norm(row_block, gain_row):
    widened = row_block.astype(jnp.float32)
    mean_square = jnp.mean(widened * widened, axis=-1, keepdims=True)
    return (widened * lax.rsqrt(mean_square + norm_eps) * gain_row).astype(jnp.bfloat16)


def segment_starts(segment_ids):
    places = jnp.arange(segment_ids.shape[0], dtype=jnp.int32)
    earlier = jnp.concatenate([segment_ids[:1] - 1, segment_ids[:-1]])
    boundary = jnp.where(segment_ids != earlier, places, jnp.zeros_like(places))
    return lax.cummax(boundary, axis=0)


def rotate(vectors, positions):
    half_width = vectors.shape[-1] // 2
    freq_steps = jnp.arange(half_width, dtype=jnp.float32)
    frequency = jnp.exp(freq_steps * (-2.0 * math.log(rope_base) / vectors.shape[-1]))
    angles = positions.astype(jnp.float32)[:, None] * frequency[None, :]
    cosine = jnp.cos(angles)[:, None, :]
    sine_part = jnp.sin(angles)[:, None, :]
    first_half = vectors[..., :half_width]
    second_half = vectors[..., half_width:]
    return jnp.concatenate(
        [
            first_half * cosine - second_half * sine_part,
            second_half * cosine + first_half * sine_part,
        ],
        axis=-1,
    )


def gather_levels(parts, level_bits, join_axes, sender):
    index_now = lax.axis_index(TENSOR)
    for level_bit in level_bits:
        arrived = sender(parts, level_bit)
        is_upper = index_now >> level_bit & 1 == 1
        joined_parts = []
        for own_part, peer_part, join_axis in zip(parts, arrived, join_axes):
            lower_first = jnp.concatenate([own_part, peer_part], join_axis)
            upper_first = jnp.concatenate([peer_part, own_part], join_axis)
            joined_parts.append(jnp.where(is_upper, upper_first, lower_first))
        parts = tuple(joined_parts)
    return parts


def fold_levels(partial_sum, level_bits, sender):
    index_now = lax.axis_index(TENSOR)
    for level_bit in reversed(level_bits):
        half_rows = partial_sum.shape[0] // 2
        lower_rows = partial_sum[:half_rows]
        upper_rows = partial_sum[half_rows:]
        is_upper = index_now >> level_bit & 1 == 1
        kept_rows = jnp.where(is_upper, upper_rows, lower_rows)
        sent_rows = jnp.where(is_upper, lower_rows, upper_rows)
        partial_sum = kept_rows + sender(sent_rows, level_bit)
    return partial_sum


def project_pairs(row_block, w_pairs, positions):
    head_size = w_pairs.shape[1] // 2
    paired = jnp.dot(row_block, w_pairs, preferred_element_type=jnp.float32)
    rotated = rotate(paired[:, None, :head_size], positions)[:, 0]
    return jnp.concatenate([rotated, paired[:, head_size:]], axis=1).astype(jnp.bfloat16)


def expert_block(rows_ref, share_ref, gate_up_ref, down_ref, out_ref):
    rows = rows_ref[...]
    inner_width = down_ref.shape[1]
    total = jnp.zeros(out_ref.shape, jnp.float32)
    for expert in range(gate_up_ref.shape[0]):
        both = jnp.dot(rows, gate_up_ref[expert], preferred_element_type=jnp.float32)
        gate_val = both[:, :inner_width]
        up_val = both[:, inner_width:]
        inner_act = (jax.nn.silu(gate_val) * up_val).astype(jnp.bfloat16)
        produced = jnp.dot(inner_act, down_ref[expert], preferred_element_type=jnp.float32)
        total = total + share_ref[:, expert : expert + 1] * produced
    out_ref[...] = total.astype(out_ref.dtype)


def dense_experts(rows_all, shares, gate_up, down_proj):
    row_count = rows_all.shape[0]
    model_width = gate_up.shape[1]
    expert_count = gate_up.shape[0]
    tile = 256
    return pl.pallas_call(
        expert_block,
        grid=(row_count // tile,),
        in_specs=[
            pl.BlockSpec((tile, model_width), lambda i: (i, 0)),
            pl.BlockSpec((tile, expert_count), lambda i: (i, 0)),
            pl.BlockSpec(gate_up.shape, lambda i: (0, 0, 0)),
            pl.BlockSpec(down_proj.shape, lambda i: (0, 0, 0)),
        ],
        out_specs=pl.BlockSpec((tile, model_width), lambda i: (i, 0)),
        out_shape=jax.ShapeDtypeStruct((row_count, model_width), jnp.bfloat16),
        compiler_params=pltpu.CompilerParams(vmem_limit_bytes=48 * 1024 * 1024),
    )(rows_all, shares, gate_up, down_proj)


def on_device(
    hidden, segment_ids, routes, route_weights, attn_gain, w_qkv, w_out, ffn_gain, w_gate_up, w_down
):
    device_count = lax.axis_size(TENSOR)
    quarters = device_count // KVH
    index_now = lax.axis_index(TENSOR)
    quarter_index = index_now // KVH
    group_index = index_now % KVH
    group_bits = list(range(KVH.bit_length() - 1))
    quarter_bits = list(range(len(group_bits), device_count.bit_length() - 1))
    seq_len = segment_ids.shape[0]
    rows_quarter = seq_len // quarters
    model_width = hidden.shape[1]
    starts = segment_starts(segment_ids)
    expert_total = w_gate_up.shape[0] * KVH
    expert_ids = jnp.arange(expert_total, dtype=jnp.int32)
    share_table = jnp.sum(
        jnp.where(
            routes[:, None, :] == expert_ids[None, :, None],
            route_weights[:, None, :],
            jnp.zeros((), route_weights.dtype),
        ),
        axis=2,
    )
    positions = jnp.arange(seq_len, dtype=jnp.int32) - starts
    own_positions = lax.dynamic_slice_in_dim(
        positions, quarter_index * rows_quarter, rows_quarter, 0
    )
    normed = rms_norm(hidden, attn_gain)
    qkv_width = w_qkv.shape[1]
    joined = jnp.concatenate([w_qkv, w_out], axis=1)
    (gathered_cols,) = gather_levels(
        (joined,),
        quarter_bits,
        (1,),
        lambda payload, level_bit: (partner(payload[0], TENSOR, level_bit),),
    )
    by_quarter = gathered_cols.reshape(model_width, quarters, joined.shape[1])
    w_group = by_quarter[:, :, :qkv_width].reshape(model_width, quarters * qkv_width)
    w_attn_out = by_quarter[:, :, qkv_width:].reshape(model_width, GQ * HD)
    w_query = w_group[:, : GQ * HD]
    w_pairs = w_group[:, GQ * HD :]
    all_rows = lax.all_gather(normed, TENSOR, axis=0, tiled=True)
    own_rows = lax.dynamic_slice_in_dim(all_rows, quarter_index * rows_quarter, rows_quarter, 0)
    key_values = project_pairs(all_rows, w_pairs, positions)
    kv_block = lax.dynamic_slice_in_dim(key_values, quarter_index * rows_quarter, rows_quarter, 0)
    query_proj = jnp.dot(own_rows, w_query, preferred_element_type=jnp.float32).reshape(
        rows_quarter, GQ, HD
    )
    queries_heads = rotate(query_proj, own_positions).astype(jnp.bfloat16).transpose(1, 0, 2)
    block_rows = min(256, rows_quarter)
    key_block = min(512, seq_len)

    def attend(block_number):
        first_row = block_number * block_rows
        block_queries = lax.dynamic_slice_in_dim(queries_heads, first_row, block_rows, 1).reshape(
            GQ * block_rows, HD
        )
        first_place = quarter_index * rows_quarter + first_row
        query_places = first_place + jnp.arange(block_rows, dtype=jnp.int32)
        query_starts = lax.dynamic_slice_in_dim(starts, first_place, block_rows, 0)
        lowest = query_starts[0] // key_block
        highest = (first_place + block_rows - 1) // key_block + 1

        def step_keys(key_number, loop_state):
            row_peak, totals, accumulated = loop_state
            key_offset = key_number * key_block
            block_pairs = lax.dynamic_slice_in_dim(key_values, key_offset, key_block, 0)
            key_places = key_offset + jnp.arange(key_block, dtype=jnp.int32)
            allowed = (key_places[None, :] <= query_places[:, None]) & (
                key_places[None, :] >= query_starts[:, None]
            )
            scores = (
                lax.dot_general(
                    block_queries,
                    block_pairs[:, :HD],
                    (((1,), (1,)), ((), ())),
                    preferred_element_type=jnp.float32,
                )
                * attn_scale
            )
            scores = jnp.where(jnp.tile(allowed, (GQ, 1)), scores, -jnp.inf)
            new_peak = jnp.maximum(row_peak, jnp.max(scores, axis=1))
            weights = jnp.exp(scores - new_peak[:, None])
            factor = jnp.exp(row_peak - new_peak)
            totals = totals * factor + jnp.sum(weights, axis=1)
            accumulated = accumulated * factor[:, None] + jnp.dot(
                weights.astype(jnp.bfloat16),
                block_pairs[:, HD:],
                preferred_element_type=jnp.float32,
            )
            return (new_peak, totals, accumulated)

        start_state = (
            jnp.full((GQ * block_rows,), masked_floor, jnp.float32),
            jnp.zeros((GQ * block_rows,), jnp.float32),
            jnp.zeros((GQ * block_rows, HD), jnp.float32),
        )
        row_peak, totals, accumulated = lax.fori_loop(lowest, highest, step_keys, start_state)
        mixed = (accumulated / totals[:, None]).astype(jnp.bfloat16).reshape(GQ, block_rows, HD)
        return mixed.transpose(1, 0, 2).reshape(block_rows, GQ * HD)

    attended = lax.map(attend, jnp.arange(rows_quarter // block_rows, dtype=jnp.int32)).reshape(
        rows_quarter, GQ * HD
    )
    partial_proj = lax.dot_general(
        attended, w_attn_out, (((1,), (1,)), ((), ())), preferred_element_type=jnp.float32
    )
    projection = fold_levels(
        partial_proj,
        group_bits,
        lambda sent_rows, level_bit: partner(
            sent_rows.astype(jnp.bfloat16), TENSOR, level_bit
        ).astype(sent_rows.dtype),
    )
    after_attention = (hidden.astype(jnp.float32) + residual_scale * projection).astype(
        jnp.bfloat16
    )
    expert_in = rms_norm(after_attention, ffn_gain)
    local_experts = w_gate_up.shape[0]
    share_cols = 128 * pl.cdiv(expert_total, 128)
    carried = jnp.concatenate(
        [
            expert_in,
            share_table,
            jnp.zeros((share_table.shape[0], share_cols - expert_total), jnp.bfloat16),
        ],
        axis=1,
    )
    by_chip = lax.all_gather(carried, CHIPS, axis=0, tiled=True)
    rows_all = lax.all_gather(by_chip, "tc", axis=0, tiled=True)
    local_shares = lax.dynamic_slice_in_dim(
        rows_all[:, model_width : model_width + expert_total],
        group_index * local_experts,
        local_experts,
        1,
    ).astype(jnp.float32)
    expert_part = dense_experts(rows_all, local_shares, w_gate_up, w_down)
    core_sum = lax.psum_scatter(expert_part, "tc", scatter_dimension=0, tiled=True)
    expert_sum = lax.psum_scatter(core_sum, CHIPS, scatter_dimension=0, tiled=True).astype(
        jnp.float32
    )
    hidden_out = (after_attention.astype(jnp.float32) + residual_scale * expert_sum).astype(
        jnp.bfloat16
    )
    return (after_attention, hidden_out, kv_block[None])


def solution(mesh):
    grid = mesh.devices.reshape(mesh.devices.shape[0], -1, 4, 2)
    mesh = jax.sharding.Mesh(grid, ("dp",) + TENSOR)
    placed = (
        P(("dp",) + TENSOR, None),
        P("dp"),
        P(("dp",) + TENSOR, None),
        P(("dp",) + TENSOR, None),
        P(),
        P(None, TENSOR),
        P(None, TENSOR),
        P(),
        P(TENSOR, None, None),
        P(TENSOR, None, None),
    )
    return jax.shard_map(
        on_device,
        mesh=mesh,
        in_specs=placed,
        out_specs=(P(("dp",) + TENSOR, None), P(("dp",) + TENSOR, None), P(TENSOR, "dp", None)),
        check_vma=False,
    )
```

```python
import math

import jax
import jax.numpy as jnp
from jax import lax
from jax.sharding import PartitionSpec as P
from jax.experimental import pallas as pl
from jax.experimental.pallas import tpu as pltpu

KVH = 8
HD = 64
GQ = 3
CHIPS = ("ty", "tx")
TENSOR = ("ty", "tx", "tc")


attn_scale = 0.015625
residual_scale = 0.22
rope_base = 10000.0
norm_eps = 1e-06
masked_floor = -1e30


def partner(value, axis, apart):
    mask = 2**apart
    pairs = [(source, source ^ mask) for source in range(lax.axis_size(axis))]
    return lax.ppermute(value, axis, pairs)


def rms_norm(row_block, gain_row):
    widened = row_block.astype(jnp.float32)
    mean_square = jnp.mean(widened * widened, axis=-1, keepdims=True)
    return (widened * lax.rsqrt(mean_square + norm_eps) * gain_row).astype(jnp.bfloat16)


def segment_starts(segment_ids):
    places = jnp.arange(segment_ids.shape[0], dtype=jnp.int32)
    earlier = jnp.concatenate([segment_ids[:1] - 1, segment_ids[:-1]])
    boundary = jnp.where(segment_ids != earlier, places, jnp.zeros_like(places))
    return lax.cummax(boundary, axis=0)


def rotate(vectors, positions):
    half_width = vectors.shape[-1] // 2
    freq_steps = jnp.arange(half_width, dtype=jnp.float32)
    frequency = jnp.exp(freq_steps * (-2.0 * math.log(rope_base) / vectors.shape[-1]))
    angles = positions.astype(jnp.float32)[:, None] * frequency[None, :]
    cosine = jnp.cos(angles)[:, None, :]
    sine_part = jnp.sin(angles)[:, None, :]
    first_half = vectors[..., :half_width]
    second_half = vectors[..., half_width:]
    return jnp.concatenate(
        [
            first_half * cosine - second_half * sine_part,
            second_half * cosine + first_half * sine_part,
        ],
        axis=-1,
    )


def gather_levels(parts, level_bits, join_axes, sender):
    index_now = lax.axis_index(TENSOR)
    for level_bit in level_bits:
        arrived = sender(parts, level_bit)
        is_upper = index_now >> level_bit & 1 == 1
        joined_parts = []
        for own_part, peer_part, join_axis in zip(parts, arrived, join_axes):
            lower_first = jnp.concatenate([own_part, peer_part], join_axis)
            upper_first = jnp.concatenate([peer_part, own_part], join_axis)
            joined_parts.append(jnp.where(is_upper, upper_first, lower_first))
        parts = tuple(joined_parts)
    return parts


def fold_levels(partial_sum, level_bits, sender):
    index_now = lax.axis_index(TENSOR)
    for level_bit in reversed(level_bits):
        half_rows = partial_sum.shape[0] // 2
        lower_rows = partial_sum[:half_rows]
        upper_rows = partial_sum[half_rows:]
        is_upper = index_now >> level_bit & 1 == 1
        kept_rows = jnp.where(is_upper, upper_rows, lower_rows)
        sent_rows = jnp.where(is_upper, lower_rows, upper_rows)
        partial_sum = kept_rows + sender(sent_rows, level_bit)
    return partial_sum


def project_pairs(row_block, w_pairs, positions):
    head_size = w_pairs.shape[1] // 2
    paired = jnp.dot(row_block, w_pairs, preferred_element_type=jnp.float32)
    rotated = rotate(paired[:, None, :head_size], positions)[:, 0]
    return jnp.concatenate([rotated, paired[:, head_size:]], axis=1).astype(jnp.bfloat16)


def expert_block(rows_ref, share_ref, gate_up_ref, down_ref, out_ref):
    model_width = gate_up_ref.shape[1]
    rows = rows_ref[:, :model_width]
    inner_width = down_ref.shape[1]
    total = jnp.zeros((rows.shape[0], model_width), jnp.float32)
    for expert in range(gate_up_ref.shape[0]):
        both = jnp.dot(rows, gate_up_ref[expert], preferred_element_type=jnp.float32)
        gate_val = both[:, :inner_width]
        up_val = both[:, inner_width:]
        inner_act = (jax.nn.silu(gate_val) * up_val).astype(jnp.bfloat16)
        produced = jnp.dot(inner_act, down_ref[expert], preferred_element_type=jnp.float32)
        total = total + share_ref[:, expert : expert + 1] * produced
    piece = out_ref.shape[3]
    for part in range(4):
        out_ref[part % 2, part // 2, 0] = total[part * piece : (part + 1) * piece].astype(
            out_ref.dtype
        )


def tile_slot(tile_number):
    return (tile_number // 2) % 2 * 4 + (tile_number // 4) % 2 * 2 + tile_number % 2


def dense_experts(rows_all, shares, gate_up, down_proj):
    row_count, carried_width = rows_all.shape
    model_width = gate_up.shape[1]
    expert_count = gate_up.shape[0]
    piece = row_count // 32
    tile = 4 * piece
    tiles = row_count // tile
    return pl.pallas_call(
        expert_block,
        grid=(tiles,),
        in_specs=[
            pl.BlockSpec((tile, carried_width), lambda i: (i, 0)),
            pl.BlockSpec((tile, expert_count), lambda i: (i, 0)),
            pl.BlockSpec(gate_up.shape, lambda i: (0, 0, 0)),
            pl.BlockSpec(down_proj.shape, lambda i: (0, 0, 0)),
        ],
        out_specs=pl.BlockSpec(
            (2, 2, 1, piece, model_width), lambda i: (0, 0, tile_slot(i), 0, 0)
        ),
        out_shape=jax.ShapeDtypeStruct((2, 2, tiles, piece, model_width), jnp.bfloat16),
        compiler_params=pltpu.CompilerParams(vmem_limit_bytes=48 * 1024 * 1024),
    )(rows_all, shares, gate_up, down_proj)


def fold_bits(partial_sum, level_bits):
    index_now = lax.axis_index(TENSOR)
    for level_bit in level_bits:
        half_rows = partial_sum.shape[0] // 2
        lower_rows = partial_sum[:half_rows]
        upper_rows = partial_sum[half_rows:]
        is_upper = index_now >> level_bit & 1 == 1
        kept_rows = jnp.where(is_upper, upper_rows, lower_rows)
        sent_rows = jnp.where(is_upper, lower_rows, upper_rows)
        arrived = partner(sent_rows.astype(jnp.bfloat16), TENSOR, level_bit)
        partial_sum = kept_rows.astype(jnp.float32) + arrived.astype(jnp.float32)
    return partial_sum

def on_device(
    hidden, segment_ids, routes, route_weights, attn_gain, w_qkv, w_out, ffn_gain, w_gate_up, w_down
):
    device_count = lax.axis_size(TENSOR)
    quarters = device_count // KVH
    index_now = lax.axis_index(TENSOR)
    quarter_index = index_now // KVH
    group_index = index_now % KVH
    group_bits = list(range(KVH.bit_length() - 1))
    quarter_bits = list(range(len(group_bits), device_count.bit_length() - 1))
    seq_len = segment_ids.shape[0]
    rows_quarter = seq_len // quarters
    model_width = hidden.shape[1]
    starts = segment_starts(segment_ids)
    expert_total = w_gate_up.shape[0] * KVH
    expert_ids = jnp.arange(expert_total, dtype=jnp.int32)
    share_table = jnp.sum(
        jnp.where(
            routes[:, None, :] == expert_ids[None, :, None],
            route_weights[:, None, :],
            jnp.zeros((), route_weights.dtype),
        ),
        axis=2,
    )
    positions = jnp.arange(seq_len, dtype=jnp.int32) - starts
    own_positions = lax.dynamic_slice_in_dim(
        positions, quarter_index * rows_quarter, rows_quarter, 0
    )
    normed = rms_norm(hidden, attn_gain)
    qkv_width = w_qkv.shape[1]
    joined = jnp.concatenate([w_qkv, w_out], axis=1)
    (gathered_cols,) = gather_levels(
        (joined,),
        quarter_bits,
        (1,),
        lambda payload, level_bit: (partner(payload[0], TENSOR, level_bit),),
    )
    by_quarter = gathered_cols.reshape(model_width, quarters, joined.shape[1])
    w_group = by_quarter[:, :, :qkv_width].reshape(model_width, quarters * qkv_width)
    w_attn_out = by_quarter[:, :, qkv_width:].reshape(model_width, GQ * HD)
    w_query = w_group[:, : GQ * HD]
    w_pairs = w_group[:, GQ * HD :]
    all_rows = lax.all_gather(normed, TENSOR, axis=0, tiled=True)
    own_rows = lax.dynamic_slice_in_dim(all_rows, quarter_index * rows_quarter, rows_quarter, 0)
    key_values = project_pairs(all_rows, w_pairs, positions)
    kv_block = lax.dynamic_slice_in_dim(key_values, quarter_index * rows_quarter, rows_quarter, 0)
    query_proj = jnp.dot(own_rows, w_query, preferred_element_type=jnp.float32).reshape(
        rows_quarter, GQ, HD
    )
    queries_heads = rotate(query_proj, own_positions).astype(jnp.bfloat16).transpose(1, 0, 2)
    block_rows = min(256, rows_quarter)
    key_block = min(512, seq_len)

    def attend(block_number):
        first_row = block_number * block_rows
        block_queries = lax.dynamic_slice_in_dim(queries_heads, first_row, block_rows, 1).reshape(
            GQ * block_rows, HD
        )
        first_place = quarter_index * rows_quarter + first_row
        query_places = first_place + jnp.arange(block_rows, dtype=jnp.int32)
        query_starts = lax.dynamic_slice_in_dim(starts, first_place, block_rows, 0)
        lowest = query_starts[0] // key_block
        highest = (first_place + block_rows - 1) // key_block + 1

        def step_keys(key_number, loop_state):
            row_peak, totals, accumulated = loop_state
            key_offset = key_number * key_block
            block_pairs = lax.dynamic_slice_in_dim(key_values, key_offset, key_block, 0)
            key_places = key_offset + jnp.arange(key_block, dtype=jnp.int32)
            allowed = (key_places[None, :] <= query_places[:, None]) & (
                key_places[None, :] >= query_starts[:, None]
            )
            scores = (
                lax.dot_general(
                    block_queries,
                    block_pairs[:, :HD],
                    (((1,), (1,)), ((), ())),
                    preferred_element_type=jnp.float32,
                )
                * attn_scale
            )
            scores = jnp.where(jnp.tile(allowed, (GQ, 1)), scores, -jnp.inf)
            new_peak = jnp.maximum(row_peak, jnp.max(scores, axis=1))
            weights = jnp.exp(scores - new_peak[:, None])
            factor = jnp.exp(row_peak - new_peak)
            totals = totals * factor + jnp.sum(weights, axis=1)
            accumulated = accumulated * factor[:, None] + jnp.dot(
                weights.astype(jnp.bfloat16),
                block_pairs[:, HD:],
                preferred_element_type=jnp.float32,
            )
            return (new_peak, totals, accumulated)

        start_state = (
            jnp.full((GQ * block_rows,), masked_floor, jnp.float32),
            jnp.zeros((GQ * block_rows,), jnp.float32),
            jnp.zeros((GQ * block_rows, HD), jnp.float32),
        )
        row_peak, totals, accumulated = lax.fori_loop(lowest, highest, step_keys, start_state)
        mixed = (accumulated / totals[:, None]).astype(jnp.bfloat16).reshape(GQ, block_rows, HD)
        return mixed.transpose(1, 0, 2).reshape(block_rows, GQ * HD)

    attended = lax.map(attend, jnp.arange(rows_quarter // block_rows, dtype=jnp.int32)).reshape(
        rows_quarter, GQ * HD
    )
    partial_proj = lax.dot_general(
        attended, w_attn_out, (((1,), (1,)), ((), ())), preferred_element_type=jnp.float32
    )
    projection = fold_levels(
        partial_proj,
        group_bits,
        lambda sent_rows, level_bit: partner(
            sent_rows.astype(jnp.bfloat16), TENSOR, level_bit
        ).astype(sent_rows.dtype),
    )
    after_attention = (hidden.astype(jnp.float32) + residual_scale * projection).astype(
        jnp.bfloat16
    )
    expert_in = rms_norm(after_attention, ffn_gain)
    local_experts = w_gate_up.shape[0]
    share_cols = 128 * pl.cdiv(expert_total, 128)
    carried = jnp.concatenate(
        [
            expert_in,
            share_table,
            jnp.zeros((share_table.shape[0], share_cols - expert_total), jnp.bfloat16),
        ],
        axis=1,
    )
    rows_all = lax.all_gather(carried, TENSOR, axis=0, tiled=True)
    local_shares = lax.dynamic_slice_in_dim(
        rows_all[:, model_width : model_width + expert_total],
        group_index * local_experts,
        local_experts,
        1,
    ).astype(jnp.float32)
    expert_part = dense_experts(rows_all, local_shares, w_gate_up, w_down)
    expert_sum = fold_bits(expert_part.reshape(-1, model_width), (0, 1, 3, 4, 2))
    hidden_out = (after_attention.astype(jnp.float32) + residual_scale * expert_sum).astype(
        jnp.bfloat16
    )
    return (after_attention, hidden_out, kv_block[None])


def solution(mesh):
    grid = mesh.devices.reshape(mesh.devices.shape[0], -1, 4, 2)
    mesh = jax.sharding.Mesh(grid, ("dp",) + TENSOR)
    placed = (
        P(("dp",) + TENSOR, None),
        P("dp"),
        P(("dp",) + TENSOR, None),
        P(("dp",) + TENSOR, None),
        P(),
        P(None, TENSOR),
        P(None, TENSOR),
        P(),
        P(TENSOR, None, None),
        P(TENSOR, None, None),
    )
    return jax.shard_map(
        on_device,
        mesh=mesh,
        in_specs=placed,
        out_specs=(P(("dp",) + TENSOR, None), P(("dp",) + TENSOR, None), P(TENSOR, "dp", None)),
        check_vma=False,
    )
```

```python
import math

import jax
import jax.numpy as jnp
from jax import lax
from jax.sharding import PartitionSpec as P
from jax.experimental import pallas as pl
from jax.experimental.pallas import tpu as pltpu

KVH = 8
HD = 64
GQ = 3
CHIPS = ("ty", "tx")
TENSOR = ("ty", "tx", "tc")


attn_scale = 0.015625
residual_scale = 0.22
rope_base = 10000.0
norm_eps = 1e-06
masked_floor = -1e30


def partner(value, axis, apart):
    mask = 2**apart
    pairs = [(source, source ^ mask) for source in range(lax.axis_size(axis))]
    split_axis = 0 if value.shape[0] >= value.shape[1] else 1
    pieces = 4 if value.shape[split_axis] % 32 == 0 else 1
    parts = jnp.split(value, pieces, axis=split_axis)
    moved = [lax.ppermute(part, axis, pairs) for part in parts]
    return jnp.concatenate(moved, axis=split_axis) if pieces > 1 else moved[0]


def rms_norm(row_block, gain_row):
    widened = row_block.astype(jnp.float32)
    mean_square = jnp.mean(widened * widened, axis=-1, keepdims=True)
    return (widened * lax.rsqrt(mean_square + norm_eps) * gain_row).astype(jnp.bfloat16)


def segment_starts(segment_ids):
    places = jnp.arange(segment_ids.shape[0], dtype=jnp.int32)
    earlier = jnp.concatenate([segment_ids[:1] - 1, segment_ids[:-1]])
    boundary = jnp.where(segment_ids != earlier, places, jnp.zeros_like(places))
    return lax.cummax(boundary, axis=0)


def rotate(vectors, positions):
    half_width = vectors.shape[-1] // 2
    freq_steps = jnp.arange(half_width, dtype=jnp.float32)
    frequency = jnp.exp(freq_steps * (-2.0 * math.log(rope_base) / vectors.shape[-1]))
    angles = positions.astype(jnp.float32)[:, None] * frequency[None, :]
    cosine = jnp.cos(angles)[:, None, :]
    sine_part = jnp.sin(angles)[:, None, :]
    first_half = vectors[..., :half_width]
    second_half = vectors[..., half_width:]
    return jnp.concatenate(
        [
            first_half * cosine - second_half * sine_part,
            second_half * cosine + first_half * sine_part,
        ],
        axis=-1,
    )


def gather_levels(parts, level_bits, join_axes, sender):
    index_now = lax.axis_index(TENSOR)
    for level_bit in level_bits:
        arrived = sender(parts, level_bit)
        is_upper = index_now >> level_bit & 1 == 1
        joined_parts = []
        for own_part, peer_part, join_axis in zip(parts, arrived, join_axes):
            lower_first = jnp.concatenate([own_part, peer_part], join_axis)
            upper_first = jnp.concatenate([peer_part, own_part], join_axis)
            joined_parts.append(jnp.where(is_upper, upper_first, lower_first))
        parts = tuple(joined_parts)
    return parts


def fold_levels(partial_sum, level_bits, sender):
    index_now = lax.axis_index(TENSOR)
    for level_bit in reversed(level_bits):
        half_rows = partial_sum.shape[0] // 2
        lower_rows = partial_sum[:half_rows]
        upper_rows = partial_sum[half_rows:]
        is_upper = index_now >> level_bit & 1 == 1
        kept_rows = jnp.where(is_upper, upper_rows, lower_rows)
        sent_rows = jnp.where(is_upper, lower_rows, upper_rows)
        partial_sum = kept_rows + sender(sent_rows, level_bit)
    return partial_sum


def project_pairs(row_block, w_pairs, positions):
    head_size = w_pairs.shape[1] // 2
    paired = jnp.dot(row_block, w_pairs, preferred_element_type=jnp.float32)
    rotated = rotate(paired[:, None, :head_size], positions)[:, 0]
    return jnp.concatenate([rotated, paired[:, head_size:]], axis=1).astype(jnp.bfloat16)


def expert_block(rows_ref, share_ref, gate_up_ref, down_ref, out_ref):
    model_width = gate_up_ref.shape[1]
    rows = rows_ref[:, :model_width]
    inner_width = down_ref.shape[1]
    total = jnp.zeros((rows.shape[0], model_width), jnp.float32)
    for expert in range(gate_up_ref.shape[0]):
        both = jnp.dot(rows, gate_up_ref[expert], preferred_element_type=jnp.float32)
        gate_val = both[:, :inner_width]
        up_val = both[:, inner_width:]
        inner_act = (jax.nn.silu(gate_val) * up_val).astype(jnp.bfloat16)
        produced = jnp.dot(inner_act, down_ref[expert], preferred_element_type=jnp.float32)
        total = total + share_ref[:, expert : expert + 1] * produced
    piece = out_ref.shape[3]
    for part in range(4):
        out_ref[part % 2, part // 2, 0] = total[part * piece : (part + 1) * piece].astype(
            out_ref.dtype
        )


def tile_slot(tile_number):
    return (tile_number // 2) % 2 * 4 + (tile_number // 4) % 2 * 2 + tile_number % 2


def dense_experts(rows_all, shares, gate_up, down_proj):
    row_count, carried_width = rows_all.shape
    model_width = gate_up.shape[1]
    expert_count = gate_up.shape[0]
    piece = row_count // 32
    tile = 4 * piece
    tiles = row_count // tile
    return pl.pallas_call(
        expert_block,
        grid=(tiles,),
        in_specs=[
            pl.BlockSpec((tile, carried_width), lambda i: (i, 0)),
            pl.BlockSpec((tile, expert_count), lambda i: (i, 0)),
            pl.BlockSpec(gate_up.shape, lambda i: (0, 0, 0)),
            pl.BlockSpec(down_proj.shape, lambda i: (0, 0, 0)),
        ],
        out_specs=pl.BlockSpec(
            (2, 2, 1, piece, model_width), lambda i: (0, 0, tile_slot(i), 0, 0)
        ),
        out_shape=jax.ShapeDtypeStruct((2, 2, tiles, piece, model_width), jnp.bfloat16),
        compiler_params=pltpu.CompilerParams(vmem_limit_bytes=48 * 1024 * 1024),
    )(rows_all, shares, gate_up, down_proj)


def fold_bits(partial_sum, level_bits):
    index_now = lax.axis_index(TENSOR)
    for level_bit in level_bits:
        half_rows = partial_sum.shape[0] // 2
        lower_rows = partial_sum[:half_rows]
        upper_rows = partial_sum[half_rows:]
        is_upper = index_now >> level_bit & 1 == 1
        kept_rows = jnp.where(is_upper, upper_rows, lower_rows)
        sent_rows = jnp.where(is_upper, lower_rows, upper_rows)
        arrived = partner(sent_rows.astype(jnp.bfloat16), TENSOR, level_bit)
        partial_sum = kept_rows.astype(jnp.float32) + arrived.astype(jnp.float32)
    return partial_sum

def on_device(
    hidden, segment_ids, routes, route_weights, attn_gain, w_qkv, w_out, ffn_gain, w_gate_up, w_down
):
    device_count = lax.axis_size(TENSOR)
    quarters = device_count // KVH
    index_now = lax.axis_index(TENSOR)
    quarter_index = index_now // KVH
    group_index = index_now % KVH
    group_bits = list(range(KVH.bit_length() - 1))
    quarter_bits = list(range(len(group_bits), device_count.bit_length() - 1))
    seq_len = segment_ids.shape[0]
    rows_quarter = seq_len // quarters
    model_width = hidden.shape[1]
    starts = segment_starts(segment_ids)
    expert_total = w_gate_up.shape[0] * KVH
    expert_ids = jnp.arange(expert_total, dtype=jnp.int32)
    share_table = jnp.sum(
        jnp.where(
            routes[:, None, :] == expert_ids[None, :, None],
            route_weights[:, None, :],
            jnp.zeros((), route_weights.dtype),
        ),
        axis=2,
    )
    positions = jnp.arange(seq_len, dtype=jnp.int32) - starts
    own_positions = lax.dynamic_slice_in_dim(
        positions, quarter_index * rows_quarter, rows_quarter, 0
    )
    normed = rms_norm(hidden, attn_gain)
    qkv_width = w_qkv.shape[1]
    joined = jnp.concatenate([w_qkv, w_out], axis=1)
    (gathered_cols,) = gather_levels(
        (joined,),
        quarter_bits,
        (1,),
        lambda payload, level_bit: (partner(payload[0], TENSOR, level_bit),),
    )
    by_quarter = gathered_cols.reshape(model_width, quarters, joined.shape[1])
    w_group = by_quarter[:, :, :qkv_width].reshape(model_width, quarters * qkv_width)
    w_attn_out = by_quarter[:, :, qkv_width:].reshape(model_width, GQ * HD)
    w_query = w_group[:, : GQ * HD]
    w_pairs = w_group[:, GQ * HD :]
    all_rows = lax.all_gather(normed, TENSOR, axis=0, tiled=True)
    own_rows = lax.dynamic_slice_in_dim(all_rows, quarter_index * rows_quarter, rows_quarter, 0)
    key_values = project_pairs(all_rows, w_pairs, positions)
    kv_block = lax.dynamic_slice_in_dim(key_values, quarter_index * rows_quarter, rows_quarter, 0)
    query_proj = jnp.dot(own_rows, w_query, preferred_element_type=jnp.float32).reshape(
        rows_quarter, GQ, HD
    )
    queries_heads = rotate(query_proj, own_positions).astype(jnp.bfloat16).transpose(1, 0, 2)
    block_rows = min(256, rows_quarter)
    key_block = min(512, seq_len)

    def attend(block_number):
        first_row = block_number * block_rows
        block_queries = lax.dynamic_slice_in_dim(queries_heads, first_row, block_rows, 1).reshape(
            GQ * block_rows, HD
        )
        first_place = quarter_index * rows_quarter + first_row
        query_places = first_place + jnp.arange(block_rows, dtype=jnp.int32)
        query_starts = lax.dynamic_slice_in_dim(starts, first_place, block_rows, 0)
        lowest = query_starts[0] // key_block
        highest = (first_place + block_rows - 1) // key_block + 1

        def step_keys(key_number, loop_state):
            row_peak, totals, accumulated = loop_state
            key_offset = key_number * key_block
            block_pairs = lax.dynamic_slice_in_dim(key_values, key_offset, key_block, 0)
            key_places = key_offset + jnp.arange(key_block, dtype=jnp.int32)
            allowed = (key_places[None, :] <= query_places[:, None]) & (
                key_places[None, :] >= query_starts[:, None]
            )
            scores = (
                lax.dot_general(
                    block_queries,
                    block_pairs[:, :HD],
                    (((1,), (1,)), ((), ())),
                    preferred_element_type=jnp.float32,
                )
                * attn_scale
            )
            scores = jnp.where(jnp.tile(allowed, (GQ, 1)), scores, -jnp.inf)
            new_peak = jnp.maximum(row_peak, jnp.max(scores, axis=1))
            weights = jnp.exp(scores - new_peak[:, None])
            factor = jnp.exp(row_peak - new_peak)
            totals = totals * factor + jnp.sum(weights, axis=1)
            accumulated = accumulated * factor[:, None] + jnp.dot(
                weights.astype(jnp.bfloat16),
                block_pairs[:, HD:],
                preferred_element_type=jnp.float32,
            )
            return (new_peak, totals, accumulated)

        start_state = (
            jnp.full((GQ * block_rows,), masked_floor, jnp.float32),
            jnp.zeros((GQ * block_rows,), jnp.float32),
            jnp.zeros((GQ * block_rows, HD), jnp.float32),
        )
        row_peak, totals, accumulated = lax.fori_loop(lowest, highest, step_keys, start_state)
        mixed = (accumulated / totals[:, None]).astype(jnp.bfloat16).reshape(GQ, block_rows, HD)
        return mixed.transpose(1, 0, 2).reshape(block_rows, GQ * HD)

    attended = lax.map(attend, jnp.arange(rows_quarter // block_rows, dtype=jnp.int32)).reshape(
        rows_quarter, GQ * HD
    )
    partial_proj = lax.dot_general(
        attended, w_attn_out, (((1,), (1,)), ((), ())), preferred_element_type=jnp.float32
    )
    projection = fold_levels(
        partial_proj,
        group_bits,
        lambda sent_rows, level_bit: partner(
            sent_rows.astype(jnp.bfloat16), TENSOR, level_bit
        ).astype(sent_rows.dtype),
    )
    after_attention = (hidden.astype(jnp.float32) + residual_scale * projection).astype(
        jnp.bfloat16
    )
    expert_in = rms_norm(after_attention, ffn_gain)
    local_experts = w_gate_up.shape[0]
    share_cols = 128 * pl.cdiv(expert_total, 128)
    carried = jnp.concatenate(
        [
            expert_in,
            share_table,
            jnp.zeros((share_table.shape[0], share_cols - expert_total), jnp.bfloat16),
        ],
        axis=1,
    )
    rows_all = lax.all_gather(carried, TENSOR, axis=0, tiled=True)
    local_shares = lax.dynamic_slice_in_dim(
        rows_all[:, model_width : model_width + expert_total],
        group_index * local_experts,
        local_experts,
        1,
    ).astype(jnp.float32)
    expert_part = dense_experts(rows_all, local_shares, w_gate_up, w_down)
    expert_sum = fold_bits(expert_part.reshape(-1, model_width), (0, 1, 3, 4, 2))
    hidden_out = (after_attention.astype(jnp.float32) + residual_scale * expert_sum).astype(
        jnp.bfloat16
    )
    return (after_attention, hidden_out, kv_block[None])


def solution(mesh):
    grid = mesh.devices.reshape(mesh.devices.shape[0], -1, 4, 2)
    mesh = jax.sharding.Mesh(grid, ("dp",) + TENSOR)
    placed = (
        P(("dp",) + TENSOR, None),
        P("dp"),
        P(("dp",) + TENSOR, None),
        P(("dp",) + TENSOR, None),
        P(),
        P(None, TENSOR),
        P(None, TENSOR),
        P(),
        P(TENSOR, None, None),
        P(TENSOR, None, None),
    )
    return jax.shard_map(
        on_device,
        mesh=mesh,
        in_specs=placed,
        out_specs=(P(("dp",) + TENSOR, None), P(("dp",) + TENSOR, None), P(TENSOR, "dp", None)),
        check_vma=False,
    )
```

```python
import math

import jax
import jax.numpy as jnp
from jax import lax
from jax.sharding import PartitionSpec as P
from jax.experimental import pallas as pl
from jax.experimental.pallas import tpu as pltpu

KVH = 8
HD = 64
GQ = 3
CHIPS = ("ty", "tx")
TENSOR = ("ty", "tx", "tc")


attn_scale = 0.015625
residual_scale = 0.22
rope_base = 10000.0
norm_eps = 1e-06
masked_floor = -1e30


def partner(value, axis, apart):
    mask = 2**apart
    pairs = [(source, source ^ mask) for source in range(lax.axis_size(axis))]
    return lax.ppermute(value, axis, pairs)


def rms_norm(row_block, gain_row):
    widened = row_block.astype(jnp.float32)
    mean_square = jnp.mean(widened * widened, axis=-1, keepdims=True)
    return (widened * lax.rsqrt(mean_square + norm_eps) * gain_row).astype(jnp.bfloat16)


def segment_starts(segment_ids):
    places = jnp.arange(segment_ids.shape[0], dtype=jnp.int32)
    earlier = jnp.concatenate([segment_ids[:1] - 1, segment_ids[:-1]])
    boundary = jnp.where(segment_ids != earlier, places, jnp.zeros_like(places))
    return lax.cummax(boundary, axis=0)


def rotate(vectors, positions):
    half_width = vectors.shape[-1] // 2
    freq_steps = jnp.arange(half_width, dtype=jnp.float32)
    frequency = jnp.exp(freq_steps * (-2.0 * math.log(rope_base) / vectors.shape[-1]))
    angles = positions.astype(jnp.float32)[:, None] * frequency[None, :]
    cosine = jnp.cos(angles)[:, None, :]
    sine_part = jnp.sin(angles)[:, None, :]
    first_half = vectors[..., :half_width]
    second_half = vectors[..., half_width:]
    return jnp.concatenate(
        [
            first_half * cosine - second_half * sine_part,
            second_half * cosine + first_half * sine_part,
        ],
        axis=-1,
    )


def gather_levels(parts, level_bits, join_axes, sender):
    index_now = lax.axis_index(TENSOR)
    for level_bit in level_bits:
        arrived = sender(parts, level_bit)
        is_upper = index_now >> level_bit & 1 == 1
        joined_parts = []
        for own_part, peer_part, join_axis in zip(parts, arrived, join_axes):
            lower_first = jnp.concatenate([own_part, peer_part], join_axis)
            upper_first = jnp.concatenate([peer_part, own_part], join_axis)
            joined_parts.append(jnp.where(is_upper, upper_first, lower_first))
        parts = tuple(joined_parts)
    return parts


def fold_levels(partial_sum, level_bits, sender):
    index_now = lax.axis_index(TENSOR)
    for level_bit in reversed(level_bits):
        half_rows = partial_sum.shape[0] // 2
        lower_rows = partial_sum[:half_rows]
        upper_rows = partial_sum[half_rows:]
        is_upper = index_now >> level_bit & 1 == 1
        kept_rows = jnp.where(is_upper, upper_rows, lower_rows)
        sent_rows = jnp.where(is_upper, lower_rows, upper_rows)
        partial_sum = kept_rows + sender(sent_rows, level_bit)
    return partial_sum


def project_pairs(row_block, w_pairs, positions):
    head_size = w_pairs.shape[1] // 2
    paired = jnp.dot(row_block, w_pairs, preferred_element_type=jnp.float32)
    rotated = rotate(paired[:, None, :head_size], positions)[:, 0]
    return jnp.concatenate([rotated, paired[:, head_size:]], axis=1).astype(jnp.bfloat16)


def expert_block(rows_ref, share_ref, gate_up_ref, down_ref, out_ref):
    model_width = gate_up_ref.shape[1]
    rows = rows_ref[:, :model_width]
    inner_width = down_ref.shape[1]
    total = jnp.zeros((rows.shape[0], model_width), jnp.float32)
    for expert in range(gate_up_ref.shape[0]):
        both = jnp.dot(rows, gate_up_ref[expert], preferred_element_type=jnp.float32)
        gate_val = both[:, :inner_width]
        up_val = both[:, inner_width:]
        inner_act = (jax.nn.silu(gate_val) * up_val).astype(jnp.bfloat16)
        produced = jnp.dot(inner_act, down_ref[expert], preferred_element_type=jnp.float32)
        total = total + share_ref[:, expert : expert + 1] * produced
    piece = out_ref.shape[3]
    for part in range(4):
        out_ref[part % 2, part // 2, 0] = total[part * piece : (part + 1) * piece].astype(
            out_ref.dtype
        )


def tile_slot(tile_number):
    return (tile_number // 2) % 2 * 4 + (tile_number // 4) % 2 * 2 + tile_number % 2


def dense_experts(rows_all, shares, gate_up, down_proj):
    row_count, carried_width = rows_all.shape
    model_width = gate_up.shape[1]
    expert_count = gate_up.shape[0]
    piece = row_count // 32
    tile = 4 * piece
    tiles = row_count // tile
    return pl.pallas_call(
        expert_block,
        grid=(tiles,),
        in_specs=[
            pl.BlockSpec((tile, carried_width), lambda i: (i, 0)),
            pl.BlockSpec((tile, expert_count), lambda i: (i, 0)),
            pl.BlockSpec(gate_up.shape, lambda i: (0, 0, 0)),
            pl.BlockSpec(down_proj.shape, lambda i: (0, 0, 0)),
        ],
        out_specs=pl.BlockSpec(
            (2, 2, 1, piece, model_width), lambda i: (0, 0, tile_slot(i), 0, 0)
        ),
        out_shape=jax.ShapeDtypeStruct((2, 2, tiles, piece, model_width), jnp.bfloat16),
        compiler_params=pltpu.CompilerParams(vmem_limit_bytes=48 * 1024 * 1024),
    )(rows_all, shares, gate_up, down_proj)


def fold_bits(partial_sum, level_bits):
    index_now = lax.axis_index(TENSOR)
    for level_bit in level_bits:
        half_rows = partial_sum.shape[0] // 2
        lower_rows = partial_sum[:half_rows]
        upper_rows = partial_sum[half_rows:]
        is_upper = index_now >> level_bit & 1 == 1
        kept_rows = jnp.where(is_upper, upper_rows, lower_rows)
        sent_rows = jnp.where(is_upper, lower_rows, upper_rows)
        arrived = partner(sent_rows.astype(jnp.bfloat16), TENSOR, level_bit)
        partial_sum = kept_rows.astype(jnp.float32) + arrived.astype(jnp.float32)
    return partial_sum

def on_device(
    hidden, segment_ids, routes, route_weights, attn_gain, w_qkv, w_out, ffn_gain, w_gate_up, w_down
):
    device_count = lax.axis_size(TENSOR)
    quarters = device_count // KVH
    index_now = lax.axis_index(TENSOR)
    quarter_index = index_now // KVH
    group_index = index_now % KVH
    group_bits = list(range(KVH.bit_length() - 1))
    quarter_bits = list(range(len(group_bits), device_count.bit_length() - 1))
    seq_len = segment_ids.shape[0]
    rows_quarter = seq_len // quarters
    model_width = hidden.shape[1]
    starts = segment_starts(segment_ids)
    expert_total = w_gate_up.shape[0] * KVH
    expert_ids = jnp.arange(expert_total, dtype=jnp.int32)
    share_table = jnp.sum(
        jnp.where(
            routes[:, None, :] == expert_ids[None, :, None],
            route_weights[:, None, :],
            jnp.zeros((), route_weights.dtype),
        ),
        axis=2,
    )
    positions = jnp.arange(seq_len, dtype=jnp.int32) - starts
    own_positions = lax.dynamic_slice_in_dim(
        positions, quarter_index * rows_quarter, rows_quarter, 0
    )
    normed = rms_norm(hidden, attn_gain)
    qkv_width = w_qkv.shape[1]
    joined = jnp.concatenate([w_qkv, w_out], axis=1)
    (gathered_cols,) = gather_levels(
        (joined,),
        quarter_bits,
        (1,),
        lambda payload, level_bit: (partner(payload[0], TENSOR, level_bit),),
    )
    by_quarter = gathered_cols.reshape(model_width, quarters, joined.shape[1])
    w_group = by_quarter[:, :, :qkv_width].reshape(model_width, quarters * qkv_width)
    w_attn_out = by_quarter[:, :, qkv_width:].reshape(model_width, GQ * HD)
    w_query = w_group[:, : GQ * HD]
    w_pairs = w_group[:, GQ * HD :]
    (own_rows,) = gather_levels(
        (normed,),
        group_bits,
        (0,),
        lambda payload, level_bit: (partner(payload[0], TENSOR, level_bit),),
    )
    kv_block = project_pairs(own_rows, w_pairs, own_positions)
    (key_values,) = gather_levels(
        (kv_block,),
        quarter_bits,
        (0,),
        lambda payload, level_bit: (partner(payload[0], TENSOR, level_bit),),
    )
    query_proj = jnp.dot(own_rows, w_query, preferred_element_type=jnp.float32).reshape(
        rows_quarter, GQ, HD
    )
    queries_heads = rotate(query_proj, own_positions).astype(jnp.bfloat16).transpose(1, 0, 2)
    block_rows = min(256, rows_quarter)
    key_block = min(512, seq_len)

    def attend(block_number):
        first_row = block_number * block_rows
        block_queries = lax.dynamic_slice_in_dim(queries_heads, first_row, block_rows, 1).reshape(
            GQ * block_rows, HD
        )
        first_place = quarter_index * rows_quarter + first_row
        query_places = first_place + jnp.arange(block_rows, dtype=jnp.int32)
        query_starts = lax.dynamic_slice_in_dim(starts, first_place, block_rows, 0)
        lowest = query_starts[0] // key_block
        highest = (first_place + block_rows - 1) // key_block + 1

        def step_keys(key_number, loop_state):
            row_peak, totals, accumulated = loop_state
            key_offset = key_number * key_block
            block_pairs = lax.dynamic_slice_in_dim(key_values, key_offset, key_block, 0)
            key_places = key_offset + jnp.arange(key_block, dtype=jnp.int32)
            allowed = (key_places[None, :] <= query_places[:, None]) & (
                key_places[None, :] >= query_starts[:, None]
            )
            scores = (
                lax.dot_general(
                    block_queries,
                    block_pairs[:, :HD],
                    (((1,), (1,)), ((), ())),
                    preferred_element_type=jnp.float32,
                )
                * attn_scale
            )
            scores = jnp.where(jnp.tile(allowed, (GQ, 1)), scores, -jnp.inf)
            new_peak = jnp.maximum(row_peak, jnp.max(scores, axis=1))
            weights = jnp.exp(scores - new_peak[:, None])
            factor = jnp.exp(row_peak - new_peak)
            totals = totals * factor + jnp.sum(weights, axis=1)
            accumulated = accumulated * factor[:, None] + jnp.dot(
                weights.astype(jnp.bfloat16),
                block_pairs[:, HD:],
                preferred_element_type=jnp.float32,
            )
            return (new_peak, totals, accumulated)

        start_state = (
            jnp.full((GQ * block_rows,), masked_floor, jnp.float32),
            jnp.zeros((GQ * block_rows,), jnp.float32),
            jnp.zeros((GQ * block_rows, HD), jnp.float32),
        )
        row_peak, totals, accumulated = lax.fori_loop(lowest, highest, step_keys, start_state)
        mixed = (accumulated / totals[:, None]).astype(jnp.bfloat16).reshape(GQ, block_rows, HD)
        return mixed.transpose(1, 0, 2).reshape(block_rows, GQ * HD)

    attended = lax.map(attend, jnp.arange(rows_quarter // block_rows, dtype=jnp.int32)).reshape(
        rows_quarter, GQ * HD
    )
    partial_proj = lax.dot_general(
        attended, w_attn_out, (((1,), (1,)), ((), ())), preferred_element_type=jnp.float32
    )
    projection = fold_levels(
        partial_proj,
        group_bits,
        lambda sent_rows, level_bit: partner(
            sent_rows.astype(jnp.bfloat16), TENSOR, level_bit
        ).astype(sent_rows.dtype),
    )
    after_attention = (hidden.astype(jnp.float32) + residual_scale * projection).astype(
        jnp.bfloat16
    )
    expert_in = rms_norm(after_attention, ffn_gain)
    local_experts = w_gate_up.shape[0]
    share_cols = 128 * pl.cdiv(expert_total, 128)
    carried = jnp.concatenate(
        [
            expert_in,
            share_table,
            jnp.zeros((share_table.shape[0], share_cols - expert_total), jnp.bfloat16),
        ],
        axis=1,
    )
    rows_all = lax.all_gather(carried, TENSOR, axis=0, tiled=True)
    local_shares = lax.dynamic_slice_in_dim(
        rows_all[:, model_width : model_width + expert_total],
        group_index * local_experts,
        local_experts,
        1,
    ).astype(jnp.float32)
    expert_part = dense_experts(rows_all, local_shares, w_gate_up, w_down)
    expert_sum = fold_bits(expert_part.reshape(-1, model_width), (0, 1, 3, 4, 2))
    hidden_out = (after_attention.astype(jnp.float32) + residual_scale * expert_sum).astype(
        jnp.bfloat16
    )
    return (after_attention, hidden_out, kv_block[None])


def solution(mesh):
    grid = mesh.devices.reshape(mesh.devices.shape[0], -1, 4, 2)
    mesh = jax.sharding.Mesh(grid, ("dp",) + TENSOR)
    placed = (
        P(("dp",) + TENSOR, None),
        P("dp"),
        P(("dp",) + TENSOR, None),
        P(("dp",) + TENSOR, None),
        P(),
        P(None, TENSOR),
        P(None, TENSOR),
        P(),
        P(TENSOR, None, None),
        P(TENSOR, None, None),
    )
    return jax.shard_map(
        on_device,
        mesh=mesh,
        in_specs=placed,
        out_specs=(P(("dp",) + TENSOR, None), P(("dp",) + TENSOR, None), P(TENSOR, "dp", None)),
        check_vma=False,
    )
```

```python
import math

import jax
import jax.numpy as jnp
from jax import lax
from jax.sharding import PartitionSpec as P
from jax.experimental import pallas as pl
from jax.experimental.pallas import tpu as pltpu

KVH = 8
HD = 64
GQ = 3
CHIPS = ("ty", "tx")
TENSOR = ("ty", "tx", "tc")


attn_scale = 0.015625
residual_scale = 0.22
rope_base = 10000.0
norm_eps = 1e-06
masked_floor = -1e30


def partner(value, axis, apart):
    mask = 2**apart
    pairs = [(source, source ^ mask) for source in range(lax.axis_size(axis))]
    return lax.ppermute(value, axis, pairs)


def rms_norm(row_block, gain_row):
    widened = row_block.astype(jnp.float32)
    mean_square = jnp.mean(widened * widened, axis=-1, keepdims=True)
    return (widened * lax.rsqrt(mean_square + norm_eps) * gain_row).astype(jnp.bfloat16)


def segment_starts(segment_ids):
    places = jnp.arange(segment_ids.shape[0], dtype=jnp.int32)
    earlier = jnp.concatenate([segment_ids[:1] - 1, segment_ids[:-1]])
    boundary = jnp.where(segment_ids != earlier, places, jnp.zeros_like(places))
    return lax.cummax(boundary, axis=0)


def rotate(vectors, positions):
    half_width = vectors.shape[-1] // 2
    freq_steps = jnp.arange(half_width, dtype=jnp.float32)
    frequency = jnp.exp(freq_steps * (-2.0 * math.log(rope_base) / vectors.shape[-1]))
    angles = positions.astype(jnp.float32)[:, None] * frequency[None, :]
    cosine = jnp.cos(angles)[:, None, :]
    sine_part = jnp.sin(angles)[:, None, :]
    first_half = vectors[..., :half_width]
    second_half = vectors[..., half_width:]
    return jnp.concatenate(
        [
            first_half * cosine - second_half * sine_part,
            second_half * cosine + first_half * sine_part,
        ],
        axis=-1,
    )


def gather_levels(parts, level_bits, join_axes, sender):
    index_now = lax.axis_index(TENSOR)
    for level_bit in level_bits:
        arrived = sender(parts, level_bit)
        is_upper = index_now >> level_bit & 1 == 1
        joined_parts = []
        for own_part, peer_part, join_axis in zip(parts, arrived, join_axes):
            lower_first = jnp.concatenate([own_part, peer_part], join_axis)
            upper_first = jnp.concatenate([peer_part, own_part], join_axis)
            joined_parts.append(jnp.where(is_upper, upper_first, lower_first))
        parts = tuple(joined_parts)
    return parts


def fold_levels(partial_sum, level_bits, sender):
    index_now = lax.axis_index(TENSOR)
    for level_bit in reversed(level_bits):
        half_rows = partial_sum.shape[0] // 2
        lower_rows = partial_sum[:half_rows]
        upper_rows = partial_sum[half_rows:]
        is_upper = index_now >> level_bit & 1 == 1
        kept_rows = jnp.where(is_upper, upper_rows, lower_rows)
        sent_rows = jnp.where(is_upper, lower_rows, upper_rows)
        partial_sum = kept_rows + sender(sent_rows, level_bit)
    return partial_sum


def fold_any(partial_sum, layout_bits, level_bits):
    index_now = lax.axis_index(TENSOR)
    rows_left = partial_sum.shape[0] >> len(layout_bits)
    state = partial_sum.reshape((2,) * len(layout_bits) + (rows_left,) + partial_sum.shape[1:])
    dims = list(layout_bits)
    for level_bit in level_bits:
        place = dims.index(level_bit)
        lower_rows = lax.index_in_dim(state, 0, place, keepdims=False)
        upper_rows = lax.index_in_dim(state, 1, place, keepdims=False)
        is_upper = index_now >> level_bit & 1 == 1
        kept_rows = jnp.where(is_upper, upper_rows, lower_rows)
        sent_rows = jnp.where(is_upper, lower_rows, upper_rows)
        arrived = partner(sent_rows.astype(jnp.bfloat16), TENSOR, level_bit)
        state = kept_rows.astype(jnp.float32) + arrived.astype(jnp.float32)
        dims.pop(place)
    return state.reshape((rows_left,) + partial_sum.shape[1:])


def project_pairs(row_block, w_pairs, positions):
    head_size = w_pairs.shape[1] // 2
    paired = jnp.dot(row_block, w_pairs, preferred_element_type=jnp.float32)
    rotated = rotate(paired[:, None, :head_size], positions)[:, 0]
    return jnp.concatenate([rotated, paired[:, head_size:]], axis=1).astype(jnp.bfloat16)


def expert_block(rows_ref, share_ref, gate_up_ref, down_ref, out_ref):
    model_width = gate_up_ref.shape[1]
    rows = rows_ref[:, :model_width]
    inner_width = down_ref.shape[1]
    total = jnp.zeros((rows.shape[0], model_width), jnp.float32)
    for expert in range(gate_up_ref.shape[0]):
        both = jnp.dot(rows, gate_up_ref[expert], preferred_element_type=jnp.float32)
        gate_val = both[:, :inner_width]
        up_val = both[:, inner_width:]
        inner_act = (jax.nn.silu(gate_val) * up_val).astype(jnp.bfloat16)
        produced = jnp.dot(inner_act, down_ref[expert], preferred_element_type=jnp.float32)
        total = total + share_ref[:, expert : expert + 1] * produced
    piece = out_ref.shape[3]
    for part in range(4):
        out_ref[part % 2, part // 2, 0] = total[part * piece : (part + 1) * piece].astype(
            out_ref.dtype
        )


def tile_slot(tile_number):
    return (tile_number // 2) % 2 * 4 + (tile_number // 4) % 2 * 2 + tile_number % 2


def dense_experts(rows_all, shares, gate_up, down_proj):
    row_count, carried_width = rows_all.shape
    model_width = gate_up.shape[1]
    expert_count = gate_up.shape[0]
    piece = row_count // 32
    tile = 4 * piece
    tiles = row_count // tile
    return pl.pallas_call(
        expert_block,
        grid=(tiles,),
        in_specs=[
            pl.BlockSpec((tile, carried_width), lambda i: (i, 0)),
            pl.BlockSpec((tile, expert_count), lambda i: (i, 0)),
            pl.BlockSpec(gate_up.shape, lambda i: (0, 0, 0)),
            pl.BlockSpec(down_proj.shape, lambda i: (0, 0, 0)),
        ],
        out_specs=pl.BlockSpec(
            (2, 2, 1, piece, model_width), lambda i: (0, 0, tile_slot(i), 0, 0)
        ),
        out_shape=jax.ShapeDtypeStruct((2, 2, tiles, piece, model_width), jnp.bfloat16),
        compiler_params=pltpu.CompilerParams(vmem_limit_bytes=48 * 1024 * 1024),
    )(rows_all, shares, gate_up, down_proj)


def fold_bits(partial_sum, level_bits):
    index_now = lax.axis_index(TENSOR)
    for level_bit in level_bits:
        half_rows = partial_sum.shape[0] // 2
        lower_rows = partial_sum[:half_rows]
        upper_rows = partial_sum[half_rows:]
        is_upper = index_now >> level_bit & 1 == 1
        kept_rows = jnp.where(is_upper, upper_rows, lower_rows)
        sent_rows = jnp.where(is_upper, lower_rows, upper_rows)
        arrived = partner(sent_rows.astype(jnp.bfloat16), TENSOR, level_bit)
        partial_sum = kept_rows.astype(jnp.float32) + arrived.astype(jnp.float32)
    return partial_sum

def on_device(
    hidden, segment_ids, routes, route_weights, attn_gain, w_qkv, w_out, ffn_gain, w_gate_up, w_down
):
    device_count = lax.axis_size(TENSOR)
    quarters = device_count // KVH
    index_now = lax.axis_index(TENSOR)
    quarter_index = index_now // KVH
    group_index = index_now % KVH
    group_bits = list(range(KVH.bit_length() - 1))
    quarter_bits = list(range(len(group_bits), device_count.bit_length() - 1))
    seq_len = segment_ids.shape[0]
    rows_quarter = seq_len // quarters
    model_width = hidden.shape[1]
    starts = segment_starts(segment_ids)
    expert_total = w_gate_up.shape[0] * KVH
    expert_ids = jnp.arange(expert_total, dtype=jnp.int32)
    share_table = jnp.sum(
        jnp.where(
            routes[:, None, :] == expert_ids[None, :, None],
            route_weights[:, None, :],
            jnp.zeros((), route_weights.dtype),
        ),
        axis=2,
    )
    positions = jnp.arange(seq_len, dtype=jnp.int32) - starts
    own_positions = lax.dynamic_slice_in_dim(
        positions, quarter_index * rows_quarter, rows_quarter, 0
    )
    normed = rms_norm(hidden, attn_gain)
    qkv_width = w_qkv.shape[1]
    joined = jnp.concatenate([w_qkv, w_out], axis=1)
    (gathered_cols,) = gather_levels(
        (joined,),
        quarter_bits,
        (1,),
        lambda payload, level_bit: (partner(payload[0], TENSOR, level_bit),),
    )
    by_quarter = gathered_cols.reshape(model_width, quarters, joined.shape[1])
    w_group = by_quarter[:, :, :qkv_width].reshape(model_width, quarters * qkv_width)
    w_attn_out = by_quarter[:, :, qkv_width:].reshape(model_width, GQ * HD)
    w_query = w_group[:, : GQ * HD]
    w_pairs = w_group[:, GQ * HD :]
    (own_rows,) = gather_levels(
        (normed,),
        group_bits,
        (0,),
        lambda payload, level_bit: (partner(payload[0], TENSOR, level_bit),),
    )
    kv_block = project_pairs(own_rows, w_pairs, own_positions)
    (key_values,) = gather_levels(
        (kv_block,),
        quarter_bits,
        (0,),
        lambda payload, level_bit: (partner(payload[0], TENSOR, level_bit),),
    )
    query_proj = jnp.dot(own_rows, w_query, preferred_element_type=jnp.float32).reshape(
        rows_quarter, GQ, HD
    )
    queries_heads = rotate(query_proj, own_positions).astype(jnp.bfloat16).transpose(1, 0, 2)
    block_rows = min(256, rows_quarter)
    key_block = min(512, seq_len)

    def attend(block_number):
        first_row = block_number * block_rows
        block_queries = lax.dynamic_slice_in_dim(queries_heads, first_row, block_rows, 1).reshape(
            GQ * block_rows, HD
        )
        first_place = quarter_index * rows_quarter + first_row
        query_places = first_place + jnp.arange(block_rows, dtype=jnp.int32)
        query_starts = lax.dynamic_slice_in_dim(starts, first_place, block_rows, 0)
        lowest = query_starts[0] // key_block
        highest = (first_place + block_rows - 1) // key_block + 1

        def step_keys(key_number, loop_state):
            row_peak, totals, accumulated = loop_state
            key_offset = key_number * key_block
            block_pairs = lax.dynamic_slice_in_dim(key_values, key_offset, key_block, 0)
            key_places = key_offset + jnp.arange(key_block, dtype=jnp.int32)
            allowed = (key_places[None, :] <= query_places[:, None]) & (
                key_places[None, :] >= query_starts[:, None]
            )
            scores = (
                lax.dot_general(
                    block_queries,
                    block_pairs[:, :HD],
                    (((1,), (1,)), ((), ())),
                    preferred_element_type=jnp.float32,
                )
                * attn_scale
            )
            scores = jnp.where(jnp.tile(allowed, (GQ, 1)), scores, -jnp.inf)
            new_peak = jnp.maximum(row_peak, jnp.max(scores, axis=1))
            weights = jnp.exp(scores - new_peak[:, None])
            factor = jnp.exp(row_peak - new_peak)
            totals = totals * factor + jnp.sum(weights, axis=1)
            accumulated = accumulated * factor[:, None] + jnp.dot(
                weights.astype(jnp.bfloat16),
                block_pairs[:, HD:],
                preferred_element_type=jnp.float32,
            )
            return (new_peak, totals, accumulated)

        start_state = (
            jnp.full((GQ * block_rows,), masked_floor, jnp.float32),
            jnp.zeros((GQ * block_rows,), jnp.float32),
            jnp.zeros((GQ * block_rows, HD), jnp.float32),
        )
        row_peak, totals, accumulated = lax.fori_loop(lowest, highest, step_keys, start_state)
        mixed = (accumulated / totals[:, None]).astype(jnp.bfloat16).reshape(GQ, block_rows, HD)
        return mixed.transpose(1, 0, 2).reshape(block_rows, GQ * HD)

    attended = lax.map(attend, jnp.arange(rows_quarter // block_rows, dtype=jnp.int32)).reshape(
        rows_quarter, GQ * HD
    )
    partial_proj = lax.dot_general(
        attended, w_attn_out, (((1,), (1,)), ((), ())), preferred_element_type=jnp.float32
    )
    projection = fold_any(partial_proj, group_bits[::-1], group_bits)
    after_attention = (hidden.astype(jnp.float32) + residual_scale * projection).astype(
        jnp.bfloat16
    )
    expert_in = rms_norm(after_attention, ffn_gain)
    local_experts = w_gate_up.shape[0]
    share_cols = 128 * pl.cdiv(expert_total, 128)
    carried = jnp.concatenate(
        [
            expert_in,
            share_table,
            jnp.zeros((share_table.shape[0], share_cols - expert_total), jnp.bfloat16),
        ],
        axis=1,
    )
    rows_all = lax.all_gather(carried, TENSOR, axis=0, tiled=True)
    local_shares = lax.dynamic_slice_in_dim(
        rows_all[:, model_width : model_width + expert_total],
        group_index * local_experts,
        local_experts,
        1,
    ).astype(jnp.float32)
    expert_part = dense_experts(rows_all, local_shares, w_gate_up, w_down)
    flat_part = expert_part.reshape(-1, model_width)
    half_width = model_width // 2
    layout = (0, 1, 3, 4, 2)
    expert_sum = jnp.concatenate(
        [
            fold_any(flat_part[:, :half_width], layout, (0, 1, 3, 4, 2)),
            fold_any(flat_part[:, half_width:], layout, (0, 3, 1, 2, 4)),
        ],
        axis=1,
    )
    hidden_out = (after_attention.astype(jnp.float32) + residual_scale * expert_sum).astype(
        jnp.bfloat16
    )
    return (after_attention, hidden_out, kv_block[None])


def solution(mesh):
    grid = mesh.devices.reshape(mesh.devices.shape[0], -1, 4, 2)
    mesh = jax.sharding.Mesh(grid, ("dp",) + TENSOR)
    placed = (
        P(("dp",) + TENSOR, None),
        P("dp"),
        P(("dp",) + TENSOR, None),
        P(("dp",) + TENSOR, None),
        P(),
        P(None, TENSOR),
        P(None, TENSOR),
        P(),
        P(TENSOR, None, None),
        P(TENSOR, None, None),
    )
    return jax.shard_map(
        on_device,
        mesh=mesh,
        in_specs=placed,
        out_specs=(P(("dp",) + TENSOR, None), P(("dp",) + TENSOR, None), P(TENSOR, "dp", None)),
        check_vma=False,
    )
```

```python
import math

import jax
import jax.numpy as jnp
from jax import lax
from jax.sharding import PartitionSpec as P
from jax.experimental import pallas as pl
from jax.experimental.pallas import tpu as pltpu

KVH = 8
HD = 64
GQ = 3
CHIPS = ("ty", "tx")
TENSOR = ("ty", "tx", "tc")


attn_scale = 0.015625
residual_scale = 0.22
rope_base = 10000.0
norm_eps = 1e-06
masked_floor = -1e30


def partner(value, axis, apart):
    mask = 2**apart
    pairs = [(source, source ^ mask) for source in range(lax.axis_size(axis))]
    return lax.ppermute(value, axis, pairs)


def rms_norm(row_block, gain_row):
    widened = row_block.astype(jnp.float32)
    mean_square = jnp.mean(widened * widened, axis=-1, keepdims=True)
    return (widened * lax.rsqrt(mean_square + norm_eps) * gain_row).astype(jnp.bfloat16)


def segment_starts(segment_ids):
    places = jnp.arange(segment_ids.shape[0], dtype=jnp.int32)
    earlier = jnp.concatenate([segment_ids[:1] - 1, segment_ids[:-1]])
    boundary = jnp.where(segment_ids != earlier, places, jnp.zeros_like(places))
    return lax.cummax(boundary, axis=0)


def rotate(vectors, positions):
    half_width = vectors.shape[-1] // 2
    freq_steps = jnp.arange(half_width, dtype=jnp.float32)
    frequency = jnp.exp(freq_steps * (-2.0 * math.log(rope_base) / vectors.shape[-1]))
    angles = positions.astype(jnp.float32)[:, None] * frequency[None, :]
    cosine = jnp.cos(angles)[:, None, :]
    sine_part = jnp.sin(angles)[:, None, :]
    first_half = vectors[..., :half_width]
    second_half = vectors[..., half_width:]
    return jnp.concatenate(
        [
            first_half * cosine - second_half * sine_part,
            second_half * cosine + first_half * sine_part,
        ],
        axis=-1,
    )


def gather_levels(parts, level_bits, join_axes, sender):
    index_now = lax.axis_index(TENSOR)
    for level_bit in level_bits:
        arrived = sender(parts, level_bit)
        is_upper = index_now >> level_bit & 1 == 1
        joined_parts = []
        for own_part, peer_part, join_axis in zip(parts, arrived, join_axes):
            lower_first = jnp.concatenate([own_part, peer_part], join_axis)
            upper_first = jnp.concatenate([peer_part, own_part], join_axis)
            joined_parts.append(jnp.where(is_upper, upper_first, lower_first))
        parts = tuple(joined_parts)
    return parts


def fold_levels(partial_sum, level_bits, sender):
    index_now = lax.axis_index(TENSOR)
    for level_bit in reversed(level_bits):
        half_rows = partial_sum.shape[0] // 2
        lower_rows = partial_sum[:half_rows]
        upper_rows = partial_sum[half_rows:]
        is_upper = index_now >> level_bit & 1 == 1
        kept_rows = jnp.where(is_upper, upper_rows, lower_rows)
        sent_rows = jnp.where(is_upper, lower_rows, upper_rows)
        partial_sum = kept_rows + sender(sent_rows, level_bit)
    return partial_sum


def fold_any(partial_sum, layout_bits, level_bits):
    index_now = lax.axis_index(TENSOR)
    rows_left = partial_sum.shape[0] >> len(layout_bits)
    state = partial_sum.reshape((2,) * len(layout_bits) + (rows_left,) + partial_sum.shape[1:])
    dims = list(layout_bits)
    for level_bit in level_bits:
        place = dims.index(level_bit)
        lower_rows = lax.index_in_dim(state, 0, place, keepdims=False)
        upper_rows = lax.index_in_dim(state, 1, place, keepdims=False)
        is_upper = index_now >> level_bit & 1 == 1
        kept_rows = jnp.where(is_upper, upper_rows, lower_rows)
        sent_rows = jnp.where(is_upper, lower_rows, upper_rows)
        arrived = partner(sent_rows.astype(jnp.bfloat16), TENSOR, level_bit)
        state = kept_rows.astype(jnp.float32) + arrived.astype(jnp.float32)
        dims.pop(place)
    return state.reshape((rows_left,) + partial_sum.shape[1:])


def gather_any(part, level_bits):
    index_now = lax.axis_index(TENSOR)
    state = part
    for level_bit in level_bits:
        arrived = partner(state, TENSOR, level_bit)
        is_upper = index_now >> level_bit & 1 == 1
        lower_rows = jnp.where(is_upper, arrived, state)
        upper_rows = jnp.where(is_upper, state, arrived)
        state = jnp.stack([lower_rows, upper_rows], axis=0)
    return state


def project_pairs(row_block, w_pairs, positions):
    head_size = w_pairs.shape[1] // 2
    paired = jnp.dot(row_block, w_pairs, preferred_element_type=jnp.float32)
    rotated = rotate(paired[:, None, :head_size], positions)[:, 0]
    return jnp.concatenate([rotated, paired[:, head_size:]], axis=1).astype(jnp.bfloat16)


def expert_block(first_ref, second_ref, share_ref, gate_up_ref, down_ref, out_ref):
    half_width = second_ref.shape[1]
    rows = jnp.concatenate([first_ref[:, :half_width], second_ref[...]], axis=1)
    inner_width = down_ref.shape[1]
    total = jnp.zeros(out_ref.shape, jnp.float32)
    for expert in range(gate_up_ref.shape[0]):
        both = jnp.dot(rows, gate_up_ref[expert], preferred_element_type=jnp.float32)
        gate_val = both[:, :inner_width]
        up_val = both[:, inner_width:]
        inner_act = (jax.nn.silu(gate_val) * up_val).astype(jnp.bfloat16)
        produced = jnp.dot(inner_act, down_ref[expert], preferred_element_type=jnp.float32)
        total = total + share_ref[:, expert : expert + 1] * produced
    out_ref[...] = total.astype(out_ref.dtype)


def dense_experts(first_rows, second_rows, shares, gate_up, down_proj):
    row_count, first_width = first_rows.shape
    second_width = second_rows.shape[1]
    model_width = gate_up.shape[1]
    expert_count = gate_up.shape[0]
    tile = 256
    return pl.pallas_call(
        expert_block,
        grid=(row_count // tile,),
        in_specs=[
            pl.BlockSpec((tile, first_width), lambda i: (i, 0)),
            pl.BlockSpec((tile, second_width), lambda i: (i, 0)),
            pl.BlockSpec((tile, expert_count), lambda i: (i, 0)),
            pl.BlockSpec(gate_up.shape, lambda i: (0, 0, 0)),
            pl.BlockSpec(down_proj.shape, lambda i: (0, 0, 0)),
        ],
        out_specs=pl.BlockSpec((tile, model_width), lambda i: (i, 0)),
        out_shape=jax.ShapeDtypeStruct((row_count, model_width), jnp.bfloat16),
        compiler_params=pltpu.CompilerParams(vmem_limit_bytes=48 * 1024 * 1024),
    )(first_rows, second_rows, shares, gate_up, down_proj)


def fold_bits(partial_sum, level_bits):
    index_now = lax.axis_index(TENSOR)
    for level_bit in level_bits:
        half_rows = partial_sum.shape[0] // 2
        lower_rows = partial_sum[:half_rows]
        upper_rows = partial_sum[half_rows:]
        is_upper = index_now >> level_bit & 1 == 1
        kept_rows = jnp.where(is_upper, upper_rows, lower_rows)
        sent_rows = jnp.where(is_upper, lower_rows, upper_rows)
        arrived = partner(sent_rows.astype(jnp.bfloat16), TENSOR, level_bit)
        partial_sum = kept_rows.astype(jnp.float32) + arrived.astype(jnp.float32)
    return partial_sum

def on_device(
    hidden, segment_ids, routes, route_weights, attn_gain, w_qkv, w_out, ffn_gain, w_gate_up, w_down
):
    device_count = lax.axis_size(TENSOR)
    quarters = device_count // KVH
    index_now = lax.axis_index(TENSOR)
    quarter_index = index_now // KVH
    group_index = index_now % KVH
    group_bits = list(range(KVH.bit_length() - 1))
    quarter_bits = list(range(len(group_bits), device_count.bit_length() - 1))
    seq_len = segment_ids.shape[0]
    rows_quarter = seq_len // quarters
    model_width = hidden.shape[1]
    starts = segment_starts(segment_ids)
    expert_total = w_gate_up.shape[0] * KVH
    expert_ids = jnp.arange(expert_total, dtype=jnp.int32)
    share_table = jnp.sum(
        jnp.where(
            routes[:, None, :] == expert_ids[None, :, None],
            route_weights[:, None, :],
            jnp.zeros((), route_weights.dtype),
        ),
        axis=2,
    )
    positions = jnp.arange(seq_len, dtype=jnp.int32) - starts
    own_positions = lax.dynamic_slice_in_dim(
        positions, quarter_index * rows_quarter, rows_quarter, 0
    )
    normed = rms_norm(hidden, attn_gain)
    qkv_width = w_qkv.shape[1]
    joined = jnp.concatenate([w_qkv, w_out], axis=1)
    (gathered_cols,) = gather_levels(
        (joined,),
        quarter_bits,
        (1,),
        lambda payload, level_bit: (partner(payload[0], TENSOR, level_bit),),
    )
    by_quarter = gathered_cols.reshape(model_width, quarters, joined.shape[1])
    w_group = by_quarter[:, :, :qkv_width].reshape(model_width, quarters * qkv_width)
    w_attn_out = by_quarter[:, :, qkv_width:].reshape(model_width, GQ * HD)
    w_query = w_group[:, : GQ * HD]
    w_pairs = w_group[:, GQ * HD :]
    (own_rows,) = gather_levels(
        (normed,),
        group_bits,
        (0,),
        lambda payload, level_bit: (partner(payload[0], TENSOR, level_bit),),
    )
    kv_block = project_pairs(own_rows, w_pairs, own_positions)
    (key_values,) = gather_levels(
        (kv_block,),
        quarter_bits,
        (0,),
        lambda payload, level_bit: (partner(payload[0], TENSOR, level_bit),),
    )
    query_proj = jnp.dot(own_rows, w_query, preferred_element_type=jnp.float32).reshape(
        rows_quarter, GQ, HD
    )
    queries_heads = rotate(query_proj, own_positions).astype(jnp.bfloat16).transpose(1, 0, 2)
    block_rows = min(256, rows_quarter)
    key_block = min(512, seq_len)

    def attend(block_number):
        first_row = block_number * block_rows
        block_queries = lax.dynamic_slice_in_dim(queries_heads, first_row, block_rows, 1).reshape(
            GQ * block_rows, HD
        )
        first_place = quarter_index * rows_quarter + first_row
        query_places = first_place + jnp.arange(block_rows, dtype=jnp.int32)
        query_starts = lax.dynamic_slice_in_dim(starts, first_place, block_rows, 0)
        lowest = query_starts[0] // key_block
        highest = (first_place + block_rows - 1) // key_block + 1

        def step_keys(key_number, loop_state):
            row_peak, totals, accumulated = loop_state
            key_offset = key_number * key_block
            block_pairs = lax.dynamic_slice_in_dim(key_values, key_offset, key_block, 0)
            key_places = key_offset + jnp.arange(key_block, dtype=jnp.int32)
            allowed = (key_places[None, :] <= query_places[:, None]) & (
                key_places[None, :] >= query_starts[:, None]
            )
            scores = (
                lax.dot_general(
                    block_queries,
                    block_pairs[:, :HD],
                    (((1,), (1,)), ((), ())),
                    preferred_element_type=jnp.float32,
                )
                * attn_scale
            )
            scores = jnp.where(jnp.tile(allowed, (GQ, 1)), scores, -jnp.inf)
            new_peak = jnp.maximum(row_peak, jnp.max(scores, axis=1))
            weights = jnp.exp(scores - new_peak[:, None])
            factor = jnp.exp(row_peak - new_peak)
            totals = totals * factor + jnp.sum(weights, axis=1)
            accumulated = accumulated * factor[:, None] + jnp.dot(
                weights.astype(jnp.bfloat16),
                block_pairs[:, HD:],
                preferred_element_type=jnp.float32,
            )
            return (new_peak, totals, accumulated)

        start_state = (
            jnp.full((GQ * block_rows,), masked_floor, jnp.float32),
            jnp.zeros((GQ * block_rows,), jnp.float32),
            jnp.zeros((GQ * block_rows, HD), jnp.float32),
        )
        row_peak, totals, accumulated = lax.fori_loop(lowest, highest, step_keys, start_state)
        mixed = (accumulated / totals[:, None]).astype(jnp.bfloat16).reshape(GQ, block_rows, HD)
        return mixed.transpose(1, 0, 2).reshape(block_rows, GQ * HD)

    attended = lax.map(attend, jnp.arange(rows_quarter // block_rows, dtype=jnp.int32)).reshape(
        rows_quarter, GQ * HD
    )
    partial_proj = lax.dot_general(
        attended, w_attn_out, (((1,), (1,)), ((), ())), preferred_element_type=jnp.float32
    )
    projection = fold_any(partial_proj, group_bits[::-1], group_bits)
    after_attention = (hidden.astype(jnp.float32) + residual_scale * projection).astype(
        jnp.bfloat16
    )
    expert_in = rms_norm(after_attention, ffn_gain)
    local_experts = w_gate_up.shape[0]
    share_cols = 128 * pl.cdiv(expert_total, 128)
    half_width = model_width // 2
    carried = jnp.concatenate(
        [
            expert_in[:, :half_width],
            share_table,
            jnp.zeros((share_table.shape[0], share_cols - expert_total), jnp.bfloat16),
        ],
        axis=1,
    )
    layout = (0, 1, 3, 4, 2)
    first_order = (2, 4, 3, 1, 0)
    second_order = (4, 2, 1, 3, 0)
    first_rows = gather_any(carried, first_order)
    second_rows = gather_any(expert_in[:, half_width:], second_order)
    second_dims = list(second_order[::-1])
    second_rows = second_rows.transpose(
        [second_dims.index(bit) for bit in layout] + [len(layout), len(layout) + 1]
    )
    first_rows = first_rows.reshape(-1, first_rows.shape[-1])
    second_rows = second_rows.reshape(-1, second_rows.shape[-1])
    local_shares = lax.dynamic_slice_in_dim(
        first_rows[:, half_width : half_width + expert_total],
        group_index * local_experts,
        local_experts,
        1,
    ).astype(jnp.float32)
    expert_part = dense_experts(first_rows, second_rows, local_shares, w_gate_up, w_down)
    flat_part = expert_part
    expert_sum = jnp.concatenate(
        [
            fold_any(flat_part[:, :half_width], layout, (0, 1, 3, 4, 2)),
            fold_any(flat_part[:, half_width:], layout, (0, 3, 1, 2, 4)),
        ],
        axis=1,
    )
    hidden_out = (after_attention.astype(jnp.float32) + residual_scale * expert_sum).astype(
        jnp.bfloat16
    )
    return (after_attention, hidden_out, kv_block[None])


def solution(mesh):
    grid = mesh.devices.reshape(mesh.devices.shape[0], -1, 4, 2)
    mesh = jax.sharding.Mesh(grid, ("dp",) + TENSOR)
    placed = (
        P(("dp",) + TENSOR, None),
        P("dp"),
        P(("dp",) + TENSOR, None),
        P(("dp",) + TENSOR, None),
        P(),
        P(None, TENSOR),
        P(None, TENSOR),
        P(),
        P(TENSOR, None, None),
        P(TENSOR, None, None),
    )
    return jax.shard_map(
        on_device,
        mesh=mesh,
        in_specs=placed,
        out_specs=(P(("dp",) + TENSOR, None), P(("dp",) + TENSOR, None), P(TENSOR, "dp", None)),
        check_vma=False,
    )
```

```python
import math

import jax
import jax.numpy as jnp
from jax import lax
from jax.sharding import PartitionSpec as P
from jax.experimental import pallas as pl
from jax.experimental.pallas import tpu as pltpu

KVH = 8
HD = 64
GQ = 3
CHIPS = ("ty", "tx")
TENSOR = ("ty", "tx", "tc")


attn_scale = 0.015625
residual_scale = 0.22
rope_base = 10000.0
norm_eps = 1e-06
masked_floor = -1e30


def partner(value, axis, apart):
    mask = 2**apart
    pairs = [(source, source ^ mask) for source in range(lax.axis_size(axis))]
    return lax.ppermute(value, axis, pairs)


def rms_norm(row_block, gain_row):
    widened = row_block.astype(jnp.float32)
    mean_square = jnp.mean(widened * widened, axis=-1, keepdims=True)
    return (widened * lax.rsqrt(mean_square + norm_eps) * gain_row).astype(jnp.bfloat16)


def segment_starts(segment_ids):
    places = jnp.arange(segment_ids.shape[0], dtype=jnp.int32)
    earlier = jnp.concatenate([segment_ids[:1] - 1, segment_ids[:-1]])
    boundary = jnp.where(segment_ids != earlier, places, jnp.zeros_like(places))
    return lax.cummax(boundary, axis=0)


def rotate(vectors, positions):
    half_width = vectors.shape[-1] // 2
    freq_steps = jnp.arange(half_width, dtype=jnp.float32)
    frequency = jnp.exp(freq_steps * (-2.0 * math.log(rope_base) / vectors.shape[-1]))
    angles = positions.astype(jnp.float32)[:, None] * frequency[None, :]
    cosine = jnp.cos(angles)[:, None, :]
    sine_part = jnp.sin(angles)[:, None, :]
    first_half = vectors[..., :half_width]
    second_half = vectors[..., half_width:]
    return jnp.concatenate(
        [
            first_half * cosine - second_half * sine_part,
            second_half * cosine + first_half * sine_part,
        ],
        axis=-1,
    )


def gather_levels(parts, level_bits, join_axes, sender):
    index_now = lax.axis_index(TENSOR)
    for level_bit in level_bits:
        arrived = sender(parts, level_bit)
        is_upper = index_now >> level_bit & 1 == 1
        joined_parts = []
        for own_part, peer_part, join_axis in zip(parts, arrived, join_axes):
            lower_first = jnp.concatenate([own_part, peer_part], join_axis)
            upper_first = jnp.concatenate([peer_part, own_part], join_axis)
            joined_parts.append(jnp.where(is_upper, upper_first, lower_first))
        parts = tuple(joined_parts)
    return parts


def fold_levels(partial_sum, level_bits, sender):
    index_now = lax.axis_index(TENSOR)
    for level_bit in reversed(level_bits):
        half_rows = partial_sum.shape[0] // 2
        lower_rows = partial_sum[:half_rows]
        upper_rows = partial_sum[half_rows:]
        is_upper = index_now >> level_bit & 1 == 1
        kept_rows = jnp.where(is_upper, upper_rows, lower_rows)
        sent_rows = jnp.where(is_upper, lower_rows, upper_rows)
        partial_sum = kept_rows + sender(sent_rows, level_bit)
    return partial_sum


def fold_any(partial_sum, layout_bits, level_bits):
    index_now = lax.axis_index(TENSOR)
    rows_left = partial_sum.shape[0] >> len(layout_bits)
    state = partial_sum.reshape((2,) * len(layout_bits) + (rows_left,) + partial_sum.shape[1:])
    dims = list(layout_bits)
    for level_bit in level_bits:
        place = dims.index(level_bit)
        lower_rows = lax.index_in_dim(state, 0, place, keepdims=False)
        upper_rows = lax.index_in_dim(state, 1, place, keepdims=False)
        is_upper = index_now >> level_bit & 1 == 1
        kept_rows = jnp.where(is_upper, upper_rows, lower_rows)
        sent_rows = jnp.where(is_upper, lower_rows, upper_rows)
        arrived = partner(sent_rows.astype(jnp.bfloat16), TENSOR, level_bit)
        state = kept_rows.astype(jnp.float32) + arrived.astype(jnp.float32)
        dims.pop(place)
    return state.reshape((rows_left,) + partial_sum.shape[1:])


def gather_any(part, level_bits):
    index_now = lax.axis_index(TENSOR)
    state = part
    for level_bit in level_bits:
        arrived = partner(state, TENSOR, level_bit)
        is_upper = index_now >> level_bit & 1 == 1
        lower_rows = jnp.where(is_upper, arrived, state)
        upper_rows = jnp.where(is_upper, state, arrived)
        state = jnp.stack([lower_rows, upper_rows], axis=0)
    return state


def project_pairs(row_block, w_pairs, positions):
    head_size = w_pairs.shape[1] // 2
    paired = jnp.dot(row_block, w_pairs, preferred_element_type=jnp.float32)
    rotated = rotate(paired[:, None, :head_size], positions)[:, 0]
    return jnp.concatenate([rotated, paired[:, head_size:]], axis=1).astype(jnp.bfloat16)


def expert_block(first_ref, second_ref, share_ref, gate_up_ref, down_ref, out_ref):
    half_width = second_ref.shape[1]
    rows = jnp.concatenate([first_ref[:, :half_width], second_ref[...]], axis=1)
    inner_width = down_ref.shape[1]
    total = jnp.zeros(out_ref.shape, jnp.float32)
    for expert in range(gate_up_ref.shape[0]):
        both = jnp.dot(rows, gate_up_ref[expert], preferred_element_type=jnp.float32)
        gate_val = both[:, :inner_width]
        up_val = both[:, inner_width:]
        inner_act = (jax.nn.silu(gate_val) * up_val).astype(jnp.bfloat16)
        produced = jnp.dot(inner_act, down_ref[expert], preferred_element_type=jnp.float32)
        total = total + share_ref[:, expert : expert + 1] * produced
    out_ref[...] = total.astype(out_ref.dtype)


def dense_experts(first_rows, second_rows, shares, gate_up, down_proj):
    row_count, first_width = first_rows.shape
    second_width = second_rows.shape[1]
    model_width = gate_up.shape[1]
    expert_count = gate_up.shape[0]
    tile = 256
    return pl.pallas_call(
        expert_block,
        grid=(row_count // tile,),
        in_specs=[
            pl.BlockSpec((tile, first_width), lambda i: (i, 0)),
            pl.BlockSpec((tile, second_width), lambda i: (i, 0)),
            pl.BlockSpec((tile, expert_count), lambda i: (i, 0)),
            pl.BlockSpec(gate_up.shape, lambda i: (0, 0, 0)),
            pl.BlockSpec(down_proj.shape, lambda i: (0, 0, 0)),
        ],
        out_specs=pl.BlockSpec((tile, model_width), lambda i: (i, 0)),
        out_shape=jax.ShapeDtypeStruct((row_count, model_width), jnp.bfloat16),
        compiler_params=pltpu.CompilerParams(vmem_limit_bytes=48 * 1024 * 1024),
    )(first_rows, second_rows, shares, gate_up, down_proj)


def fold_bits(partial_sum, level_bits):
    index_now = lax.axis_index(TENSOR)
    for level_bit in level_bits:
        half_rows = partial_sum.shape[0] // 2
        lower_rows = partial_sum[:half_rows]
        upper_rows = partial_sum[half_rows:]
        is_upper = index_now >> level_bit & 1 == 1
        kept_rows = jnp.where(is_upper, upper_rows, lower_rows)
        sent_rows = jnp.where(is_upper, lower_rows, upper_rows)
        arrived = partner(sent_rows.astype(jnp.bfloat16), TENSOR, level_bit)
        partial_sum = kept_rows.astype(jnp.float32) + arrived.astype(jnp.float32)
    return partial_sum

def on_device(
    hidden, segment_ids, routes, route_weights, attn_gain, w_qkv, w_out, ffn_gain, w_gate_up, w_down
):
    device_count = lax.axis_size(TENSOR)
    quarters = device_count // KVH
    index_now = lax.axis_index(TENSOR)
    quarter_index = index_now // KVH
    group_index = index_now % KVH
    group_bits = list(range(KVH.bit_length() - 1))
    quarter_bits = list(range(len(group_bits), device_count.bit_length() - 1))
    seq_len = segment_ids.shape[0]
    rows_quarter = seq_len // quarters
    model_width = hidden.shape[1]
    starts = segment_starts(segment_ids)
    expert_total = w_gate_up.shape[0] * KVH
    expert_ids = jnp.arange(expert_total, dtype=jnp.int32)
    share_table = jnp.sum(
        jnp.where(
            routes[:, None, :] == expert_ids[None, :, None],
            route_weights[:, None, :],
            jnp.zeros((), route_weights.dtype),
        ),
        axis=2,
    )
    positions = jnp.arange(seq_len, dtype=jnp.int32) - starts
    own_positions = lax.dynamic_slice_in_dim(
        positions, quarter_index * rows_quarter, rows_quarter, 0
    )
    normed = rms_norm(hidden, attn_gain)
    qkv_width = w_qkv.shape[1]
    joined = jnp.concatenate([w_qkv, w_out], axis=1)
    (gathered_cols,) = gather_levels(
        (joined,),
        quarter_bits,
        (1,),
        lambda payload, level_bit: (partner(payload[0], TENSOR, level_bit),),
    )
    by_quarter = gathered_cols.reshape(model_width, quarters, joined.shape[1])
    w_group = by_quarter[:, :, :qkv_width].reshape(model_width, quarters * qkv_width)
    w_attn_out = by_quarter[:, :, qkv_width:].reshape(model_width, GQ * HD)
    w_query = w_group[:, : GQ * HD]
    w_pairs = w_group[:, GQ * HD :]
    (own_rows,) = gather_levels(
        (normed,),
        group_bits[::-1],
        (0,),
        lambda payload, level_bit: (partner(payload[0], TENSOR, level_bit),),
    )
    own_rows = (
        own_rows.reshape((2,) * len(group_bits) + normed.shape)
        .transpose(list(range(len(group_bits)))[::-1] + [len(group_bits), len(group_bits) + 1])
        .reshape(rows_quarter, model_width)
    )
    kv_block = project_pairs(own_rows, w_pairs, own_positions)
    (key_values,) = gather_levels(
        (kv_block,),
        quarter_bits,
        (0,),
        lambda payload, level_bit: (partner(payload[0], TENSOR, level_bit),),
    )
    query_proj = jnp.dot(own_rows, w_query, preferred_element_type=jnp.float32).reshape(
        rows_quarter, GQ, HD
    )
    queries_heads = rotate(query_proj, own_positions).astype(jnp.bfloat16).transpose(1, 0, 2)
    block_rows = min(256, rows_quarter)
    key_block = min(512, seq_len)

    def attend(block_number):
        first_row = block_number * block_rows
        block_queries = lax.dynamic_slice_in_dim(queries_heads, first_row, block_rows, 1).reshape(
            GQ * block_rows, HD
        )
        first_place = quarter_index * rows_quarter + first_row
        query_places = first_place + jnp.arange(block_rows, dtype=jnp.int32)
        query_starts = lax.dynamic_slice_in_dim(starts, first_place, block_rows, 0)
        lowest = query_starts[0] // key_block
        highest = (first_place + block_rows - 1) // key_block + 1

        def step_keys(key_number, loop_state):
            row_peak, totals, accumulated = loop_state
            key_offset = key_number * key_block
            block_pairs = lax.dynamic_slice_in_dim(key_values, key_offset, key_block, 0)
            key_places = key_offset + jnp.arange(key_block, dtype=jnp.int32)
            allowed = (key_places[None, :] <= query_places[:, None]) & (
                key_places[None, :] >= query_starts[:, None]
            )
            scores = (
                lax.dot_general(
                    block_queries,
                    block_pairs[:, :HD],
                    (((1,), (1,)), ((), ())),
                    preferred_element_type=jnp.float32,
                )
                * attn_scale
            )
            scores = jnp.where(jnp.tile(allowed, (GQ, 1)), scores, -jnp.inf)
            new_peak = jnp.maximum(row_peak, jnp.max(scores, axis=1))
            weights = jnp.exp(scores - new_peak[:, None])
            factor = jnp.exp(row_peak - new_peak)
            totals = totals * factor + jnp.sum(weights, axis=1)
            accumulated = accumulated * factor[:, None] + jnp.dot(
                weights.astype(jnp.bfloat16),
                block_pairs[:, HD:],
                preferred_element_type=jnp.float32,
            )
            return (new_peak, totals, accumulated)

        start_state = (
            jnp.full((GQ * block_rows,), masked_floor, jnp.float32),
            jnp.zeros((GQ * block_rows,), jnp.float32),
            jnp.zeros((GQ * block_rows, HD), jnp.float32),
        )
        row_peak, totals, accumulated = lax.fori_loop(lowest, highest, step_keys, start_state)
        mixed = (accumulated / totals[:, None]).astype(jnp.bfloat16).reshape(GQ, block_rows, HD)
        return mixed.transpose(1, 0, 2).reshape(block_rows, GQ * HD)

    attended = lax.map(attend, jnp.arange(rows_quarter // block_rows, dtype=jnp.int32)).reshape(
        rows_quarter, GQ * HD
    )
    partial_proj = lax.dot_general(
        attended, w_attn_out, (((1,), (1,)), ((), ())), preferred_element_type=jnp.float32
    )
    projection = fold_any(partial_proj, group_bits[::-1], group_bits)
    after_attention = (hidden.astype(jnp.float32) + residual_scale * projection).astype(
        jnp.bfloat16
    )
    expert_in = rms_norm(after_attention, ffn_gain)
    local_experts = w_gate_up.shape[0]
    share_cols = 128 * pl.cdiv(expert_total, 128)
    half_width = model_width // 2
    carried = jnp.concatenate(
        [
            expert_in[:, :half_width],
            share_table,
            jnp.zeros((share_table.shape[0], share_cols - expert_total), jnp.bfloat16),
        ],
        axis=1,
    )
    layout = (0, 1, 3, 4, 2)
    first_order = (2, 4, 3, 1, 0)
    second_order = (4, 2, 1, 3, 0)
    first_rows = gather_any(carried, first_order)
    second_rows = gather_any(expert_in[:, half_width:], second_order)
    second_dims = list(second_order[::-1])
    second_rows = second_rows.transpose(
        [second_dims.index(bit) for bit in layout] + [len(layout), len(layout) + 1]
    )
    first_rows = first_rows.reshape(-1, first_rows.shape[-1])
    second_rows = second_rows.reshape(-1, second_rows.shape[-1])
    local_shares = lax.dynamic_slice_in_dim(
        first_rows[:, half_width : half_width + expert_total],
        group_index * local_experts,
        local_experts,
        1,
    ).astype(jnp.float32)
    expert_part = dense_experts(first_rows, second_rows, local_shares, w_gate_up, w_down)
    flat_part = expert_part
    expert_sum = jnp.concatenate(
        [
            fold_any(flat_part[:, :half_width], layout, (0, 1, 3, 4, 2)),
            fold_any(flat_part[:, half_width:], layout, (0, 3, 1, 2, 4)),
        ],
        axis=1,
    )
    hidden_out = (after_attention.astype(jnp.float32) + residual_scale * expert_sum).astype(
        jnp.bfloat16
    )
    return (after_attention, hidden_out, kv_block[None])


def solution(mesh):
    grid = mesh.devices.reshape(mesh.devices.shape[0], -1, 4, 2)
    mesh = jax.sharding.Mesh(grid, ("dp",) + TENSOR)
    placed = (
        P(("dp",) + TENSOR, None),
        P("dp"),
        P(("dp",) + TENSOR, None),
        P(("dp",) + TENSOR, None),
        P(),
        P(None, TENSOR),
        P(None, TENSOR),
        P(),
        P(TENSOR, None, None),
        P(TENSOR, None, None),
    )
    return jax.shard_map(
        on_device,
        mesh=mesh,
        in_specs=placed,
        out_specs=(P(("dp",) + TENSOR, None), P(("dp",) + TENSOR, None), P(TENSOR, "dp", None)),
        check_vma=False,
    )
```

```python
import math

import jax
import jax.numpy as jnp
from jax import lax
from jax.sharding import PartitionSpec as P
from jax.experimental import pallas as pl
from jax.experimental.pallas import tpu as pltpu

KVH = 8
HD = 64
GQ = 3
CHIPS = ("ty", "tx")
TENSOR = ("ty", "tx", "tc")


attn_scale = 0.015625
residual_scale = 0.22
rope_base = 10000.0
norm_eps = 1e-06
masked_floor = -1e30


def partner(value, axis, apart):
    mask = 2**apart
    pairs = [(source, source ^ mask) for source in range(lax.axis_size(axis))]
    return lax.ppermute(value, axis, pairs)


def rms_norm(row_block, gain_row):
    widened = row_block.astype(jnp.float32)
    mean_square = jnp.mean(widened * widened, axis=-1, keepdims=True)
    return (widened * lax.rsqrt(mean_square + norm_eps) * gain_row).astype(jnp.bfloat16)


def segment_starts(segment_ids):
    places = jnp.arange(segment_ids.shape[0], dtype=jnp.int32)
    earlier = jnp.concatenate([segment_ids[:1] - 1, segment_ids[:-1]])
    boundary = jnp.where(segment_ids != earlier, places, jnp.zeros_like(places))
    return lax.cummax(boundary, axis=0)


def rotate(vectors, positions):
    half_width = vectors.shape[-1] // 2
    freq_steps = jnp.arange(half_width, dtype=jnp.float32)
    frequency = jnp.exp(freq_steps * (-2.0 * math.log(rope_base) / vectors.shape[-1]))
    angles = positions.astype(jnp.float32)[:, None] * frequency[None, :]
    cosine = jnp.cos(angles)[:, None, :]
    sine_part = jnp.sin(angles)[:, None, :]
    first_half = vectors[..., :half_width]
    second_half = vectors[..., half_width:]
    return jnp.concatenate(
        [
            first_half * cosine - second_half * sine_part,
            second_half * cosine + first_half * sine_part,
        ],
        axis=-1,
    )


def gather_levels(parts, level_bits, join_axes, sender):
    index_now = lax.axis_index(TENSOR)
    for level_bit in level_bits:
        arrived = sender(parts, level_bit)
        is_upper = index_now >> level_bit & 1 == 1
        joined_parts = []
        for own_part, peer_part, join_axis in zip(parts, arrived, join_axes):
            lower_first = jnp.concatenate([own_part, peer_part], join_axis)
            upper_first = jnp.concatenate([peer_part, own_part], join_axis)
            joined_parts.append(jnp.where(is_upper, upper_first, lower_first))
        parts = tuple(joined_parts)
    return parts


def fold_levels(partial_sum, level_bits, sender):
    index_now = lax.axis_index(TENSOR)
    for level_bit in reversed(level_bits):
        half_rows = partial_sum.shape[0] // 2
        lower_rows = partial_sum[:half_rows]
        upper_rows = partial_sum[half_rows:]
        is_upper = index_now >> level_bit & 1 == 1
        kept_rows = jnp.where(is_upper, upper_rows, lower_rows)
        sent_rows = jnp.where(is_upper, lower_rows, upper_rows)
        partial_sum = kept_rows + sender(sent_rows, level_bit)
    return partial_sum


def fold_any(partial_sum, layout_bits, level_bits):
    index_now = lax.axis_index(TENSOR)
    rows_left = partial_sum.shape[0] >> len(layout_bits)
    state = partial_sum.reshape((2,) * len(layout_bits) + (rows_left,) + partial_sum.shape[1:])
    dims = list(layout_bits)
    for level_bit in level_bits:
        place = dims.index(level_bit)
        lower_rows = lax.index_in_dim(state, 0, place, keepdims=False)
        upper_rows = lax.index_in_dim(state, 1, place, keepdims=False)
        is_upper = index_now >> level_bit & 1 == 1
        kept_rows = jnp.where(is_upper, upper_rows, lower_rows)
        sent_rows = jnp.where(is_upper, lower_rows, upper_rows)
        arrived = partner(sent_rows.astype(jnp.bfloat16), TENSOR, level_bit)
        state = kept_rows.astype(jnp.float32) + arrived.astype(jnp.float32)
        dims.pop(place)
    return state.reshape((rows_left,) + partial_sum.shape[1:])


def gather_any(part, level_bits):
    index_now = lax.axis_index(TENSOR)
    state = part
    for level_bit in level_bits:
        arrived = partner(state, TENSOR, level_bit)
        is_upper = index_now >> level_bit & 1 == 1
        lower_rows = jnp.where(is_upper, arrived, state)
        upper_rows = jnp.where(is_upper, state, arrived)
        state = jnp.stack([lower_rows, upper_rows], axis=0)
    return state


def project_pairs(row_block, w_pairs, positions):
    head_size = w_pairs.shape[1] // 2
    paired = jnp.dot(row_block, w_pairs, preferred_element_type=jnp.float32)
    rotated = rotate(paired[:, None, :head_size], positions)[:, 0]
    return jnp.concatenate([rotated, paired[:, head_size:]], axis=1).astype(jnp.bfloat16)


def expert_block(first_ref, second_ref, share_ref, gate_up_ref, down_ref, out_ref):
    half_width = second_ref.shape[1]
    rows = jnp.concatenate([first_ref[:, :half_width], second_ref[...]], axis=1)
    inner_width = down_ref.shape[1]
    total = jnp.zeros(out_ref.shape, jnp.float32)
    for expert in range(gate_up_ref.shape[0]):
        both = jnp.dot(rows, gate_up_ref[expert], preferred_element_type=jnp.float32)
        gate_val = both[:, :inner_width]
        up_val = both[:, inner_width:]
        inner_act = (jax.nn.silu(gate_val) * up_val).astype(jnp.bfloat16)
        produced = jnp.dot(inner_act, down_ref[expert], preferred_element_type=jnp.float32)
        total = total + share_ref[:, expert : expert + 1] * produced
    out_ref[...] = total.astype(out_ref.dtype)


def dense_experts(first_rows, second_rows, shares, gate_up, down_proj):
    row_count, first_width = first_rows.shape
    second_width = second_rows.shape[1]
    model_width = gate_up.shape[1]
    expert_count = gate_up.shape[0]
    tile = 256
    return pl.pallas_call(
        expert_block,
        grid=(row_count // tile,),
        in_specs=[
            pl.BlockSpec((tile, first_width), lambda i: (i, 0)),
            pl.BlockSpec((tile, second_width), lambda i: (i, 0)),
            pl.BlockSpec((tile, expert_count), lambda i: (i, 0)),
            pl.BlockSpec(gate_up.shape, lambda i: (0, 0, 0)),
            pl.BlockSpec(down_proj.shape, lambda i: (0, 0, 0)),
        ],
        out_specs=pl.BlockSpec((tile, model_width), lambda i: (i, 0)),
        out_shape=jax.ShapeDtypeStruct((row_count, model_width), jnp.bfloat16),
        compiler_params=pltpu.CompilerParams(vmem_limit_bytes=48 * 1024 * 1024),
    )(first_rows, second_rows, shares, gate_up, down_proj)


def fold_bits(partial_sum, level_bits):
    index_now = lax.axis_index(TENSOR)
    for level_bit in level_bits:
        half_rows = partial_sum.shape[0] // 2
        lower_rows = partial_sum[:half_rows]
        upper_rows = partial_sum[half_rows:]
        is_upper = index_now >> level_bit & 1 == 1
        kept_rows = jnp.where(is_upper, upper_rows, lower_rows)
        sent_rows = jnp.where(is_upper, lower_rows, upper_rows)
        arrived = partner(sent_rows.astype(jnp.bfloat16), TENSOR, level_bit)
        partial_sum = kept_rows.astype(jnp.float32) + arrived.astype(jnp.float32)
    return partial_sum

def on_device(
    hidden, segment_ids, routes, route_weights, attn_gain, w_qkv, w_out, ffn_gain, w_gate_up, w_down
):
    device_count = lax.axis_size(TENSOR)
    quarters = device_count // KVH
    index_now = lax.axis_index(TENSOR)
    quarter_index = index_now // KVH
    group_index = index_now % KVH
    group_bits = list(range(KVH.bit_length() - 1))
    quarter_bits = list(range(len(group_bits), device_count.bit_length() - 1))
    seq_len = segment_ids.shape[0]
    rows_quarter = seq_len // quarters
    model_width = hidden.shape[1]
    starts = segment_starts(segment_ids)
    expert_total = w_gate_up.shape[0] * KVH
    expert_ids = jnp.arange(expert_total, dtype=jnp.int32)
    share_table = jnp.sum(
        jnp.where(
            routes[:, None, :] == expert_ids[None, :, None],
            route_weights[:, None, :],
            jnp.zeros((), route_weights.dtype),
        ),
        axis=2,
    )
    positions = jnp.arange(seq_len, dtype=jnp.int32) - starts
    own_positions = lax.dynamic_slice_in_dim(
        positions, quarter_index * rows_quarter, rows_quarter, 0
    )
    normed = rms_norm(hidden, attn_gain)
    qkv_width = w_qkv.shape[1]
    (w_group,) = gather_levels(
        (w_qkv,),
        quarter_bits,
        (1,),
        lambda payload, level_bit: (partner(payload[0], TENSOR, level_bit),),
    )
    (w_attn_out,) = gather_levels(
        (w_out,),
        quarter_bits,
        (1,),
        lambda payload, level_bit: (partner(payload[0], TENSOR, level_bit),),
    )
    w_query = w_group[:, : GQ * HD]
    w_pairs = w_group[:, GQ * HD :]
    (own_rows,) = gather_levels(
        (normed,),
        group_bits[::-1],
        (0,),
        lambda payload, level_bit: (partner(payload[0], TENSOR, level_bit),),
    )
    own_rows = (
        own_rows.reshape((2,) * len(group_bits) + normed.shape)
        .transpose(list(range(len(group_bits)))[::-1] + [len(group_bits), len(group_bits) + 1])
        .reshape(rows_quarter, model_width)
    )
    kv_block = project_pairs(own_rows, w_pairs, own_positions)
    (key_values,) = gather_levels(
        (kv_block,),
        quarter_bits,
        (0,),
        lambda payload, level_bit: (partner(payload[0], TENSOR, level_bit),),
    )
    query_proj = jnp.dot(own_rows, w_query, preferred_element_type=jnp.float32).reshape(
        rows_quarter, GQ, HD
    )
    queries_heads = rotate(query_proj, own_positions).astype(jnp.bfloat16).transpose(1, 0, 2)
    block_rows = min(256, rows_quarter)
    key_block = min(512, seq_len)

    def attend(block_number):
        first_row = block_number * block_rows
        block_queries = lax.dynamic_slice_in_dim(queries_heads, first_row, block_rows, 1).reshape(
            GQ * block_rows, HD
        )
        first_place = quarter_index * rows_quarter + first_row
        query_places = first_place + jnp.arange(block_rows, dtype=jnp.int32)
        query_starts = lax.dynamic_slice_in_dim(starts, first_place, block_rows, 0)
        lowest = query_starts[0] // key_block
        highest = (first_place + block_rows - 1) // key_block + 1

        def step_keys(key_number, loop_state):
            row_peak, totals, accumulated = loop_state
            key_offset = key_number * key_block
            block_pairs = lax.dynamic_slice_in_dim(key_values, key_offset, key_block, 0)
            key_places = key_offset + jnp.arange(key_block, dtype=jnp.int32)
            allowed = (key_places[None, :] <= query_places[:, None]) & (
                key_places[None, :] >= query_starts[:, None]
            )
            scores = (
                lax.dot_general(
                    block_queries,
                    block_pairs[:, :HD],
                    (((1,), (1,)), ((), ())),
                    preferred_element_type=jnp.float32,
                )
                * attn_scale
            )
            scores = jnp.where(jnp.tile(allowed, (GQ, 1)), scores, -jnp.inf)
            new_peak = jnp.maximum(row_peak, jnp.max(scores, axis=1))
            weights = jnp.exp(scores - new_peak[:, None])
            factor = jnp.exp(row_peak - new_peak)
            totals = totals * factor + jnp.sum(weights, axis=1)
            accumulated = accumulated * factor[:, None] + jnp.dot(
                weights.astype(jnp.bfloat16),
                block_pairs[:, HD:],
                preferred_element_type=jnp.float32,
            )
            return (new_peak, totals, accumulated)

        start_state = (
            jnp.full((GQ * block_rows,), masked_floor, jnp.float32),
            jnp.zeros((GQ * block_rows,), jnp.float32),
            jnp.zeros((GQ * block_rows, HD), jnp.float32),
        )
        row_peak, totals, accumulated = lax.fori_loop(lowest, highest, step_keys, start_state)
        mixed = (accumulated / totals[:, None]).astype(jnp.bfloat16).reshape(GQ, block_rows, HD)
        return mixed.transpose(1, 0, 2).reshape(block_rows, GQ * HD)

    attended = lax.map(attend, jnp.arange(rows_quarter // block_rows, dtype=jnp.int32)).reshape(
        rows_quarter, GQ * HD
    )
    partial_proj = lax.dot_general(
        attended, w_attn_out, (((1,), (1,)), ((), ())), preferred_element_type=jnp.float32
    )
    projection = fold_any(partial_proj, group_bits[::-1], group_bits)
    after_attention = (hidden.astype(jnp.float32) + residual_scale * projection).astype(
        jnp.bfloat16
    )
    expert_in = rms_norm(after_attention, ffn_gain)
    local_experts = w_gate_up.shape[0]
    share_cols = 128 * pl.cdiv(expert_total, 128)
    half_width = model_width // 2
    carried = jnp.concatenate(
        [
            expert_in[:, :half_width],
            share_table,
            jnp.zeros((share_table.shape[0], share_cols - expert_total), jnp.bfloat16),
        ],
        axis=1,
    )
    layout = (0, 1, 3, 4, 2)
    first_order = (2, 4, 3, 1, 0)
    second_order = (4, 2, 1, 3, 0)
    first_rows = gather_any(carried, first_order)
    second_rows = gather_any(expert_in[:, half_width:], second_order)
    second_dims = list(second_order[::-1])
    second_rows = second_rows.transpose(
        [second_dims.index(bit) for bit in layout] + [len(layout), len(layout) + 1]
    )
    first_rows = first_rows.reshape(-1, first_rows.shape[-1])
    second_rows = second_rows.reshape(-1, second_rows.shape[-1])
    local_shares = lax.dynamic_slice_in_dim(
        first_rows[:, half_width : half_width + expert_total],
        group_index * local_experts,
        local_experts,
        1,
    ).astype(jnp.float32)
    expert_part = dense_experts(first_rows, second_rows, local_shares, w_gate_up, w_down)
    flat_part = expert_part
    expert_sum = jnp.concatenate(
        [
            fold_any(flat_part[:, :half_width], layout, (0, 1, 3, 4, 2)),
            fold_any(flat_part[:, half_width:], layout, (0, 3, 1, 2, 4)),
        ],
        axis=1,
    )
    hidden_out = (after_attention.astype(jnp.float32) + residual_scale * expert_sum).astype(
        jnp.bfloat16
    )
    return (after_attention, hidden_out, kv_block[None])


def solution(mesh):
    grid = mesh.devices.reshape(mesh.devices.shape[0], -1, 4, 2)
    mesh = jax.sharding.Mesh(grid, ("dp",) + TENSOR)
    placed = (
        P(("dp",) + TENSOR, None),
        P("dp"),
        P(("dp",) + TENSOR, None),
        P(("dp",) + TENSOR, None),
        P(),
        P(None, TENSOR),
        P(None, TENSOR),
        P(),
        P(TENSOR, None, None),
        P(TENSOR, None, None),
    )
    return jax.shard_map(
        on_device,
        mesh=mesh,
        in_specs=placed,
        out_specs=(P(("dp",) + TENSOR, None), P(("dp",) + TENSOR, None), P(TENSOR, "dp", None)),
        check_vma=False,
    )
```

```python
import math

import jax
import jax.numpy as jnp
from jax import lax
from jax.sharding import PartitionSpec as P
from jax.experimental import pallas as pl
from jax.experimental.pallas import tpu as pltpu

KVH = 8
HD = 64
GQ = 3
CHIPS = ("ty", "tx")
TENSOR = ("ty", "tx", "tc")


attn_scale = 0.015625
residual_scale = 0.22
rope_base = 10000.0
norm_eps = 1e-06
masked_floor = -1e30


def partner(value, axis, apart):
    mask = 2**apart
    pairs = [(source, source ^ mask) for source in range(lax.axis_size(axis))]
    return lax.ppermute(value, axis, pairs)


def rms_norm(row_block, gain_row):
    widened = row_block.astype(jnp.float32)
    mean_square = jnp.mean(widened * widened, axis=-1, keepdims=True)
    return (widened * lax.rsqrt(mean_square + norm_eps) * gain_row).astype(jnp.bfloat16)


def segment_starts(segment_ids):
    places = jnp.arange(segment_ids.shape[0], dtype=jnp.int32)
    earlier = jnp.concatenate([segment_ids[:1] - 1, segment_ids[:-1]])
    boundary = jnp.where(segment_ids != earlier, places, jnp.zeros_like(places))
    return lax.cummax(boundary, axis=0)


def rotate(vectors, positions):
    half_width = vectors.shape[-1] // 2
    freq_steps = jnp.arange(half_width, dtype=jnp.float32)
    frequency = jnp.exp(freq_steps * (-2.0 * math.log(rope_base) / vectors.shape[-1]))
    angles = positions.astype(jnp.float32)[:, None] * frequency[None, :]
    cosine = jnp.cos(angles)[:, None, :]
    sine_part = jnp.sin(angles)[:, None, :]
    first_half = vectors[..., :half_width]
    second_half = vectors[..., half_width:]
    return jnp.concatenate(
        [
            first_half * cosine - second_half * sine_part,
            second_half * cosine + first_half * sine_part,
        ],
        axis=-1,
    )


def gather_levels(parts, level_bits, join_axes, sender):
    index_now = lax.axis_index(TENSOR)
    for level_bit in level_bits:
        arrived = sender(parts, level_bit)
        is_upper = index_now >> level_bit & 1 == 1
        joined_parts = []
        for own_part, peer_part, join_axis in zip(parts, arrived, join_axes):
            lower_first = jnp.concatenate([own_part, peer_part], join_axis)
            upper_first = jnp.concatenate([peer_part, own_part], join_axis)
            joined_parts.append(jnp.where(is_upper, upper_first, lower_first))
        parts = tuple(joined_parts)
    return parts


def fold_levels(partial_sum, level_bits, sender):
    index_now = lax.axis_index(TENSOR)
    for level_bit in reversed(level_bits):
        half_rows = partial_sum.shape[0] // 2
        lower_rows = partial_sum[:half_rows]
        upper_rows = partial_sum[half_rows:]
        is_upper = index_now >> level_bit & 1 == 1
        kept_rows = jnp.where(is_upper, upper_rows, lower_rows)
        sent_rows = jnp.where(is_upper, lower_rows, upper_rows)
        partial_sum = kept_rows + sender(sent_rows, level_bit)
    return partial_sum


def fold_any(partial_sum, layout_bits, level_bits):
    index_now = lax.axis_index(TENSOR)
    rows_left = partial_sum.shape[0] >> len(layout_bits)
    state = partial_sum.reshape((2,) * len(layout_bits) + (rows_left,) + partial_sum.shape[1:])
    dims = list(layout_bits)
    for level_bit in level_bits:
        place = dims.index(level_bit)
        lower_rows = lax.index_in_dim(state, 0, place, keepdims=False)
        upper_rows = lax.index_in_dim(state, 1, place, keepdims=False)
        is_upper = index_now >> level_bit & 1 == 1
        kept_rows = jnp.where(is_upper, upper_rows, lower_rows)
        sent_rows = jnp.where(is_upper, lower_rows, upper_rows)
        arrived = partner(sent_rows.astype(jnp.bfloat16), TENSOR, level_bit)
        state = kept_rows.astype(jnp.float32) + arrived.astype(jnp.float32)
        dims.pop(place)
    return state.reshape((rows_left,) + partial_sum.shape[1:])


def gather_any(part, level_bits):
    index_now = lax.axis_index(TENSOR)
    state = part
    for level_bit in level_bits:
        arrived = partner(state, TENSOR, level_bit)
        is_upper = index_now >> level_bit & 1 == 1
        lower_rows = jnp.where(is_upper, arrived, state)
        upper_rows = jnp.where(is_upper, state, arrived)
        state = jnp.stack([lower_rows, upper_rows], axis=0)
    return state


def project_pairs(row_block, w_pairs, positions):
    head_size = w_pairs.shape[1] // 2
    paired = jnp.dot(row_block, w_pairs, preferred_element_type=jnp.float32)
    rotated = rotate(paired[:, None, :head_size], positions)[:, 0]
    return jnp.concatenate([rotated, paired[:, head_size:]], axis=1).astype(jnp.bfloat16)


def expert_block(first_ref, second_ref, share_ref, gate_up_ref, down_ref, out_ref):
    half_width = second_ref.shape[1]
    rows = jnp.concatenate([first_ref[:, :half_width], second_ref[...]], axis=1)
    inner_width = down_ref.shape[1]
    total = jnp.zeros(out_ref.shape, jnp.float32)
    for expert in range(gate_up_ref.shape[0]):
        both = jnp.dot(rows, gate_up_ref[expert], preferred_element_type=jnp.float32)
        gate_val = both[:, :inner_width]
        up_val = both[:, inner_width:]
        inner_act = (jax.nn.silu(gate_val) * up_val).astype(jnp.bfloat16)
        produced = jnp.dot(inner_act, down_ref[expert], preferred_element_type=jnp.float32)
        total = total + share_ref[:, expert : expert + 1] * produced
    out_ref[...] = total.astype(out_ref.dtype)


def dense_experts(first_rows, second_rows, shares, gate_up, down_proj):
    row_count, first_width = first_rows.shape
    second_width = second_rows.shape[1]
    model_width = gate_up.shape[1]
    expert_count = gate_up.shape[0]
    tile = 512
    return pl.pallas_call(
        expert_block,
        grid=(row_count // tile,),
        in_specs=[
            pl.BlockSpec((tile, first_width), lambda i: (i, 0)),
            pl.BlockSpec((tile, second_width), lambda i: (i, 0)),
            pl.BlockSpec((tile, expert_count), lambda i: (i, 0)),
            pl.BlockSpec(gate_up.shape, lambda i: (0, 0, 0)),
            pl.BlockSpec(down_proj.shape, lambda i: (0, 0, 0)),
        ],
        out_specs=pl.BlockSpec((tile, model_width), lambda i: (i, 0)),
        out_shape=jax.ShapeDtypeStruct((row_count, model_width), jnp.bfloat16),
        compiler_params=pltpu.CompilerParams(vmem_limit_bytes=48 * 1024 * 1024),
    )(first_rows, second_rows, shares, gate_up, down_proj)


def fold_bits(partial_sum, level_bits):
    index_now = lax.axis_index(TENSOR)
    for level_bit in level_bits:
        half_rows = partial_sum.shape[0] // 2
        lower_rows = partial_sum[:half_rows]
        upper_rows = partial_sum[half_rows:]
        is_upper = index_now >> level_bit & 1 == 1
        kept_rows = jnp.where(is_upper, upper_rows, lower_rows)
        sent_rows = jnp.where(is_upper, lower_rows, upper_rows)
        arrived = partner(sent_rows.astype(jnp.bfloat16), TENSOR, level_bit)
        partial_sum = kept_rows.astype(jnp.float32) + arrived.astype(jnp.float32)
    return partial_sum

def on_device(
    hidden, segment_ids, routes, route_weights, attn_gain, w_qkv, w_out, ffn_gain, w_gate_up, w_down
):
    device_count = lax.axis_size(TENSOR)
    quarters = device_count // KVH
    index_now = lax.axis_index(TENSOR)
    quarter_index = index_now // KVH
    group_index = index_now % KVH
    group_bits = list(range(KVH.bit_length() - 1))
    quarter_bits = list(range(len(group_bits), device_count.bit_length() - 1))
    seq_len = segment_ids.shape[0]
    rows_quarter = seq_len // quarters
    model_width = hidden.shape[1]
    starts = segment_starts(segment_ids)
    expert_total = w_gate_up.shape[0] * KVH
    expert_ids = jnp.arange(expert_total, dtype=jnp.int32)
    share_table = jnp.sum(
        jnp.where(
            routes[:, None, :] == expert_ids[None, :, None],
            route_weights[:, None, :],
            jnp.zeros((), route_weights.dtype),
        ),
        axis=2,
    )
    positions = jnp.arange(seq_len, dtype=jnp.int32) - starts
    own_positions = lax.dynamic_slice_in_dim(
        positions, quarter_index * rows_quarter, rows_quarter, 0
    )
    normed = rms_norm(hidden, attn_gain)
    qkv_width = w_qkv.shape[1]
    (w_group,) = gather_levels(
        (w_qkv,),
        quarter_bits,
        (1,),
        lambda payload, level_bit: (partner(payload[0], TENSOR, level_bit),),
    )
    (w_attn_out,) = gather_levels(
        (w_out,),
        quarter_bits,
        (1,),
        lambda payload, level_bit: (partner(payload[0], TENSOR, level_bit),),
    )
    w_query = w_group[:, : GQ * HD]
    w_pairs = w_group[:, GQ * HD :]
    (own_rows,) = gather_levels(
        (normed,),
        group_bits[::-1],
        (0,),
        lambda payload, level_bit: (partner(payload[0], TENSOR, level_bit),),
    )
    own_rows = (
        own_rows.reshape((2,) * len(group_bits) + normed.shape)
        .transpose(list(range(len(group_bits)))[::-1] + [len(group_bits), len(group_bits) + 1])
        .reshape(rows_quarter, model_width)
    )
    kv_block = project_pairs(own_rows, w_pairs, own_positions)
    (key_values,) = gather_levels(
        (kv_block,),
        quarter_bits,
        (0,),
        lambda payload, level_bit: (partner(payload[0], TENSOR, level_bit),),
    )
    query_proj = jnp.dot(own_rows, w_query, preferred_element_type=jnp.float32).reshape(
        rows_quarter, GQ, HD
    )
    queries_heads = rotate(query_proj, own_positions).astype(jnp.bfloat16).transpose(1, 0, 2)
    block_rows = min(256, rows_quarter)
    key_block = min(512, seq_len)

    def attend(block_number):
        first_row = block_number * block_rows
        block_queries = lax.dynamic_slice_in_dim(queries_heads, first_row, block_rows, 1).reshape(
            GQ * block_rows, HD
        )
        first_place = quarter_index * rows_quarter + first_row
        query_places = first_place + jnp.arange(block_rows, dtype=jnp.int32)
        query_starts = lax.dynamic_slice_in_dim(starts, first_place, block_rows, 0)
        lowest = query_starts[0] // key_block
        highest = (first_place + block_rows - 1) // key_block + 1

        def step_keys(key_number, loop_state):
            row_peak, totals, accumulated = loop_state
            key_offset = key_number * key_block
            block_pairs = lax.dynamic_slice_in_dim(key_values, key_offset, key_block, 0)
            key_places = key_offset + jnp.arange(key_block, dtype=jnp.int32)
            allowed = (key_places[None, :] <= query_places[:, None]) & (
                key_places[None, :] >= query_starts[:, None]
            )
            scores = (
                lax.dot_general(
                    block_queries,
                    block_pairs[:, :HD],
                    (((1,), (1,)), ((), ())),
                    preferred_element_type=jnp.float32,
                )
                * attn_scale
            )
            scores = jnp.where(jnp.tile(allowed, (GQ, 1)), scores, -jnp.inf)
            new_peak = jnp.maximum(row_peak, jnp.max(scores, axis=1))
            weights = jnp.exp(scores - new_peak[:, None])
            factor = jnp.exp(row_peak - new_peak)
            totals = totals * factor + jnp.sum(weights, axis=1)
            accumulated = accumulated * factor[:, None] + jnp.dot(
                weights.astype(jnp.bfloat16),
                block_pairs[:, HD:],
                preferred_element_type=jnp.float32,
            )
            return (new_peak, totals, accumulated)

        start_state = (
            jnp.full((GQ * block_rows,), masked_floor, jnp.float32),
            jnp.zeros((GQ * block_rows,), jnp.float32),
            jnp.zeros((GQ * block_rows, HD), jnp.float32),
        )
        row_peak, totals, accumulated = lax.fori_loop(lowest, highest, step_keys, start_state)
        mixed = (accumulated / totals[:, None]).astype(jnp.bfloat16).reshape(GQ, block_rows, HD)
        return mixed.transpose(1, 0, 2).reshape(block_rows, GQ * HD)

    attended = lax.map(attend, jnp.arange(rows_quarter // block_rows, dtype=jnp.int32)).reshape(
        rows_quarter, GQ * HD
    )
    partial_proj = lax.dot_general(
        attended, w_attn_out, (((1,), (1,)), ((), ())), preferred_element_type=jnp.float32
    )
    projection = fold_any(partial_proj, group_bits[::-1], group_bits)
    after_attention = (hidden.astype(jnp.float32) + residual_scale * projection).astype(
        jnp.bfloat16
    )
    expert_in = rms_norm(after_attention, ffn_gain)
    local_experts = w_gate_up.shape[0]
    share_cols = 128 * pl.cdiv(expert_total, 128)
    half_width = model_width // 2
    carried = jnp.concatenate(
        [
            expert_in[:, :half_width],
            share_table,
            jnp.zeros((share_table.shape[0], share_cols - expert_total), jnp.bfloat16),
        ],
        axis=1,
    )
    layout = (0, 1, 3, 4, 2)
    first_order = (2, 4, 3, 1, 0)
    second_order = (4, 2, 1, 3, 0)
    first_rows = gather_any(carried, first_order)
    second_rows = gather_any(expert_in[:, half_width:], second_order)
    second_dims = list(second_order[::-1])
    second_rows = second_rows.transpose(
        [second_dims.index(bit) for bit in layout] + [len(layout), len(layout) + 1]
    )
    first_rows = first_rows.reshape(-1, first_rows.shape[-1])
    second_rows = second_rows.reshape(-1, second_rows.shape[-1])
    local_shares = lax.dynamic_slice_in_dim(
        first_rows[:, half_width : half_width + expert_total],
        group_index * local_experts,
        local_experts,
        1,
    ).astype(jnp.float32)
    expert_part = dense_experts(first_rows, second_rows, local_shares, w_gate_up, w_down)
    flat_part = expert_part
    expert_sum = jnp.concatenate(
        [
            fold_any(flat_part[:, :half_width], layout, (0, 1, 3, 4, 2)),
            fold_any(flat_part[:, half_width:], layout, (0, 3, 1, 2, 4)),
        ],
        axis=1,
    )
    hidden_out = (after_attention.astype(jnp.float32) + residual_scale * expert_sum).astype(
        jnp.bfloat16
    )
    return (after_attention, hidden_out, kv_block[None])


def solution(mesh):
    grid = mesh.devices.reshape(mesh.devices.shape[0], -1, 4, 2)
    mesh = jax.sharding.Mesh(grid, ("dp",) + TENSOR)
    placed = (
        P(("dp",) + TENSOR, None),
        P("dp"),
        P(("dp",) + TENSOR, None),
        P(("dp",) + TENSOR, None),
        P(),
        P(None, TENSOR),
        P(None, TENSOR),
        P(),
        P(TENSOR, None, None),
        P(TENSOR, None, None),
    )
    return jax.shard_map(
        on_device,
        mesh=mesh,
        in_specs=placed,
        out_specs=(P(("dp",) + TENSOR, None), P(("dp",) + TENSOR, None), P(TENSOR, "dp", None)),
        check_vma=False,
    )
```

```python
import math

import jax
import jax.numpy as jnp
from jax import lax
from jax.sharding import PartitionSpec as P
from jax.experimental import pallas as pl
from jax.experimental.pallas import tpu as pltpu

KVH = 8
HD = 64
GQ = 3
CHIPS = ("ty", "tx")
TENSOR = ("ty", "tx", "tc")


attn_scale = 0.015625
residual_scale = 0.22
rope_base = 10000.0
norm_eps = 1e-06
masked_floor = -1e30


def partner(value, axis, apart):
    mask = 2**apart
    pairs = [(source, source ^ mask) for source in range(lax.axis_size(axis))]
    return lax.ppermute(value, axis, pairs)


def rms_norm(row_block, gain_row):
    widened = row_block.astype(jnp.float32)
    mean_square = jnp.mean(widened * widened, axis=-1, keepdims=True)
    return (widened * lax.rsqrt(mean_square + norm_eps) * gain_row).astype(jnp.bfloat16)


def segment_starts(segment_ids):
    places = jnp.arange(segment_ids.shape[0], dtype=jnp.int32)
    earlier = jnp.concatenate([segment_ids[:1] - 1, segment_ids[:-1]])
    boundary = jnp.where(segment_ids != earlier, places, jnp.zeros_like(places))
    return lax.cummax(boundary, axis=0)


def rotate(vectors, positions):
    half_width = vectors.shape[-1] // 2
    freq_steps = jnp.arange(half_width, dtype=jnp.float32)
    frequency = jnp.exp(freq_steps * (-2.0 * math.log(rope_base) / vectors.shape[-1]))
    angles = positions.astype(jnp.float32)[:, None] * frequency[None, :]
    cosine = jnp.cos(angles)[:, None, :]
    sine_part = jnp.sin(angles)[:, None, :]
    first_half = vectors[..., :half_width]
    second_half = vectors[..., half_width:]
    return jnp.concatenate(
        [
            first_half * cosine - second_half * sine_part,
            second_half * cosine + first_half * sine_part,
        ],
        axis=-1,
    )


def gather_levels(parts, level_bits, join_axes, sender):
    index_now = lax.axis_index(TENSOR)
    for level_bit in level_bits:
        arrived = sender(parts, level_bit)
        is_upper = index_now >> level_bit & 1 == 1
        joined_parts = []
        for own_part, peer_part, join_axis in zip(parts, arrived, join_axes):
            lower_first = jnp.concatenate([own_part, peer_part], join_axis)
            upper_first = jnp.concatenate([peer_part, own_part], join_axis)
            joined_parts.append(jnp.where(is_upper, upper_first, lower_first))
        parts = tuple(joined_parts)
    return parts


def fold_levels(partial_sum, level_bits, sender):
    index_now = lax.axis_index(TENSOR)
    for level_bit in reversed(level_bits):
        half_rows = partial_sum.shape[0] // 2
        lower_rows = partial_sum[:half_rows]
        upper_rows = partial_sum[half_rows:]
        is_upper = index_now >> level_bit & 1 == 1
        kept_rows = jnp.where(is_upper, upper_rows, lower_rows)
        sent_rows = jnp.where(is_upper, lower_rows, upper_rows)
        partial_sum = kept_rows + sender(sent_rows, level_bit)
    return partial_sum


def fold_any(partial_sum, layout_bits, level_bits):
    index_now = lax.axis_index(TENSOR)
    rows_left = partial_sum.shape[0] >> len(layout_bits)
    state = partial_sum.reshape((2,) * len(layout_bits) + (rows_left,) + partial_sum.shape[1:])
    dims = list(layout_bits)
    for level_bit in level_bits:
        place = dims.index(level_bit)
        lower_rows = lax.index_in_dim(state, 0, place, keepdims=False)
        upper_rows = lax.index_in_dim(state, 1, place, keepdims=False)
        is_upper = index_now >> level_bit & 1 == 1
        kept_rows = jnp.where(is_upper, upper_rows, lower_rows)
        sent_rows = jnp.where(is_upper, lower_rows, upper_rows)
        arrived = partner(sent_rows.astype(jnp.bfloat16), TENSOR, level_bit)
        state = kept_rows.astype(jnp.float32) + arrived.astype(jnp.float32)
        dims.pop(place)
    return state.reshape((rows_left,) + partial_sum.shape[1:])


def gather_any(part, level_bits):
    index_now = lax.axis_index(TENSOR)
    state = part
    for level_bit in level_bits:
        arrived = partner(state, TENSOR, level_bit)
        is_upper = index_now >> level_bit & 1 == 1
        lower_rows = jnp.where(is_upper, arrived, state)
        upper_rows = jnp.where(is_upper, state, arrived)
        state = jnp.stack([lower_rows, upper_rows], axis=0)
    return state


def project_pairs(row_block, w_pairs, positions):
    head_size = w_pairs.shape[1] // 2
    paired = jnp.dot(row_block, w_pairs, preferred_element_type=jnp.float32)
    rotated = rotate(paired[:, None, :head_size], positions)[:, 0]
    return jnp.concatenate([rotated, paired[:, head_size:]], axis=1).astype(jnp.bfloat16)


def expert_block(first_ref, second_ref, share_ref, gate_up_ref, down_ref, out_ref):
    half_width = second_ref.shape[1]
    rows = jnp.concatenate([first_ref[:, :half_width], second_ref[...]], axis=1)
    inner_width = down_ref.shape[1]
    total = jnp.zeros(out_ref.shape, jnp.float32)
    for expert in range(gate_up_ref.shape[0]):
        both = jnp.dot(rows, gate_up_ref[expert], preferred_element_type=jnp.float32)
        gate_val = both[:, :inner_width]
        up_val = both[:, inner_width:]
        inner_act = (jax.nn.silu(gate_val) * up_val).astype(jnp.bfloat16)
        produced = jnp.dot(inner_act, down_ref[expert], preferred_element_type=jnp.float32)
        total = total + share_ref[:, expert : expert + 1] * produced
    out_ref[...] = total.astype(out_ref.dtype)


def dense_experts(first_rows, second_rows, shares, gate_up, down_proj):
    row_count, first_width = first_rows.shape
    second_width = second_rows.shape[1]
    model_width = gate_up.shape[1]
    expert_count = gate_up.shape[0]
    tile = 512
    return pl.pallas_call(
        expert_block,
        grid=(row_count // tile,),
        in_specs=[
            pl.BlockSpec((tile, first_width), lambda i: (i, 0)),
            pl.BlockSpec((tile, second_width), lambda i: (i, 0)),
            pl.BlockSpec((tile, expert_count), lambda i: (i, 0)),
            pl.BlockSpec(gate_up.shape, lambda i: (0, 0, 0)),
            pl.BlockSpec(down_proj.shape, lambda i: (0, 0, 0)),
        ],
        out_specs=pl.BlockSpec((tile, model_width), lambda i: (i, 0)),
        out_shape=jax.ShapeDtypeStruct((row_count, model_width), jnp.bfloat16),
        compiler_params=pltpu.CompilerParams(vmem_limit_bytes=48 * 1024 * 1024),
    )(first_rows, second_rows, shares, gate_up, down_proj)


def fold_bits(partial_sum, level_bits):
    index_now = lax.axis_index(TENSOR)
    for level_bit in level_bits:
        half_rows = partial_sum.shape[0] // 2
        lower_rows = partial_sum[:half_rows]
        upper_rows = partial_sum[half_rows:]
        is_upper = index_now >> level_bit & 1 == 1
        kept_rows = jnp.where(is_upper, upper_rows, lower_rows)
        sent_rows = jnp.where(is_upper, lower_rows, upper_rows)
        arrived = partner(sent_rows.astype(jnp.bfloat16), TENSOR, level_bit)
        partial_sum = kept_rows.astype(jnp.float32) + arrived.astype(jnp.float32)
    return partial_sum

def on_device(
    hidden, segment_ids, routes, route_weights, attn_gain, w_qkv, w_out, ffn_gain, w_gate_up, w_down
):
    device_count = lax.axis_size(TENSOR)
    quarters = device_count // KVH
    index_now = lax.axis_index(TENSOR)
    quarter_index = index_now // KVH
    group_index = index_now % KVH
    group_bits = list(range(KVH.bit_length() - 1))
    quarter_bits = list(range(len(group_bits), device_count.bit_length() - 1))
    seq_len = segment_ids.shape[0]
    rows_quarter = seq_len // quarters
    model_width = hidden.shape[1]
    starts = segment_starts(segment_ids)
    expert_total = w_gate_up.shape[0] * KVH
    expert_ids = jnp.arange(expert_total, dtype=jnp.int32)
    share_table = jnp.sum(
        jnp.where(
            routes[:, None, :] == expert_ids[None, :, None],
            route_weights[:, None, :],
            jnp.zeros((), route_weights.dtype),
        ),
        axis=2,
    )
    positions = jnp.arange(seq_len, dtype=jnp.int32) - starts
    own_positions = lax.dynamic_slice_in_dim(
        positions, quarter_index * rows_quarter, rows_quarter, 0
    )
    normed = rms_norm(hidden, attn_gain)
    qkv_width = w_qkv.shape[1]
    (w_group,) = gather_levels(
        (w_qkv,),
        quarter_bits,
        (1,),
        lambda payload, level_bit: (partner(payload[0], TENSOR, level_bit),),
    )
    (w_attn_out,) = gather_levels(
        (w_out,),
        quarter_bits,
        (1,),
        lambda payload, level_bit: (partner(payload[0], TENSOR, level_bit),),
    )
    w_query = w_group[:, : GQ * HD]
    w_pairs = w_group[:, GQ * HD :]
    (own_rows,) = gather_levels(
        (normed,),
        group_bits[::-1],
        (0,),
        lambda payload, level_bit: (partner(payload[0], TENSOR, level_bit),),
    )
    own_rows = (
        own_rows.reshape((2,) * len(group_bits) + normed.shape)
        .transpose(list(range(len(group_bits)))[::-1] + [len(group_bits), len(group_bits) + 1])
        .reshape(rows_quarter, model_width)
    )
    kv_block = project_pairs(own_rows, w_pairs, own_positions)
    (key_values,) = gather_levels(
        (kv_block,),
        quarter_bits,
        (0,),
        lambda payload, level_bit: (partner(payload[0], TENSOR, level_bit),),
    )
    query_proj = jnp.dot(own_rows, w_query, preferred_element_type=jnp.float32).reshape(
        rows_quarter, GQ, HD
    )
    queries_heads = rotate(query_proj, own_positions).astype(jnp.bfloat16).transpose(1, 0, 2)
    block_rows = min(256, rows_quarter)
    key_block = min(512, seq_len)

    def attend(block_number):
        first_row = block_number * block_rows
        block_queries = lax.dynamic_slice_in_dim(queries_heads, first_row, block_rows, 1).reshape(
            GQ * block_rows, HD
        )
        first_place = quarter_index * rows_quarter + first_row
        query_places = first_place + jnp.arange(block_rows, dtype=jnp.int32)
        query_starts = lax.dynamic_slice_in_dim(starts, first_place, block_rows, 0)
        lowest = query_starts[0] // key_block
        highest = (first_place + block_rows - 1) // key_block + 1

        def step_keys(key_number, loop_state):
            row_peak, totals, accumulated = loop_state
            key_offset = key_number * key_block
            block_pairs = lax.dynamic_slice_in_dim(key_values, key_offset, key_block, 0)
            key_places = key_offset + jnp.arange(key_block, dtype=jnp.int32)
            allowed = (key_places[None, :] <= query_places[:, None]) & (
                key_places[None, :] >= query_starts[:, None]
            )
            scores = (
                lax.dot_general(
                    block_queries,
                    block_pairs[:, :HD],
                    (((1,), (1,)), ((), ())),
                    preferred_element_type=jnp.float32,
                )
                * attn_scale
            )
            scores = jnp.where(jnp.tile(allowed, (GQ, 1)), scores, -jnp.inf)
            new_peak = jnp.maximum(row_peak, jnp.max(scores, axis=1))
            weights = jnp.exp(scores - new_peak[:, None])
            factor = jnp.exp(row_peak - new_peak)
            totals = totals * factor + jnp.sum(weights, axis=1)
            accumulated = accumulated * factor[:, None] + jnp.dot(
                weights.astype(jnp.bfloat16),
                block_pairs[:, HD:],
                preferred_element_type=jnp.float32,
            )
            return (new_peak, totals, accumulated)

        start_state = (
            jnp.full((GQ * block_rows,), masked_floor, jnp.float32),
            jnp.zeros((GQ * block_rows,), jnp.float32),
            jnp.zeros((GQ * block_rows, HD), jnp.float32),
        )
        row_peak, totals, accumulated = lax.fori_loop(lowest, highest, step_keys, start_state)
        mixed = (accumulated / totals[:, None]).astype(jnp.bfloat16).reshape(GQ, block_rows, HD)
        return mixed.transpose(1, 0, 2).reshape(block_rows, GQ * HD)

    attended = lax.map(attend, jnp.arange(rows_quarter // block_rows, dtype=jnp.int32)).reshape(
        rows_quarter, GQ * HD
    )
    partial_proj = lax.dot_general(
        attended, w_attn_out, (((1,), (1,)), ((), ())), preferred_element_type=jnp.float32
    )
    projection = fold_any(partial_proj, group_bits[::-1], group_bits)
    after_attention = (hidden.astype(jnp.float32) + residual_scale * projection).astype(
        jnp.bfloat16
    )
    expert_in = rms_norm(after_attention, ffn_gain)
    local_experts = w_gate_up.shape[0]
    share_cols = 128 * pl.cdiv(expert_total, 128)
    half_width = model_width // 2
    carried = jnp.concatenate(
        [
            expert_in[:, :half_width],
            share_table,
            jnp.zeros((share_table.shape[0], share_cols - expert_total), jnp.bfloat16),
        ],
        axis=1,
    )
    layout = (1, 3, 4, 2)
    first_order = (2, 4, 3, 1)
    second_order = (4, 2, 1, 3)
    first_rows = gather_any(carried, first_order)
    second_rows = gather_any(expert_in[:, half_width:], second_order)
    second_dims = list(second_order[::-1])
    second_perm = [second_dims.index(bit) for bit in layout] + [len(layout), len(layout) + 1]

    def run_half(first_part, second_part):
        first_flat = first_part.reshape(-1, first_part.shape[-1])
        second_flat = second_part.transpose(second_perm).reshape(-1, second_part.shape[-1])
        part_shares = lax.dynamic_slice_in_dim(
            first_flat[:, half_width : half_width + expert_total],
            group_index * local_experts,
            local_experts,
            1,
        ).astype(jnp.float32)
        return dense_experts(first_flat, second_flat, part_shares, w_gate_up, w_down)

    own_part = run_half(first_rows, second_rows)
    peer_part = run_half(partner(first_rows, TENSOR, 0), partner(second_rows, TENSOR, 0))
    flat_part = own_part.astype(jnp.float32) + partner(peer_part, TENSOR, 0).astype(jnp.float32)
    expert_sum = jnp.concatenate(
        [
            fold_any(flat_part[:, :half_width], layout, (1, 3, 4, 2)),
            fold_any(flat_part[:, half_width:], layout, (3, 1, 2, 4)),
        ],
        axis=1,
    )
    hidden_out = (after_attention.astype(jnp.float32) + residual_scale * expert_sum).astype(
        jnp.bfloat16
    )
    return (after_attention, hidden_out, kv_block[None])


def solution(mesh):
    grid = mesh.devices.reshape(mesh.devices.shape[0], -1, 4, 2)
    mesh = jax.sharding.Mesh(grid, ("dp",) + TENSOR)
    placed = (
        P(("dp",) + TENSOR, None),
        P("dp"),
        P(("dp",) + TENSOR, None),
        P(("dp",) + TENSOR, None),
        P(),
        P(None, TENSOR),
        P(None, TENSOR),
        P(),
        P(TENSOR, None, None),
        P(TENSOR, None, None),
    )
    return jax.shard_map(
        on_device,
        mesh=mesh,
        in_specs=placed,
        out_specs=(P(("dp",) + TENSOR, None), P(("dp",) + TENSOR, None), P(TENSOR, "dp", None)),
        check_vma=False,
    )
```

```python
import math

import jax
import jax.numpy as jnp
from jax import lax
from jax.sharding import PartitionSpec as P
from jax.experimental import pallas as pl
from jax.experimental.pallas import tpu as pltpu

KVH = 8
HD = 64
GQ = 3
CHIPS = ("ty", "tx")
TENSOR = ("ty", "tx", "tc")


attn_scale = 0.015625
residual_scale = 0.22
rope_base = 10000.0
norm_eps = 1e-06
masked_floor = -1e30


def partner(value, axis, apart):
    mask = 2**apart
    pairs = [(source, source ^ mask) for source in range(lax.axis_size(axis))]
    return lax.ppermute(value, axis, pairs)


def rms_norm(row_block, gain_row):
    widened = row_block.astype(jnp.float32)
    mean_square = jnp.mean(widened * widened, axis=-1, keepdims=True)
    return (widened * lax.rsqrt(mean_square + norm_eps) * gain_row).astype(jnp.bfloat16)


def segment_starts(segment_ids):
    places = jnp.arange(segment_ids.shape[0], dtype=jnp.int32)
    earlier = jnp.concatenate([segment_ids[:1] - 1, segment_ids[:-1]])
    boundary = jnp.where(segment_ids != earlier, places, jnp.zeros_like(places))
    return lax.cummax(boundary, axis=0)


def rotate(vectors, positions):
    half_width = vectors.shape[-1] // 2
    freq_steps = jnp.arange(half_width, dtype=jnp.float32)
    frequency = jnp.exp(freq_steps * (-2.0 * math.log(rope_base) / vectors.shape[-1]))
    angles = positions.astype(jnp.float32)[:, None] * frequency[None, :]
    cosine = jnp.cos(angles)[:, None, :]
    sine_part = jnp.sin(angles)[:, None, :]
    first_half = vectors[..., :half_width]
    second_half = vectors[..., half_width:]
    return jnp.concatenate(
        [
            first_half * cosine - second_half * sine_part,
            second_half * cosine + first_half * sine_part,
        ],
        axis=-1,
    )


def gather_levels(parts, level_bits, join_axes, sender):
    index_now = lax.axis_index(TENSOR)
    for level_bit in level_bits:
        arrived = sender(parts, level_bit)
        is_upper = index_now >> level_bit & 1 == 1
        joined_parts = []
        for own_part, peer_part, join_axis in zip(parts, arrived, join_axes):
            lower_first = jnp.concatenate([own_part, peer_part], join_axis)
            upper_first = jnp.concatenate([peer_part, own_part], join_axis)
            joined_parts.append(jnp.where(is_upper, upper_first, lower_first))
        parts = tuple(joined_parts)
    return parts


def fold_levels(partial_sum, level_bits, sender):
    index_now = lax.axis_index(TENSOR)
    for level_bit in reversed(level_bits):
        half_rows = partial_sum.shape[0] // 2
        lower_rows = partial_sum[:half_rows]
        upper_rows = partial_sum[half_rows:]
        is_upper = index_now >> level_bit & 1 == 1
        kept_rows = jnp.where(is_upper, upper_rows, lower_rows)
        sent_rows = jnp.where(is_upper, lower_rows, upper_rows)
        partial_sum = kept_rows + sender(sent_rows, level_bit)
    return partial_sum


def fold_any(partial_sum, layout_bits, level_bits):
    index_now = lax.axis_index(TENSOR)
    rows_left = partial_sum.shape[0] >> len(layout_bits)
    state = partial_sum.reshape((2,) * len(layout_bits) + (rows_left,) + partial_sum.shape[1:])
    dims = list(layout_bits)
    for level_bit in level_bits:
        place = dims.index(level_bit)
        lower_rows = lax.index_in_dim(state, 0, place, keepdims=False)
        upper_rows = lax.index_in_dim(state, 1, place, keepdims=False)
        is_upper = index_now >> level_bit & 1 == 1
        kept_rows = jnp.where(is_upper, upper_rows, lower_rows)
        sent_rows = jnp.where(is_upper, lower_rows, upper_rows)
        arrived = partner(sent_rows.astype(jnp.bfloat16), TENSOR, level_bit)
        state = kept_rows.astype(jnp.float32) + arrived.astype(jnp.float32)
        dims.pop(place)
    return state.reshape((rows_left,) + partial_sum.shape[1:])


def gather_any(part, level_bits):
    index_now = lax.axis_index(TENSOR)
    state = part
    for level_bit in level_bits:
        arrived = partner(state, TENSOR, level_bit)
        is_upper = index_now >> level_bit & 1 == 1
        lower_rows = jnp.where(is_upper, arrived, state)
        upper_rows = jnp.where(is_upper, state, arrived)
        state = jnp.stack([lower_rows, upper_rows], axis=0)
    return state


def project_pairs(row_block, w_pairs, positions):
    head_size = w_pairs.shape[1] // 2
    paired = jnp.dot(row_block, w_pairs, preferred_element_type=jnp.float32)
    rotated = rotate(paired[:, None, :head_size], positions)[:, 0]
    return jnp.concatenate([rotated, paired[:, head_size:]], axis=1).astype(jnp.bfloat16)


def expert_block(first_ref, second_ref, share_ref, gate_up_ref, down_ref, out_ref):
    half_width = second_ref.shape[1]
    rows = jnp.concatenate([first_ref[:, :half_width], second_ref[...]], axis=1)
    expert_count, inner_width, model_width = down_ref.shape
    scaled = []
    for expert in range(expert_count):
        both = jnp.dot(rows, gate_up_ref[expert], preferred_element_type=jnp.float32)
        gate_val = both[:, :inner_width]
        up_val = both[:, inner_width:]
        inner_act = jax.nn.silu(gate_val) * up_val * share_ref[:, expert : expert + 1]
        scaled.append(inner_act.astype(jnp.bfloat16))
    joined = jnp.concatenate(scaled, axis=1)
    down_all = down_ref[...].reshape(expert_count * inner_width, model_width)
    total = jnp.dot(joined, down_all, preferred_element_type=jnp.float32)
    out_ref[...] = total.astype(out_ref.dtype)


def dense_experts(first_rows, second_rows, shares, gate_up, down_proj):
    row_count, first_width = first_rows.shape
    second_width = second_rows.shape[1]
    model_width = gate_up.shape[1]
    expert_count = gate_up.shape[0]
    tile = 512
    return pl.pallas_call(
        expert_block,
        grid=(row_count // tile,),
        in_specs=[
            pl.BlockSpec((tile, first_width), lambda i: (i, 0)),
            pl.BlockSpec((tile, second_width), lambda i: (i, 0)),
            pl.BlockSpec((tile, expert_count), lambda i: (i, 0)),
            pl.BlockSpec(gate_up.shape, lambda i: (0, 0, 0)),
            pl.BlockSpec(down_proj.shape, lambda i: (0, 0, 0)),
        ],
        out_specs=pl.BlockSpec((tile, model_width), lambda i: (i, 0)),
        out_shape=jax.ShapeDtypeStruct((row_count, model_width), jnp.bfloat16),
        compiler_params=pltpu.CompilerParams(vmem_limit_bytes=48 * 1024 * 1024),
    )(first_rows, second_rows, shares, gate_up, down_proj)


def fold_bits(partial_sum, level_bits):
    index_now = lax.axis_index(TENSOR)
    for level_bit in level_bits:
        half_rows = partial_sum.shape[0] // 2
        lower_rows = partial_sum[:half_rows]
        upper_rows = partial_sum[half_rows:]
        is_upper = index_now >> level_bit & 1 == 1
        kept_rows = jnp.where(is_upper, upper_rows, lower_rows)
        sent_rows = jnp.where(is_upper, lower_rows, upper_rows)
        arrived = partner(sent_rows.astype(jnp.bfloat16), TENSOR, level_bit)
        partial_sum = kept_rows.astype(jnp.float32) + arrived.astype(jnp.float32)
    return partial_sum

def on_device(
    hidden, segment_ids, routes, route_weights, attn_gain, w_qkv, w_out, ffn_gain, w_gate_up, w_down
):
    device_count = lax.axis_size(TENSOR)
    quarters = device_count // KVH
    index_now = lax.axis_index(TENSOR)
    quarter_index = index_now // KVH
    group_index = index_now % KVH
    group_bits = list(range(KVH.bit_length() - 1))
    quarter_bits = list(range(len(group_bits), device_count.bit_length() - 1))
    seq_len = segment_ids.shape[0]
    rows_quarter = seq_len // quarters
    model_width = hidden.shape[1]
    starts = segment_starts(segment_ids)
    expert_total = w_gate_up.shape[0] * KVH
    expert_ids = jnp.arange(expert_total, dtype=jnp.int32)
    share_table = jnp.sum(
        jnp.where(
            routes[:, None, :] == expert_ids[None, :, None],
            route_weights[:, None, :],
            jnp.zeros((), route_weights.dtype),
        ),
        axis=2,
    )
    positions = jnp.arange(seq_len, dtype=jnp.int32) - starts
    own_positions = lax.dynamic_slice_in_dim(
        positions, quarter_index * rows_quarter, rows_quarter, 0
    )
    normed = rms_norm(hidden, attn_gain)
    qkv_width = w_qkv.shape[1]
    (w_group,) = gather_levels(
        (w_qkv,),
        quarter_bits,
        (1,),
        lambda payload, level_bit: (partner(payload[0], TENSOR, level_bit),),
    )
    (w_attn_out,) = gather_levels(
        (w_out,),
        quarter_bits,
        (1,),
        lambda payload, level_bit: (partner(payload[0], TENSOR, level_bit),),
    )
    w_query = w_group[:, : GQ * HD]
    w_pairs = w_group[:, GQ * HD :]
    (own_rows,) = gather_levels(
        (normed,),
        group_bits[::-1],
        (0,),
        lambda payload, level_bit: (partner(payload[0], TENSOR, level_bit),),
    )
    own_rows = (
        own_rows.reshape((2,) * len(group_bits) + normed.shape)
        .transpose(list(range(len(group_bits)))[::-1] + [len(group_bits), len(group_bits) + 1])
        .reshape(rows_quarter, model_width)
    )
    kv_block = project_pairs(own_rows, w_pairs, own_positions)
    (key_values,) = gather_levels(
        (kv_block,),
        quarter_bits,
        (0,),
        lambda payload, level_bit: (partner(payload[0], TENSOR, level_bit),),
    )
    query_proj = jnp.dot(own_rows, w_query, preferred_element_type=jnp.float32).reshape(
        rows_quarter, GQ, HD
    )
    queries_heads = rotate(query_proj, own_positions).astype(jnp.bfloat16).transpose(1, 0, 2)
    block_rows = min(256, rows_quarter)
    key_block = min(512, seq_len)

    def attend(block_number):
        first_row = block_number * block_rows
        block_queries = lax.dynamic_slice_in_dim(queries_heads, first_row, block_rows, 1).reshape(
            GQ * block_rows, HD
        )
        first_place = quarter_index * rows_quarter + first_row
        query_places = first_place + jnp.arange(block_rows, dtype=jnp.int32)
        query_starts = lax.dynamic_slice_in_dim(starts, first_place, block_rows, 0)
        lowest = query_starts[0] // key_block
        highest = (first_place + block_rows - 1) // key_block + 1

        def step_keys(key_number, loop_state):
            row_peak, totals, accumulated = loop_state
            key_offset = key_number * key_block
            block_pairs = lax.dynamic_slice_in_dim(key_values, key_offset, key_block, 0)
            key_places = key_offset + jnp.arange(key_block, dtype=jnp.int32)
            allowed = (key_places[None, :] <= query_places[:, None]) & (
                key_places[None, :] >= query_starts[:, None]
            )
            scores = (
                lax.dot_general(
                    block_queries,
                    block_pairs[:, :HD],
                    (((1,), (1,)), ((), ())),
                    preferred_element_type=jnp.float32,
                )
                * attn_scale
            )
            scores = jnp.where(jnp.tile(allowed, (GQ, 1)), scores, -jnp.inf)
            new_peak = jnp.maximum(row_peak, jnp.max(scores, axis=1))
            weights = jnp.exp(scores - new_peak[:, None])
            factor = jnp.exp(row_peak - new_peak)
            totals = totals * factor + jnp.sum(weights, axis=1)
            accumulated = accumulated * factor[:, None] + jnp.dot(
                weights.astype(jnp.bfloat16),
                block_pairs[:, HD:],
                preferred_element_type=jnp.float32,
            )
            return (new_peak, totals, accumulated)

        start_state = (
            jnp.full((GQ * block_rows,), masked_floor, jnp.float32),
            jnp.zeros((GQ * block_rows,), jnp.float32),
            jnp.zeros((GQ * block_rows, HD), jnp.float32),
        )
        row_peak, totals, accumulated = lax.fori_loop(lowest, highest, step_keys, start_state)
        mixed = (accumulated / totals[:, None]).astype(jnp.bfloat16).reshape(GQ, block_rows, HD)
        return mixed.transpose(1, 0, 2).reshape(block_rows, GQ * HD)

    attended = lax.map(attend, jnp.arange(rows_quarter // block_rows, dtype=jnp.int32)).reshape(
        rows_quarter, GQ * HD
    )
    partial_proj = lax.dot_general(
        attended, w_attn_out, (((1,), (1,)), ((), ())), preferred_element_type=jnp.float32
    )
    projection = fold_any(partial_proj, group_bits[::-1], group_bits)
    after_attention = (hidden.astype(jnp.float32) + residual_scale * projection).astype(
        jnp.bfloat16
    )
    expert_in = rms_norm(after_attention, ffn_gain)
    local_experts = w_gate_up.shape[0]
    share_cols = 128 * pl.cdiv(expert_total, 128)
    half_width = model_width // 2
    carried = jnp.concatenate(
        [
            expert_in[:, :half_width],
            share_table,
            jnp.zeros((share_table.shape[0], share_cols - expert_total), jnp.bfloat16),
        ],
        axis=1,
    )
    layout = (0, 1, 3, 4, 2)
    first_order = (2, 4, 3, 1, 0)
    second_order = (4, 2, 1, 3, 0)
    first_rows = gather_any(carried, first_order)
    second_rows = gather_any(expert_in[:, half_width:], second_order)
    second_dims = list(second_order[::-1])
    second_rows = second_rows.transpose(
        [second_dims.index(bit) for bit in layout] + [len(layout), len(layout) + 1]
    )
    first_rows = first_rows.reshape(-1, first_rows.shape[-1])
    second_rows = second_rows.reshape(-1, second_rows.shape[-1])
    local_shares = lax.dynamic_slice_in_dim(
        first_rows[:, half_width : half_width + expert_total],
        group_index * local_experts,
        local_experts,
        1,
    ).astype(jnp.float32)
    expert_part = dense_experts(first_rows, second_rows, local_shares, w_gate_up, w_down)
    flat_part = expert_part
    expert_sum = jnp.concatenate(
        [
            fold_any(flat_part[:, :half_width], layout, (0, 1, 3, 4, 2)),
            fold_any(flat_part[:, half_width:], layout, (0, 3, 1, 2, 4)),
        ],
        axis=1,
    )
    hidden_out = (after_attention.astype(jnp.float32) + residual_scale * expert_sum).astype(
        jnp.bfloat16
    )
    return (after_attention, hidden_out, kv_block[None])


def solution(mesh):
    grid = mesh.devices.reshape(mesh.devices.shape[0], -1, 4, 2)
    mesh = jax.sharding.Mesh(grid, ("dp",) + TENSOR)
    placed = (
        P(("dp",) + TENSOR, None),
        P("dp"),
        P(("dp",) + TENSOR, None),
        P(("dp",) + TENSOR, None),
        P(),
        P(None, TENSOR),
        P(None, TENSOR),
        P(),
        P(TENSOR, None, None),
        P(TENSOR, None, None),
    )
    return jax.shard_map(
        on_device,
        mesh=mesh,
        in_specs=placed,
        out_specs=(P(("dp",) + TENSOR, None), P(("dp",) + TENSOR, None), P(TENSOR, "dp", None)),
        check_vma=False,
    )
```

```python
import math

import jax
import jax.numpy as jnp
from jax import lax
from jax.sharding import PartitionSpec as P
from jax.experimental import pallas as pl
from jax.experimental.pallas import tpu as pltpu

KVH = 8
HD = 64
GQ = 3
CHIPS = ("ty", "tx")
TENSOR = ("ty", "tx", "tc")


attn_scale = 0.015625
residual_scale = 0.22
rope_base = 10000.0
norm_eps = 1e-06
masked_floor = -1e30


def partner(value, axis, apart):
    mask = 2**apart
    pairs = [(source, source ^ mask) for source in range(lax.axis_size(axis))]
    return lax.ppermute(value, axis, pairs)


def rms_norm(row_block, gain_row):
    widened = row_block.astype(jnp.float32)
    mean_square = jnp.mean(widened * widened, axis=-1, keepdims=True)
    return (widened * lax.rsqrt(mean_square + norm_eps) * gain_row).astype(jnp.bfloat16)


def segment_starts(segment_ids):
    places = jnp.arange(segment_ids.shape[0], dtype=jnp.int32)
    earlier = jnp.concatenate([segment_ids[:1] - 1, segment_ids[:-1]])
    boundary = jnp.where(segment_ids != earlier, places, jnp.zeros_like(places))
    return lax.cummax(boundary, axis=0)


def rotate(vectors, positions):
    half_width = vectors.shape[-1] // 2
    freq_steps = jnp.arange(half_width, dtype=jnp.float32)
    frequency = jnp.exp(freq_steps * (-2.0 * math.log(rope_base) / vectors.shape[-1]))
    angles = positions.astype(jnp.float32)[:, None] * frequency[None, :]
    cosine = jnp.cos(angles)[:, None, :]
    sine_part = jnp.sin(angles)[:, None, :]
    first_half = vectors[..., :half_width]
    second_half = vectors[..., half_width:]
    return jnp.concatenate(
        [
            first_half * cosine - second_half * sine_part,
            second_half * cosine + first_half * sine_part,
        ],
        axis=-1,
    )


def gather_levels(parts, level_bits, join_axes, sender):
    index_now = lax.axis_index(TENSOR)
    for level_bit in level_bits:
        arrived = sender(parts, level_bit)
        is_upper = index_now >> level_bit & 1 == 1
        joined_parts = []
        for own_part, peer_part, join_axis in zip(parts, arrived, join_axes):
            lower_first = jnp.concatenate([own_part, peer_part], join_axis)
            upper_first = jnp.concatenate([peer_part, own_part], join_axis)
            joined_parts.append(jnp.where(is_upper, upper_first, lower_first))
        parts = tuple(joined_parts)
    return parts


def fold_levels(partial_sum, level_bits, sender):
    index_now = lax.axis_index(TENSOR)
    for level_bit in reversed(level_bits):
        half_rows = partial_sum.shape[0] // 2
        lower_rows = partial_sum[:half_rows]
        upper_rows = partial_sum[half_rows:]
        is_upper = index_now >> level_bit & 1 == 1
        kept_rows = jnp.where(is_upper, upper_rows, lower_rows)
        sent_rows = jnp.where(is_upper, lower_rows, upper_rows)
        partial_sum = kept_rows + sender(sent_rows, level_bit)
    return partial_sum


def fold_any(partial_sum, layout_bits, level_bits):
    index_now = lax.axis_index(TENSOR)
    rows_left = partial_sum.shape[0] >> len(layout_bits)
    state = partial_sum.reshape((2,) * len(layout_bits) + (rows_left,) + partial_sum.shape[1:])
    dims = list(layout_bits)
    for level_bit in level_bits:
        place = dims.index(level_bit)
        lower_rows = lax.index_in_dim(state, 0, place, keepdims=False)
        upper_rows = lax.index_in_dim(state, 1, place, keepdims=False)
        is_upper = index_now >> level_bit & 1 == 1
        kept_rows = jnp.where(is_upper, upper_rows, lower_rows)
        sent_rows = jnp.where(is_upper, lower_rows, upper_rows)
        arrived = partner(sent_rows.astype(jnp.bfloat16), TENSOR, level_bit)
        state = kept_rows.astype(jnp.float32) + arrived.astype(jnp.float32)
        dims.pop(place)
    return state.reshape((rows_left,) + partial_sum.shape[1:])


def gather_any(part, level_bits):
    index_now = lax.axis_index(TENSOR)
    state = part
    for level_bit in level_bits:
        arrived = partner(state, TENSOR, level_bit)
        is_upper = index_now >> level_bit & 1 == 1
        lower_rows = jnp.where(is_upper, arrived, state)
        upper_rows = jnp.where(is_upper, state, arrived)
        state = jnp.stack([lower_rows, upper_rows], axis=0)
    return state


def project_pairs(row_block, w_pairs, positions):
    head_size = w_pairs.shape[1] // 2
    paired = jnp.dot(row_block, w_pairs, preferred_element_type=jnp.float32)
    rotated = rotate(paired[:, None, :head_size], positions)[:, 0]
    return jnp.concatenate([rotated, paired[:, head_size:]], axis=1).astype(jnp.bfloat16)


def expert_block(first_ref, second_ref, share_ref, gate_up_ref, down_ref, out_ref):
    half_width = second_ref.shape[1]
    rows = jnp.concatenate([first_ref[:, :half_width], second_ref[...]], axis=1)
    expert_count, inner_width, model_width = down_ref.shape
    scaled = []
    for expert in range(expert_count):
        both = jnp.dot(rows, gate_up_ref[expert], preferred_element_type=jnp.float32)
        gate_val = both[:, :inner_width]
        up_val = both[:, inner_width:]
        inner_act = jax.nn.silu(gate_val) * up_val * share_ref[:, expert : expert + 1]
        scaled.append(inner_act.astype(jnp.bfloat16))
    joined = jnp.concatenate(scaled, axis=1)
    down_all = down_ref[...].reshape(expert_count * inner_width, model_width)
    total = jnp.dot(joined, down_all, preferred_element_type=jnp.float32)
    out_ref[...] = total.astype(out_ref.dtype)


def dense_experts(first_rows, second_rows, shares, gate_up, down_proj):
    row_count, first_width = first_rows.shape
    second_width = second_rows.shape[1]
    model_width = gate_up.shape[1]
    expert_count = gate_up.shape[0]
    tile = 1024
    return pl.pallas_call(
        expert_block,
        grid=(row_count // tile,),
        in_specs=[
            pl.BlockSpec((tile, first_width), lambda i: (i, 0)),
            pl.BlockSpec((tile, second_width), lambda i: (i, 0)),
            pl.BlockSpec((tile, expert_count), lambda i: (i, 0)),
            pl.BlockSpec(gate_up.shape, lambda i: (0, 0, 0)),
            pl.BlockSpec(down_proj.shape, lambda i: (0, 0, 0)),
        ],
        out_specs=pl.BlockSpec((tile, model_width), lambda i: (i, 0)),
        out_shape=jax.ShapeDtypeStruct((row_count, model_width), jnp.bfloat16),
        compiler_params=pltpu.CompilerParams(vmem_limit_bytes=48 * 1024 * 1024),
    )(first_rows, second_rows, shares, gate_up, down_proj)


def fold_bits(partial_sum, level_bits):
    index_now = lax.axis_index(TENSOR)
    for level_bit in level_bits:
        half_rows = partial_sum.shape[0] // 2
        lower_rows = partial_sum[:half_rows]
        upper_rows = partial_sum[half_rows:]
        is_upper = index_now >> level_bit & 1 == 1
        kept_rows = jnp.where(is_upper, upper_rows, lower_rows)
        sent_rows = jnp.where(is_upper, lower_rows, upper_rows)
        arrived = partner(sent_rows.astype(jnp.bfloat16), TENSOR, level_bit)
        partial_sum = kept_rows.astype(jnp.float32) + arrived.astype(jnp.float32)
    return partial_sum

def on_device(
    hidden, segment_ids, routes, route_weights, attn_gain, w_qkv, w_out, ffn_gain, w_gate_up, w_down
):
    device_count = lax.axis_size(TENSOR)
    quarters = device_count // KVH
    index_now = lax.axis_index(TENSOR)
    quarter_index = index_now // KVH
    group_index = index_now % KVH
    group_bits = list(range(KVH.bit_length() - 1))
    quarter_bits = list(range(len(group_bits), device_count.bit_length() - 1))
    seq_len = segment_ids.shape[0]
    rows_quarter = seq_len // quarters
    model_width = hidden.shape[1]
    starts = segment_starts(segment_ids)
    expert_total = w_gate_up.shape[0] * KVH
    expert_ids = jnp.arange(expert_total, dtype=jnp.int32)
    share_table = jnp.sum(
        jnp.where(
            routes[:, None, :] == expert_ids[None, :, None],
            route_weights[:, None, :],
            jnp.zeros((), route_weights.dtype),
        ),
        axis=2,
    )
    positions = jnp.arange(seq_len, dtype=jnp.int32) - starts
    own_positions = lax.dynamic_slice_in_dim(
        positions, quarter_index * rows_quarter, rows_quarter, 0
    )
    normed = rms_norm(hidden, attn_gain)
    qkv_width = w_qkv.shape[1]
    (w_group,) = gather_levels(
        (w_qkv,),
        quarter_bits,
        (1,),
        lambda payload, level_bit: (partner(payload[0], TENSOR, level_bit),),
    )
    (w_attn_out,) = gather_levels(
        (w_out,),
        quarter_bits,
        (1,),
        lambda payload, level_bit: (partner(payload[0], TENSOR, level_bit),),
    )
    w_query = w_group[:, : GQ * HD]
    w_pairs = w_group[:, GQ * HD :]
    (own_rows,) = gather_levels(
        (normed,),
        group_bits[::-1],
        (0,),
        lambda payload, level_bit: (partner(payload[0], TENSOR, level_bit),),
    )
    own_rows = (
        own_rows.reshape((2,) * len(group_bits) + normed.shape)
        .transpose(list(range(len(group_bits)))[::-1] + [len(group_bits), len(group_bits) + 1])
        .reshape(rows_quarter, model_width)
    )
    kv_block = project_pairs(own_rows, w_pairs, own_positions)
    (key_values,) = gather_levels(
        (kv_block,),
        quarter_bits,
        (0,),
        lambda payload, level_bit: (partner(payload[0], TENSOR, level_bit),),
    )
    query_proj = jnp.dot(own_rows, w_query, preferred_element_type=jnp.float32).reshape(
        rows_quarter, GQ, HD
    )
    queries_heads = rotate(query_proj, own_positions).astype(jnp.bfloat16).transpose(1, 0, 2)
    block_rows = min(256, rows_quarter)
    key_block = min(512, seq_len)

    def attend(block_number):
        first_row = block_number * block_rows
        block_queries = lax.dynamic_slice_in_dim(queries_heads, first_row, block_rows, 1).reshape(
            GQ * block_rows, HD
        )
        first_place = quarter_index * rows_quarter + first_row
        query_places = first_place + jnp.arange(block_rows, dtype=jnp.int32)
        query_starts = lax.dynamic_slice_in_dim(starts, first_place, block_rows, 0)
        lowest = query_starts[0] // key_block
        highest = (first_place + block_rows - 1) // key_block + 1

        def step_keys(key_number, loop_state):
            row_peak, totals, accumulated = loop_state
            key_offset = key_number * key_block
            block_pairs = lax.dynamic_slice_in_dim(key_values, key_offset, key_block, 0)
            key_places = key_offset + jnp.arange(key_block, dtype=jnp.int32)
            allowed = (key_places[None, :] <= query_places[:, None]) & (
                key_places[None, :] >= query_starts[:, None]
            )
            scores = (
                lax.dot_general(
                    block_queries,
                    block_pairs[:, :HD],
                    (((1,), (1,)), ((), ())),
                    preferred_element_type=jnp.float32,
                )
                * attn_scale
            )
            scores = jnp.where(jnp.tile(allowed, (GQ, 1)), scores, -jnp.inf)
            new_peak = jnp.maximum(row_peak, jnp.max(scores, axis=1))
            weights = jnp.exp(scores - new_peak[:, None])
            factor = jnp.exp(row_peak - new_peak)
            totals = totals * factor + jnp.sum(weights, axis=1)
            accumulated = accumulated * factor[:, None] + jnp.dot(
                weights.astype(jnp.bfloat16),
                block_pairs[:, HD:],
                preferred_element_type=jnp.float32,
            )
            return (new_peak, totals, accumulated)

        start_state = (
            jnp.full((GQ * block_rows,), masked_floor, jnp.float32),
            jnp.zeros((GQ * block_rows,), jnp.float32),
            jnp.zeros((GQ * block_rows, HD), jnp.float32),
        )
        row_peak, totals, accumulated = lax.fori_loop(lowest, highest, step_keys, start_state)
        mixed = (accumulated / totals[:, None]).astype(jnp.bfloat16).reshape(GQ, block_rows, HD)
        return mixed.transpose(1, 0, 2).reshape(block_rows, GQ * HD)

    attended = lax.map(attend, jnp.arange(rows_quarter // block_rows, dtype=jnp.int32)).reshape(
        rows_quarter, GQ * HD
    )
    partial_proj = lax.dot_general(
        attended, w_attn_out, (((1,), (1,)), ((), ())), preferred_element_type=jnp.float32
    )
    projection = fold_any(partial_proj, group_bits[::-1], group_bits)
    after_attention = (hidden.astype(jnp.float32) + residual_scale * projection).astype(
        jnp.bfloat16
    )
    expert_in = rms_norm(after_attention, ffn_gain)
    local_experts = w_gate_up.shape[0]
    share_cols = 128 * pl.cdiv(expert_total, 128)
    half_width = model_width // 2
    carried = jnp.concatenate(
        [
            expert_in[:, :half_width],
            share_table,
            jnp.zeros((share_table.shape[0], share_cols - expert_total), jnp.bfloat16),
        ],
        axis=1,
    )
    layout = (0, 1, 3, 4, 2)
    first_order = (2, 4, 3, 1, 0)
    second_order = (4, 2, 1, 3, 0)
    first_rows = gather_any(carried, first_order)
    second_rows = gather_any(expert_in[:, half_width:], second_order)
    second_dims = list(second_order[::-1])
    second_rows = second_rows.transpose(
        [second_dims.index(bit) for bit in layout] + [len(layout), len(layout) + 1]
    )
    first_rows = first_rows.reshape(-1, first_rows.shape[-1])
    second_rows = second_rows.reshape(-1, second_rows.shape[-1])
    local_shares = lax.dynamic_slice_in_dim(
        first_rows[:, half_width : half_width + expert_total],
        group_index * local_experts,
        local_experts,
        1,
    ).astype(jnp.float32)
    expert_part = dense_experts(first_rows, second_rows, local_shares, w_gate_up, w_down)
    flat_part = expert_part
    expert_sum = jnp.concatenate(
        [
            fold_any(flat_part[:, :half_width], layout, (0, 1, 3, 4, 2)),
            fold_any(flat_part[:, half_width:], layout, (0, 3, 1, 2, 4)),
        ],
        axis=1,
    )
    hidden_out = (after_attention.astype(jnp.float32) + residual_scale * expert_sum).astype(
        jnp.bfloat16
    )
    return (after_attention, hidden_out, kv_block[None])


def solution(mesh):
    grid = mesh.devices.reshape(mesh.devices.shape[0], -1, 4, 2)
    mesh = jax.sharding.Mesh(grid, ("dp",) + TENSOR)
    placed = (
        P(("dp",) + TENSOR, None),
        P("dp"),
        P(("dp",) + TENSOR, None),
        P(("dp",) + TENSOR, None),
        P(),
        P(None, TENSOR),
        P(None, TENSOR),
        P(),
        P(TENSOR, None, None),
        P(TENSOR, None, None),
    )
    return jax.shard_map(
        on_device,
        mesh=mesh,
        in_specs=placed,
        out_specs=(P(("dp",) + TENSOR, None), P(("dp",) + TENSOR, None), P(TENSOR, "dp", None)),
        check_vma=False,
    )
```

```python
import math

import jax
import jax.numpy as jnp
from jax import lax
from jax.sharding import PartitionSpec as P
from jax.experimental import pallas as pl
from jax.experimental.pallas import tpu as pltpu

KVH = 8
HD = 64
GQ = 3
CHIPS = ("ty", "tx")
TENSOR = ("ty", "tx", "tc")


attn_scale = 0.015625
residual_scale = 0.22
rope_base = 10000.0
norm_eps = 1e-06
masked_floor = -1e30


def partner(value, axis, apart):
    mask = 2**apart
    pairs = [(source, source ^ mask) for source in range(lax.axis_size(axis))]
    return lax.ppermute(value, axis, pairs)


def rms_norm(row_block, gain_row):
    widened = row_block.astype(jnp.float32)
    mean_square = jnp.mean(widened * widened, axis=-1, keepdims=True)
    return (widened * lax.rsqrt(mean_square + norm_eps) * gain_row).astype(jnp.bfloat16)


def segment_starts(segment_ids):
    places = jnp.arange(segment_ids.shape[0], dtype=jnp.int32)
    earlier = jnp.concatenate([segment_ids[:1] - 1, segment_ids[:-1]])
    boundary = jnp.where(segment_ids != earlier, places, jnp.zeros_like(places))
    return lax.cummax(boundary, axis=0)


def rotate(vectors, positions):
    half_width = vectors.shape[-1] // 2
    freq_steps = jnp.arange(half_width, dtype=jnp.float32)
    frequency = jnp.exp(freq_steps * (-2.0 * math.log(rope_base) / vectors.shape[-1]))
    angles = positions.astype(jnp.float32)[:, None] * frequency[None, :]
    cosine = jnp.cos(angles)[:, None, :]
    sine_part = jnp.sin(angles)[:, None, :]
    first_half = vectors[..., :half_width]
    second_half = vectors[..., half_width:]
    return jnp.concatenate(
        [
            first_half * cosine - second_half * sine_part,
            second_half * cosine + first_half * sine_part,
        ],
        axis=-1,
    )


def gather_levels(parts, level_bits, join_axes, sender):
    index_now = lax.axis_index(TENSOR)
    for level_bit in level_bits:
        arrived = sender(parts, level_bit)
        is_upper = index_now >> level_bit & 1 == 1
        joined_parts = []
        for own_part, peer_part, join_axis in zip(parts, arrived, join_axes):
            lower_first = jnp.concatenate([own_part, peer_part], join_axis)
            upper_first = jnp.concatenate([peer_part, own_part], join_axis)
            joined_parts.append(jnp.where(is_upper, upper_first, lower_first))
        parts = tuple(joined_parts)
    return parts


def fold_levels(partial_sum, level_bits, sender):
    index_now = lax.axis_index(TENSOR)
    for level_bit in reversed(level_bits):
        half_rows = partial_sum.shape[0] // 2
        lower_rows = partial_sum[:half_rows]
        upper_rows = partial_sum[half_rows:]
        is_upper = index_now >> level_bit & 1 == 1
        kept_rows = jnp.where(is_upper, upper_rows, lower_rows)
        sent_rows = jnp.where(is_upper, lower_rows, upper_rows)
        partial_sum = kept_rows + sender(sent_rows, level_bit)
    return partial_sum


def fold_any(partial_sum, layout_bits, level_bits):
    index_now = lax.axis_index(TENSOR)
    rows_left = partial_sum.shape[0] >> len(layout_bits)
    state = partial_sum.reshape((2,) * len(layout_bits) + (rows_left,) + partial_sum.shape[1:])
    dims = list(layout_bits)
    for level_bit in level_bits:
        place = dims.index(level_bit)
        lower_rows = lax.index_in_dim(state, 0, place, keepdims=False)
        upper_rows = lax.index_in_dim(state, 1, place, keepdims=False)
        is_upper = index_now >> level_bit & 1 == 1
        kept_rows = jnp.where(is_upper, upper_rows, lower_rows)
        sent_rows = jnp.where(is_upper, lower_rows, upper_rows)
        arrived = partner(sent_rows.astype(jnp.bfloat16), TENSOR, level_bit)
        state = kept_rows.astype(jnp.float32) + arrived.astype(jnp.float32)
        dims.pop(place)
    return state.reshape((rows_left,) + partial_sum.shape[1:])


def gather_any(part, level_bits):
    index_now = lax.axis_index(TENSOR)
    state = part
    for level_bit in level_bits:
        arrived = partner(state, TENSOR, level_bit)
        is_upper = index_now >> level_bit & 1 == 1
        lower_rows = jnp.where(is_upper, arrived, state)
        upper_rows = jnp.where(is_upper, state, arrived)
        state = jnp.stack([lower_rows, upper_rows], axis=0)
    return state


def project_pairs(row_block, w_pairs, positions):
    head_size = w_pairs.shape[1] // 2
    paired = jnp.dot(row_block, w_pairs, preferred_element_type=jnp.float32)
    rotated = rotate(paired[:, None, :head_size], positions)[:, 0]
    return jnp.concatenate([rotated, paired[:, head_size:]], axis=1).astype(jnp.bfloat16)


def expert_block(first_ref, second_ref, share_ref, gate_up_ref, down_ref, out_ref):
    half_width = second_ref.shape[1]
    rows = jnp.concatenate([first_ref[:, :half_width], second_ref[...]], axis=1)
    expert_count, inner_width, model_width = down_ref.shape
    scaled = []
    for expert in range(expert_count):
        both = jnp.dot(rows, gate_up_ref[expert], preferred_element_type=jnp.float32)
        gate_val = both[:, :inner_width]
        up_val = both[:, inner_width:]
        inner_act = jax.nn.silu(gate_val) * up_val * share_ref[:, expert : expert + 1]
        scaled.append(inner_act.astype(jnp.bfloat16))
    joined = jnp.concatenate(scaled, axis=1)
    down_all = down_ref[...].reshape(expert_count * inner_width, model_width)
    total = jnp.dot(joined, down_all, preferred_element_type=jnp.float32)
    out_ref[...] = total.astype(out_ref.dtype)


def dense_experts(first_rows, second_rows, shares, gate_up, down_proj):
    row_count, first_width = first_rows.shape
    second_width = second_rows.shape[1]
    model_width = gate_up.shape[1]
    expert_count = gate_up.shape[0]
    tile = 512
    return pl.pallas_call(
        expert_block,
        grid=(row_count // tile,),
        in_specs=[
            pl.BlockSpec((tile, first_width), lambda i: (i, 0)),
            pl.BlockSpec((tile, second_width), lambda i: (i, 0)),
            pl.BlockSpec((tile, expert_count), lambda i: (i, 0)),
            pl.BlockSpec(gate_up.shape, lambda i: (0, 0, 0)),
            pl.BlockSpec(down_proj.shape, lambda i: (0, 0, 0)),
        ],
        out_specs=pl.BlockSpec((tile, model_width), lambda i: (i, 0)),
        out_shape=jax.ShapeDtypeStruct((row_count, model_width), jnp.bfloat16),
        compiler_params=pltpu.CompilerParams(vmem_limit_bytes=48 * 1024 * 1024),
    )(first_rows, second_rows, shares, gate_up, down_proj)


def fold_bits(partial_sum, level_bits):
    index_now = lax.axis_index(TENSOR)
    for level_bit in level_bits:
        half_rows = partial_sum.shape[0] // 2
        lower_rows = partial_sum[:half_rows]
        upper_rows = partial_sum[half_rows:]
        is_upper = index_now >> level_bit & 1 == 1
        kept_rows = jnp.where(is_upper, upper_rows, lower_rows)
        sent_rows = jnp.where(is_upper, lower_rows, upper_rows)
        arrived = partner(sent_rows.astype(jnp.bfloat16), TENSOR, level_bit)
        partial_sum = kept_rows.astype(jnp.float32) + arrived.astype(jnp.float32)
    return partial_sum

def on_device(
    hidden, segment_ids, routes, route_weights, attn_gain, w_qkv, w_out, ffn_gain, w_gate_up, w_down
):
    device_count = lax.axis_size(TENSOR)
    quarters = device_count // KVH
    index_now = lax.axis_index(TENSOR)
    quarter_index = index_now // KVH
    group_index = index_now % KVH
    group_bits = list(range(KVH.bit_length() - 1))
    quarter_bits = list(range(len(group_bits), device_count.bit_length() - 1))
    seq_len = segment_ids.shape[0]
    rows_quarter = seq_len // quarters
    model_width = hidden.shape[1]
    starts = segment_starts(segment_ids)
    expert_total = w_gate_up.shape[0] * KVH
    expert_ids = jnp.arange(expert_total, dtype=jnp.int32)
    share_table = jnp.sum(
        jnp.where(
            routes[:, None, :] == expert_ids[None, :, None],
            route_weights[:, None, :],
            jnp.zeros((), route_weights.dtype),
        ),
        axis=2,
    )
    positions = jnp.arange(seq_len, dtype=jnp.int32) - starts
    own_positions = lax.dynamic_slice_in_dim(
        positions, quarter_index * rows_quarter, rows_quarter, 0
    )
    normed = rms_norm(hidden, attn_gain)
    qkv_width = w_qkv.shape[1]
    (w_group,) = gather_levels(
        (w_qkv,),
        quarter_bits,
        (1,),
        lambda payload, level_bit: (partner(payload[0], TENSOR, level_bit),),
    )
    (w_attn_out,) = gather_levels(
        (w_out,),
        quarter_bits,
        (1,),
        lambda payload, level_bit: (partner(payload[0], TENSOR, level_bit),),
    )
    w_query = w_group[:, : GQ * HD]
    w_pairs = w_group[:, GQ * HD :]
    (own_rows,) = gather_levels(
        (normed,),
        group_bits[::-1],
        (0,),
        lambda payload, level_bit: (partner(payload[0], TENSOR, level_bit),),
    )
    own_rows = (
        own_rows.reshape((2,) * len(group_bits) + normed.shape)
        .transpose(list(range(len(group_bits)))[::-1] + [len(group_bits), len(group_bits) + 1])
        .reshape(rows_quarter, model_width)
    )
    kv_block = project_pairs(own_rows, w_pairs, own_positions)
    (key_values,) = gather_levels(
        (kv_block,),
        quarter_bits,
        (0,),
        lambda payload, level_bit: (partner(payload[0], TENSOR, level_bit),),
    )
    query_proj = jnp.dot(own_rows, w_query, preferred_element_type=jnp.float32).reshape(
        rows_quarter, GQ, HD
    )
    queries_heads = rotate(query_proj, own_positions).astype(jnp.bfloat16).transpose(1, 0, 2)
    block_rows = min(256, rows_quarter)
    key_block = min(512, seq_len)

    def attend(block_number):
        first_row = block_number * block_rows
        block_queries = lax.dynamic_slice_in_dim(queries_heads, first_row, block_rows, 1).reshape(
            GQ * block_rows, HD
        )
        first_place = quarter_index * rows_quarter + first_row
        query_places = first_place + jnp.arange(block_rows, dtype=jnp.int32)
        query_starts = lax.dynamic_slice_in_dim(starts, first_place, block_rows, 0)
        lowest = query_starts[0] // key_block
        highest = (first_place + block_rows - 1) // key_block + 1

        def step_keys(key_number, loop_state):
            row_peak, totals, accumulated = loop_state
            key_offset = key_number * key_block
            block_pairs = lax.dynamic_slice_in_dim(key_values, key_offset, key_block, 0)
            key_places = key_offset + jnp.arange(key_block, dtype=jnp.int32)
            allowed = (key_places[None, :] <= query_places[:, None]) & (
                key_places[None, :] >= query_starts[:, None]
            )
            scores = (
                lax.dot_general(
                    block_queries,
                    block_pairs[:, :HD],
                    (((1,), (1,)), ((), ())),
                    preferred_element_type=jnp.float32,
                )
                * attn_scale
            )
            scores = jnp.where(jnp.tile(allowed, (GQ, 1)), scores, -jnp.inf)
            new_peak = jnp.maximum(row_peak, jnp.max(scores, axis=1))
            weights = jnp.exp(scores - new_peak[:, None])
            factor = jnp.exp(row_peak - new_peak)
            totals = totals * factor + jnp.sum(weights, axis=1)
            accumulated = accumulated * factor[:, None] + jnp.dot(
                weights.astype(jnp.bfloat16),
                block_pairs[:, HD:],
                preferred_element_type=jnp.float32,
            )
            return (new_peak, totals, accumulated)

        start_state = (
            jnp.full((GQ * block_rows,), masked_floor, jnp.float32),
            jnp.zeros((GQ * block_rows,), jnp.float32),
            jnp.zeros((GQ * block_rows, HD), jnp.float32),
        )
        row_peak, totals, accumulated = lax.fori_loop(lowest, highest, step_keys, start_state)
        mixed = (accumulated / totals[:, None]).astype(jnp.bfloat16).reshape(GQ, block_rows, HD)
        return mixed.transpose(1, 0, 2).reshape(block_rows, GQ * HD)

    attended = lax.map(attend, jnp.arange(rows_quarter // block_rows, dtype=jnp.int32)).reshape(
        rows_quarter, GQ * HD
    )
    partial_proj = lax.dot_general(
        attended, w_attn_out, (((1,), (1,)), ((), ())), preferred_element_type=jnp.float32
    )
    projection = fold_any(partial_proj, group_bits[::-1], group_bits)
    after_attention = (hidden.astype(jnp.float32) + residual_scale * projection).astype(
        jnp.bfloat16
    )
    expert_in = rms_norm(after_attention, ffn_gain)
    local_experts = w_gate_up.shape[0]
    share_cols = 128 * pl.cdiv(expert_total, 128)
    half_width = model_width // 2
    carried = jnp.concatenate(
        [
            expert_in[:, :half_width],
            share_table,
            jnp.zeros((share_table.shape[0], share_cols - expert_total), jnp.bfloat16),
        ],
        axis=1,
    )
    layout = (0, 1, 3, 4, 2)
    first_order = (2, 4, 3, 1, 0)
    second_order = (4, 2, 1, 3, 0)
    first_rows = gather_any(carried, first_order)
    second_rows = gather_any(expert_in[:, half_width:], second_order)
    second_dims = list(second_order[::-1])
    second_rows = second_rows.transpose(
        [second_dims.index(bit) for bit in layout] + [len(layout), len(layout) + 1]
    )
    first_rows = first_rows.reshape(-1, first_rows.shape[-1])
    second_rows = second_rows.reshape(-1, second_rows.shape[-1])
    local_shares = lax.dynamic_slice_in_dim(
        first_rows[:, half_width : half_width + expert_total],
        group_index * local_experts,
        local_experts,
        1,
    ).astype(jnp.float32)
    expert_part = dense_experts(first_rows, second_rows, local_shares, w_gate_up, w_down)
    half_rows = expert_part.shape[0] // 2
    core_upper = lax.axis_index(TENSOR) & 1 == 1
    kept_rows = jnp.where(core_upper, expert_part[half_rows:], expert_part[:half_rows])
    sent_rows = jnp.where(core_upper, expert_part[:half_rows], expert_part[half_rows:])
    flat_part = kept_rows.astype(jnp.float32) + partner(sent_rows, TENSOR, 0).astype(jnp.float32)
    rest = layout[1:]
    expert_sum = jnp.concatenate(
        [
            fold_any(flat_part[:, :half_width], rest, (1, 3, 4, 2)),
            fold_any(flat_part[:, half_width:], rest, (3, 1, 2, 4)),
        ],
        axis=1,
    )
    hidden_out = (after_attention.astype(jnp.float32) + residual_scale * expert_sum).astype(
        jnp.bfloat16
    )
    return (after_attention, hidden_out, kv_block[None])


def solution(mesh):
    grid = mesh.devices.reshape(mesh.devices.shape[0], -1, 4, 2)
    mesh = jax.sharding.Mesh(grid, ("dp",) + TENSOR)
    placed = (
        P(("dp",) + TENSOR, None),
        P("dp"),
        P(("dp",) + TENSOR, None),
        P(("dp",) + TENSOR, None),
        P(),
        P(None, TENSOR),
        P(None, TENSOR),
        P(),
        P(TENSOR, None, None),
        P(TENSOR, None, None),
    )
    return jax.shard_map(
        on_device,
        mesh=mesh,
        in_specs=placed,
        out_specs=(P(("dp",) + TENSOR, None), P(("dp",) + TENSOR, None), P(TENSOR, "dp", None)),
        check_vma=False,
    )
```
